32 devices in a mesh: fsdp: 8 (over y, x, core), grp: 4 (over z).
Axes of the slice: x: 2, y: 2, z: 4, core: 2. Of those that a mesh axis runs over, the one named last changes fastest.
Arguments:
- tokens: bfloat16 [12288, 1536], P(('fsdp', 'grp')), may hold values from -6 to 6
- block_order: int32 [8, 4], P('fsdp'), may hold values from 0 to 3, each once within a row
- cont_lengths: int32 [8, 2, 4], P('fsdp'), may hold values from 1 to 192, 384 in all within a row
- gain_attn: float32 [1536], replicated, may hold values from 0.5 to 1.5
- w_qkv: bfloat16 [1536, 4608], P(('fsdp', 'grp')), may hold values from -0.15625 to 0.15625
- w_forget: bfloat16 [1536, 24], P(('fsdp', 'grp')), may hold values from -0.15625 to 0.15625
- b_forget: float32 [24], replicated, may hold values from 3 to 9
- w_out: bfloat16 [1536, 1536], P(('fsdp', 'grp')), may hold values from -0.625 to 0.625
- gain_ffn: float32 [1536], replicated, may hold values from 0.5 to 1.5
- w_gate_up: bfloat16 [1536, 8192], P(('fsdp', 'grp')), may hold values from -0.15625 to 0.15625
- w_down: bfloat16 [4096, 1536], P(('fsdp', 'grp')), may hold values from -0.09375 to 0.09375
- grad_out: bfloat16 [12288, 1536], P(('fsdp', 'grp')), may hold values from -6 to 6
Outputs:
- out: bfloat16 [12288, 1536], P(('fsdp', 'grp'))
- grad_tokens: bfloat16 [12288, 1536], P(('fsdp', 'grp'))
- grad_gain_attn: float32 [1536], replicated
- grad_w_qkv: float32 [1536, 4608], P(('fsdp', 'grp'))
- grad_w_forget: float32 [1536, 24], P(('fsdp', 'grp'))
- grad_b_forget: float32 [24], replicated
- grad_w_out: float32 [1536, 1536], P(('fsdp', 'grp'))
- grad_gain_ffn: float32 [1536], replicated
- grad_w_gate_up: float32 [1536, 8192], P(('fsdp', 'grp'))
- grad_w_down: float32 [4096, 1536], P(('fsdp', 'grp'))
The draws below stay inside these ranges and needn't reach their ends.
Inputs may be any that keep to these rules, and one draw needn't show every extreme that they name: Each row of block_order is a permutation of 0 to 3. `cont_lengths`: each row of 4 lengths sums to 384, and its largest entry is 192.
All inputs are finite; a program needn't handle non-finite values.
Results may differ from the reference program's by a relative error of at most 0.015.
The reference program's roundings to bfloat16 on the way count: a program that leaves them out, or rounds other values in their place, can miss the bound.
Values may be sent and summed in bfloat16 or wider, within the bound.
A program may use at most 320 MiB of HBM per device.

```python
import math
import jax
import jax.numpy as jnp
import numpy as np
from jax import lax

D = 1536
H = 24
HD = 64
FF = 4096
TOK_DEV = 384
CONT_DEV = 4
CONT_MOST = 192
PROMPT = 768
BLOCKS = 4
GROUPS = 8
TOKENS = 12288
N_FSDP = 8
N_GRP = 4


def block_scale(key, extent, cuts, least, top_value):
    level, own = 1.0, jax.random.fold_in(key, 6)
    for position, shards_of in cuts:
        heights = jnp.exp(jax.random.uniform(jax.random.fold_in(own, position), (shards_of,), jnp.float32, least / len(cuts), top_value / len(cuts)))
        level = level * jnp.repeat(heights, extent[position] // shards_of).reshape([-1 if axis == position else 1 for axis in range(len(extent))])
    return level


def split_up(amount, total, reach, slope):
    weights = [(1 << 20) // math.isqrt(grade ** slope) + 1 for grade in range(2, amount + 1)]
    rest, given = total - reach - (amount - 1), [1] * (amount - 1)
    while rest > 0:
        candidates = [i for i in range(amount - 1) if given[i] < reach]
        pool, remaining = sum([weights[i] for i in candidates]), rest
        for i in candidates:
            addition = min(reach - given[i], max(1, remaining * weights[i] // pool), rest)
            given[i] = given[i] + addition
            rest = rest - addition
    return np.array([reach] + given)


def ragged(key, amount, total, most, skew):
    if amount == 2:
        one = jax.random.randint(key, (), max(1, total - most), min(most, total - 1) + 1)
        return jnp.stack([one, total - one])
    sizes = jnp.asarray(split_up(amount, total, most, skew), jnp.int32)
    couples = (amount - 1) // 2
    giver, sink = sizes[1:1 + 2 * couples:2], sizes[2:2 + 2 * couples:2]
    margin = jnp.minimum(giver - 1, most - sink)
    moved = jax.random.randint(jax.random.fold_in(key, 1), (couples,), 0, 1 << 20) % (margin + 1)
    sizes = sizes.at[1:1 + 2 * couples:2].set(giver - moved).at[2:2 + 2 * couples:2].set(sink + moved)
    return sizes[jax.random.permutation(jax.random.fold_in(key, 2), amount)]


def gaussian(key, dims, width, limit, cuts=(), held_as=jnp.bfloat16):
    values = jax.random.normal(key, dims, jnp.float32) * width
    if len(cuts) > 0:
        values = block_scale(key, dims, cuts, -0.22, 0.18) * values
    return jnp.clip(values, min=-limit, max=limit).astype(held_as)


def setup_inputs(seed: int = 0) -> dict:
    streams_of = jax.random.split(jax.random.key(seed), 13)
    tokens = gaussian(streams_of[0], (TOKENS, D), 1.0, 6.0, ((0, 32),))
    block_order = jax.vmap(lambda own: jax.random.permutation(own, BLOCKS))(jax.random.split(streams_of[1], GROUPS)).reshape((GROUPS, BLOCKS)).astype(jnp.int32)
    cont_lengths = jax.vmap(lambda own: ragged(own, CONT_DEV, TOK_DEV, CONT_MOST, 2))(jax.random.split(streams_of[2], GROUPS * (BLOCKS - 2))).reshape((GROUPS, BLOCKS - 2, CONT_DEV)).astype(jnp.int32)
    gain_attn = jnp.clip(1.0 + 0.1 * jax.random.normal(streams_of[3], (D,), jnp.float32), 0.5, 1.5)
    w_qkv = gaussian(streams_of[4], (D, 3 * D), D ** -0.5, 0.15625, ((0, 32),))
    w_forget = gaussian(streams_of[5], (D, H), D ** -0.5, 0.15625, ((0, 32),))
    b_forget = jnp.clip(jax.random.uniform(streams_of[6], (H,), jnp.float32, 3.0, 9.0), 3.0, 9.0)
    w_out = gaussian(streams_of[7], (D, D), (D // 16) ** -0.5, 0.625, ((0, 32),))
    gain_ffn = jnp.clip(1.0 + 0.1 * jax.random.normal(streams_of[8], (D,), jnp.float32), 0.5, 1.5)
    w_gate_up = gaussian(streams_of[9], (D, 2 * FF), D ** -0.5, 0.15625, ((0, 32),))
    w_down = gaussian(streams_of[10], (FF, D), FF ** -0.5, 0.09375, ((0, 32),))
    grad_out = gaussian(streams_of[11], (TOKENS, D), 1.0, 6.0, ((0, 32),))
    return dict(tokens=tokens, block_order=block_order, cont_lengths=cont_lengths, gain_attn=gain_attn, w_qkv=w_qkv, w_forget=w_forget, b_forget=b_forget, w_out=w_out, gain_ffn=gain_ffn, w_gate_up=w_gate_up, w_down=w_down, grad_out=grad_out)


@jax.custom_vjp
def low(v):
    return lax.optimization_barrier(v.astype(jnp.bfloat16)).astype(jnp.float32)

@jax.custom_vjp
def low_back(v):
    return v

def low_keep(v):
    return (low(v), None)

def low_pass(kept, grad):
    return (grad,)

def back_keep(v):
    return (v, None)

def back_low(kept, grad):
    return (low(grad),)
low.defvjp(low_keep, low_pass)
low_back.defvjp(back_keep, back_low)
EPSILON = 1e-05
HIGHEST = lax.Precision.HIGHEST

def norm_rows(features):
    row_scale = lax.rsqrt(lax.optimization_barrier(jnp.mean(features * features, axis=-1, keepdims=True)) + EPSILON)
    return features * row_scale

def attend(query_rows, key_rows, value_rows, query_decay, key_decay, allowed):
    query_heads = query_rows.reshape(query_rows.shape[0], H, HD)
    key_heads = key_rows.reshape(key_rows.shape[0], H, HD)
    value_heads = value_rows.reshape(value_rows.shape[0], H, HD)
    raw_scores = low_back(jnp.einsum('qhd,khd->hqk', query_heads, key_heads, precision=HIGHEST) * HD ** (-0.5))
    scores = raw_scores + query_decay.T[:, :, None] - key_decay.T[:, None, :]
    scores = jnp.where(allowed[None], scores, -jnp.inf)
    weights = jax.nn.softmax(scores, axis=-1)
    mixed = jnp.einsum('hqk,khd->qhd', low(weights), value_heads, precision=HIGHEST)
    return mixed.reshape(query_rows.shape[0], D)

def group_layer(params, x_group, slots, lengths):
    gain_a, w_qkv, w_f, b_f, w_o, gain_f, w_gu, w_d = params
    act = low(norm_rows(x_group) * gain_a)
    mixed = jnp.dot(act, w_qkv, precision=HIGHEST)
    logits = low_back(jnp.dot(act, w_f, precision=HIGHEST) + b_f)
    log_keep = jax.nn.log_sigmoid(logits)
    queries = low(low_back(mixed[:, :D]))
    keys = low(low_back(mixed[:, D:2 * D]))
    values = low(low_back(mixed[:, 2 * D:]))

    def blocks_of(matrix):
        return matrix.reshape(N_GRP, TOK_DEV, matrix.shape[1])[slots]
    query_blocks = blocks_of(queries)
    key_blocks = blocks_of(keys)
    value_blocks = blocks_of(values)
    log_blocks = blocks_of(log_keep)
    prompt_q = query_blocks[:2].reshape(PROMPT, D)
    prompt_k = key_blocks[:2].reshape(PROMPT, D)
    prompt_v = value_blocks[:2].reshape(PROMPT, D)
    prompt_cum = jnp.cumsum(log_blocks[:2].reshape(PROMPT, H), axis=0)
    prompt_pos = jnp.arange(PROMPT, dtype=jnp.int32)
    causal = prompt_pos[None, :] <= prompt_pos[:, None]
    results = [attend(prompt_q, prompt_k, prompt_v, prompt_cum, prompt_cum, causal).reshape(2, TOK_DEV, D)]
    local_pos = jnp.arange(TOK_DEV, dtype=jnp.int32)
    for block in range(2, N_GRP):
        seg_ends = jnp.cumsum(lengths[block - 2])
        segment = lax.optimization_barrier(jnp.sum((local_pos[:, None] >= seg_ends[None, :]).astype(jnp.int32), axis=1))
        within = jnp.logical_and(segment[:, None] == segment[None, :], local_pos[None, :] <= local_pos[:, None])
        local_cum = jnp.dot(within.astype(log_blocks.dtype), log_blocks[block], precision=HIGHEST)
        query_decay = prompt_cum[-1][None, :] + local_cum
        key_rows = jnp.concatenate([prompt_k, key_blocks[block]], axis=0)
        value_rows = jnp.concatenate([prompt_v, value_blocks[block]], axis=0)
        key_decay = jnp.concatenate([prompt_cum, local_cum], axis=0)
        allowed = jnp.concatenate([jnp.ones((TOK_DEV, PROMPT), dtype=jnp.bool_), within], axis=1)
        results.append(attend(query_blocks[block], key_rows, value_rows, query_decay, key_decay, allowed)[None])
    attn_blocks = jnp.concatenate(results, axis=0)
    attn_places = jnp.zeros_like(attn_blocks).at[slots].set(attn_blocks)
    attn_o = low(low_back(attn_places.reshape(N_GRP * TOK_DEV, D)))
    branch = low_back(jnp.dot(attn_o, w_o, precision=HIGHEST))
    resid = x_group + branch
    act_two = low(norm_rows(resid) * gain_f)
    both = jnp.dot(act_two, w_gu, precision=HIGHEST)
    gate = low_back(both[:, :FF])
    up_part = low_back(both[:, FF:])
    hidden_act = low(jax.nn.silu(gate) * up_part)
    return resid + jnp.dot(hidden_act, w_d, precision=HIGHEST)

def reference(tokens, block_order, cont_lengths, gain_attn, w_qkv, w_forget, b_forget, w_out, gain_ffn, w_gate_up, w_down, grad_out):
    inputs = tokens.astype(jnp.float32)
    params = (gain_attn.astype(jnp.float32), w_qkv.astype(jnp.float32), w_forget.astype(jnp.float32), b_forget.astype(jnp.float32), w_out.astype(jnp.float32), gain_ffn.astype(jnp.float32), w_gate_up.astype(jnp.float32), w_down.astype(jnp.float32))

    def forward(x_all, weights):

        def step(carry, pieces):
            x_group, slots, lengths = pieces
            return (carry, jax.checkpoint(group_layer)(weights, x_group, slots, lengths))
        stacked = x_all.reshape(N_FSDP, N_GRP * TOK_DEV, D)
        _, outputs = lax.scan(step, jnp.zeros((), jnp.float32), (stacked, block_order, cont_lengths))
        return outputs.reshape(TOKENS, D)
    result, pullback = jax.vjp(forward, inputs, params)
    grad_x, grads = pullback(grad_out.astype(jnp.float32))
    return (result.astype(jnp.bfloat16), grad_x.astype(jnp.bfloat16), grads[0], grads[1], grads[2], grads[3], grads[4], grads[5], grads[6], grads[7])
```

```python
import functools

import jax
import jax.numpy as jnp
from jax import lax
from jax.experimental import pallas as pl
from jax.experimental.pallas import tpu as pltpu
from jax.sharding import PartitionSpec as P

EPSILON = 1e-05
NEG = -1e30
HIGHEST = lax.Precision.HIGHEST
MESH = pl.DeviceIdType.MESH
F32 = jnp.float32
BF16 = jnp.bfloat16


def flip_bit(value, bit):
    return value + bit - 2 * bit * ((value // bit) % 2)


def flip(value, mask):
    bit = 1
    while bit <= mask:
        if mask & bit:
            value = flip_bit(value, bit)
        bit *= 2
    return value


def swap(value, axis, mask):
    return lax.ppermute(value, axis, [(i, i ^ mask) for i in range(lax.axis_size(axis))])


def gather_parts(shapes):
    return [(w, h) for w, s in enumerate(shapes) for h in (0, 1) if h == 0 or s[1] % 256 == 0]


def gather_kernel(shapes, n_fsdp, n_grp, *refs):
    count = len(shapes)
    ins, outs = refs[:count], refs[count : 2 * count]
    send_sem, recv_sem, local_sem = refs[2 * count :]
    f, z = lax.axis_index("fsdp"), lax.axis_index("grp")
    bits = [1 << i for i in range(1, n_fsdp.bit_length() - 1)]

    def peer(fk, zk):
        return {"fsdp": flip(f, fk), "grp": flip(z, zk)}

    barrier = pltpu.get_barrier_semaphore()
    peers = [(0, k) for k in range(1, n_grp)] + [(b, 0) for b in bits] + [(1, 0)]
    for fk, zk in peers:
        pl.semaphore_signal(barrier, inc=1, device_id=peer(fk, zk), device_id_type=MESH)
    pl.semaphore_wait(barrier, len(peers))

    parts = gather_parts(shapes)
    orders = [bits if h == 0 else bits[::-1] for _, h in parts]
    sends = []

    def half(w, h):
        width = shapes[w][1] // 2
        return pl.ds(0, shapes[w][1]) if width % 128 else pl.ds(h * width, width)

    def piece(w, h, fk, zk):
        return outs[w].at[flip(f, fk) * n_grp + flip(z, zk), :, half(w, h)]

    def send(p, fk, zk, to_f, to_z, own):
        w, h = parts[p]
        copy = pltpu.make_async_remote_copy(
            src_ref=ins[w].at[:, half(w, h)] if own else piece(w, h, fk, zk),
            dst_ref=piece(w, h, fk, zk),
            send_sem=send_sem.at[len(sends)],
            recv_sem=recv_sem.at[p, (fk ^ to_f) * n_grp + (zk ^ to_z)],
            device_id=peer(to_f, to_z),
            device_id_type=MESH,
        )
        copy.start()
        sends.append(copy)

    def arrived(p, fk, zk):
        view = piece(*parts[p], fk, zk)
        pltpu.make_async_remote_copy(
            src_ref=view,
            dst_ref=view,
            send_sem=send_sem.at[0],
            recv_sem=recv_sem.at[p, fk * n_grp + zk],
            device_id=peer(1, 0),
            device_id_type=MESH,
        ).wait_recv()

    def forward(p, stage, fk, zk, own=False):
        for bit in orders[p][stage:]:
            send(p, fk, zk, bit, 0, own)
        send(p, fk, zk, 1, 0, own)

    local = []
    for w in range(count):
        copy = pltpu.make_async_copy(ins[w], outs[w].at[f * n_grp + z], local_sem.at[w])
        copy.start()
        local.append(copy)
    for p in range(len(parts)):
        for k in range(1, n_grp):
            send(p, 0, 0, 0, k, True)
        forward(p, 0, 0, 0, True)
    for k in range(1, n_grp):
        for p in range(len(parts)):
            arrived(p, 0, k)
            forward(p, 0, 0, k)
    have = [[0] for _ in parts]
    for stage in range(len(bits)):
        for a in range(len(have[0])):
            for k in range(n_grp):
                for p in range(len(parts)):
                    fk = have[p][a] ^ orders[p][stage]
                    arrived(p, fk, k)
                    forward(p, stage + 1, fk, k)
        have = [known + [v ^ orders[p][stage] for v in known] for p, known in enumerate(have)]
    for a in range(len(have[0])):
        for k in range(n_grp):
            for p in range(len(parts)):
                arrived(p, have[p][a] ^ 1, k)
    for copy in local:
        copy.wait()
    for copy in sends:
        copy.wait_send()


def gather_rows(weights, collective_id):
    n_fsdp, n_grp = lax.axis_size("fsdp"), lax.axis_size("grp")
    shapes = [w.shape for w in weights]
    count = len(weights)
    per_part = (n_grp - 1) + n_grp * (n_fsdp // 2 - 1) + n_grp * (n_fsdp // 2)
    full = pl.pallas_call(
        functools.partial(gather_kernel, shapes, n_fsdp, n_grp),
        out_shape=[
            jax.ShapeDtypeStruct((n_fsdp * n_grp,) + w.shape, w.dtype) for w in weights
        ],
        in_specs=[pl.BlockSpec(memory_space=pl.ANY)] * count,
        out_specs=[pl.BlockSpec(memory_space=pl.ANY)] * count,
        scratch_shapes=[
            pltpu.SemaphoreType.DMA((per_part * len(gather_parts(shapes)),)),
            pltpu.SemaphoreType.DMA((len(gather_parts(shapes)), n_fsdp * n_grp)),
            pltpu.SemaphoreType.DMA((count,)),
        ],
        compiler_params=pltpu.CompilerParams(
            collective_id=collective_id, has_side_effects=True
        ),
        name="gather_rows",
    )(*weights)
    return [v.reshape(-1, v.shape[2]) for v in full]


def dot_lanes(a, b):
    return lax.dot_general(a, b, (((1,), (1,)), ((), ())), preferred_element_type=F32)


def dot_rows(a, b):
    return lax.dot_general(a, b, (((0,), (0,)), ((), ())), preferred_element_type=F32)


def seen_blocks(block):
    if block == 0:
        return [(0, 0)]
    if block == 1:
        return [(0, None), (1, 0)]
    return [(0, None), (1, None), (block, block - 1)]


def head_setup(c_ref, head_size):
    head = pl.program_id(1)
    lanes = lax.broadcasted_iota(jnp.int32, (1, 2 * head_size), 1)
    mine = lanes // head_size == head
    columns = lax.broadcasted_iota(jnp.int32, (1, c_ref.shape[3]), 1)

    def decay(block):
        return jnp.sum(
            jnp.where(columns == head, c_ref[0, block], 0.0), axis=1, keepdims=True
        )

    return mine, decay


def attend_kernel(blocks, head_size, rel_ref, x_ref, c_ref, mask_ref, o_ref, lse_ref):
    mine, decay = head_setup(c_ref, head_size)
    scale = head_size**-0.5
    decays = [decay(b) for b in range(blocks)]
    for block in range(blocks):
        place = rel_ref[block]
        query = jnp.where(mine, x_ref[place, 0] * scale, 0).astype(BF16)
        scores = []
        for other, mask in seen_blocks(block):
            s = dot_lanes(x_ref[rel_ref[other], 1], query) - decays[other]
            if mask is not None:
                s = s + mask_ref[mask]
            scores.append(s)
        top = functools.reduce(
            jnp.maximum, [jnp.max(s, axis=0, keepdims=True) for s in scores]
        )
        total, mixed = 0.0, 0.0
        for s, (other, _) in zip(scores, seen_blocks(block)):
            weight = jnp.exp(s - top)
            total = total + jnp.sum(weight, axis=0, keepdims=True)
            mixed = mixed + dot_rows(x_ref[rel_ref[other], 2], weight.astype(BF16))
        lse_ref[0, 0, pl.ds(block, 1), :] = top + jnp.log(total)
        result = (mixed / total).T.astype(BF16)
        o_ref[place] = jnp.where(mine, result, o_ref[place])


def attend_back_kernel(
    blocks, head_size, rel_ref, x_ref, do_ref, c_ref, mask_ref, lse_ref, dx_ref, dcq_ref, dck_ref
):
    mine, decay = head_setup(c_ref, head_size)
    scale = head_size**-0.5
    decays = [decay(b) for b in range(blocks)]
    key_grads, value_grads, decay_grads = [None] * blocks, [None] * blocks, [None] * blocks

    def add(store, index, value):
        store[index] = value if store[index] is None else store[index] + value

    def put(place, part, value):
        dx_ref[place, part] = jnp.where(mine, value.astype(BF16), dx_ref[place, part])

    for block in range(blocks):
        place = rel_ref[block]
        query = jnp.where(mine, x_ref[place, 0] * scale, 0).astype(BF16)
        grad_o = jnp.where(mine, do_ref[place], 0).astype(BF16)
        lse = lse_ref[0, 0, pl.ds(block, 1), :]
        weights, grads, delta = [], [], 0.0
        for other, mask in seen_blocks(block):
            s = dot_lanes(x_ref[rel_ref[other], 1], query) - decays[other]
            if mask is not None:
                s = s + mask_ref[mask]
            weight = jnp.exp(s - lse)
            grad = dot_lanes(x_ref[rel_ref[other], 2], grad_o)
            delta = delta + jnp.sum(weight * grad, axis=0, keepdims=True)
            weights.append(weight)
            grads.append(grad)
        query_grad, query_decay = 0.0, 0.0
        for weight, grad, (other, _) in zip(weights, grads, seen_blocks(block)):
            ds = weight * (grad - delta)
            query_decay = query_decay + jnp.sum(ds, axis=0, keepdims=True)
            add(decay_grads, other, jnp.sum(ds, axis=1, keepdims=True))
            low = ds.astype(BF16)
            query_grad = query_grad + dot_rows(x_ref[rel_ref[other], 1], low)
            add(key_grads, other, jnp.dot(low, query, preferred_element_type=F32))
            add(
                value_grads,
                other,
                jnp.dot(weight.astype(BF16), grad_o, preferred_element_type=F32),
            )
        put(place, 0, (query_grad * scale).T)
        dcq_ref[0, 0, pl.ds(block, 1), :] = query_decay
    columns = lax.broadcasted_iota(jnp.int32, (1, dck_ref.shape[3]), 1)
    for block in range(blocks):
        place = rel_ref[block]
        put(place, 1, key_grads[block])
        put(place, 2, value_grads[block])
        dck_ref[0, block] = jnp.where(
            columns == pl.program_id(1), decay_grads[block], dck_ref[0, block]
        )


def attention_specs(blocks, rows, pair_width):
    x_spec = pl.BlockSpec((blocks, 3, rows, pair_width), lambda p, h, rel: (0, 0, 0, p))
    o_spec = pl.BlockSpec((blocks, rows, pair_width), lambda p, h, rel: (0, 0, p))
    c_spec = pl.BlockSpec((1, blocks, rows, 8), lambda p, h, rel: (p, 0, 0, 0))
    m_spec = pl.BlockSpec((3, rows, rows), lambda p, h, rel: (0, 0, 0))
    l_spec = pl.BlockSpec((1, 1, 8, rows), lambda p, h, rel: (p, h, 0, 0))
    return x_spec, o_spec, c_spec, m_spec, l_spec


def attend(rel, x, decay, masks, head_size):
    blocks, _, rows, width = x.shape
    pairs = width // (2 * head_size)
    x_spec, o_spec, c_spec, m_spec, l_spec = attention_specs(blocks, rows, 2 * head_size)
    return pl.pallas_call(
        functools.partial(attend_kernel, blocks, head_size),
        out_shape=[
            jax.ShapeDtypeStruct((blocks, rows, width), BF16),
            jax.ShapeDtypeStruct((pairs, 2, 8, rows), F32),
        ],
        grid_spec=pltpu.PrefetchScalarGridSpec(
            num_scalar_prefetch=1,
            grid=(pairs, 2),
            in_specs=[x_spec, c_spec, m_spec],
            out_specs=[o_spec, l_spec],
        ),
        compiler_params=pltpu.CompilerParams(vmem_limit_bytes=48 << 20),
        cost_estimate=pl.CostEstimate(
            flops=60_000_000_000, bytes_accessed=12_000_000, transcendentals=8_000_000
        ),
        name="attend",
    )(rel, x, decay, masks)


def attend_back(rel, x, grad_o, decay, masks, lse, head_size):
    blocks, _, rows, width = x.shape
    pairs = width // (2 * head_size)
    x_spec, o_spec, c_spec, m_spec, l_spec = attention_specs(blocks, rows, 2 * head_size)
    return pl.pallas_call(
        functools.partial(attend_back_kernel, blocks, head_size),
        out_shape=[
            jax.ShapeDtypeStruct(x.shape, BF16),
            jax.ShapeDtypeStruct((pairs, 2, 8, rows), F32),
            jax.ShapeDtypeStruct((pairs, blocks, rows, 8), F32),
        ],
        grid_spec=pltpu.PrefetchScalarGridSpec(
            num_scalar_prefetch=1,
            grid=(pairs, 2),
            in_specs=[x_spec, o_spec, c_spec, m_spec, l_spec],
            out_specs=[x_spec, l_spec, c_spec],
        ),
        compiler_params=pltpu.CompilerParams(vmem_limit_bytes=56 << 20),
        cost_estimate=pl.CostEstimate(
            flops=120_000_000_000, bytes_accessed=16_000_000, transcendentals=8_000_000
        ),
        name="attend_back",
    )(rel, x, grad_o, decay, masks, lse)


def weight_grad_kernel(count, own_ids, other_ids, l_ref, l_other_ref, r_ref, r_other_ref, *outs):
    def side(ref, ids):
        return jnp.concatenate([ref[ids[k]] for k in range(2 * count)], axis=0)

    total = jnp.dot(side(l_ref, own_ids), r_ref[...], preferred_element_type=F32)
    total = total + jnp.dot(
        side(l_other_ref, other_ids), r_other_ref[...], preferred_element_type=F32
    )
    total = total.astype(BF16).reshape(2 * count, -1, total.shape[1])
    outs[0][...] = total[:count]
    outs[1][...] = total[count:]


def weight_grad(own_ids, other_ids, l_own, l_other, r_own, r_other, start, width):
    count = own_ids.shape[0] // 2
    _, rows, tok = l_own.shape
    limit = 1536 if rows * count < 1024 else 512
    tile = max(t for t in range(128, limit + 1, 128) if width % t == 0 and start % t == 0)
    steps, first = width // tile, start // tile
    whole = lambda v: pl.BlockSpec(v.shape, lambda n, own, other: (0, 0, 0))
    r_spec = pl.BlockSpec((tok, tile), lambda n, own, other: (0, first + n))
    out_spec = pl.BlockSpec((count, rows, tile), lambda n, own, other: (0, 0, n))
    return pl.pallas_call(
        functools.partial(weight_grad_kernel, count),
        out_shape=[jax.ShapeDtypeStruct((count, rows, width), BF16)] * 2,
        grid_spec=pltpu.PrefetchScalarGridSpec(
            num_scalar_prefetch=2,
            grid=(steps,),
            in_specs=[whole(l_own), whole(l_other), r_spec, r_spec],
            out_specs=[out_spec, out_spec],
        ),
        compiler_params=pltpu.CompilerParams(vmem_limit_bytes=48 << 20),
        cost_estimate=pl.CostEstimate(
            flops=8 * count * rows * tok * width,
            bytes_accessed=2 * (2 * count * rows * width + 2 * tok * width),
            transcendentals=0,
        ),
        name="weight_grad",
    )(own_ids, other_ids, l_own, l_other, r_own, r_other)


def split_rows(left):
    n_fsdp = lax.axis_size("fsdp")
    turned = left.T.reshape(n_fsdp, left.shape[1] // n_fsdp, left.shape[0])
    parity = lax.axis_index("fsdp") % 2
    halves = turned.reshape(n_fsdp // 2, 2, *turned.shape[1:])
    away = lax.dynamic_index_in_dim(halves, 1 - parity, 1, keepdims=False)
    return turned, swap(away, "fsdp", 1)


class RowSum:
    def __init__(self, left, columns):
        self.bits = [1 << i for i in range(lax.axis_size("fsdp").bit_length() - 2)]
        f = lax.axis_index("fsdp")
        self.held, self.away, self.orders = [], [], []
        for part, (right, right_other, start, width) in enumerate(columns):
            order = self.bits if part % 2 else self.bits[::-1]
            keep = [0]
            for bit in reversed(order[1:]):
                keep = keep + [k ^ bit for k in keep]
            ids = jnp.stack([flip(f // 2, k) for k in [k ^ order[0] for k in keep] + keep])
            away, held = weight_grad(
                2 * ids + f % 2, ids, left[0], left[1], right, right_other, start, width
            )
            self.held.append(held)
            self.away.append(away)
            self.orders.append(order)

    def after(self, *values):
        tied = lax.optimization_barrier((self.away, self.held) + values)
        self.away, self.held = tied[0], tied[1]
        return tied[2:]

    def send(self):
        self.arrived = [swap(v, "fsdp", 2 * o[0]) for v, o in zip(self.away, self.orders)]

    def halve(self):
        away, held = [], []
        for mine, new, order in zip(self.held, self.arrived, self.orders):
            total = mine.astype(F32) + new.astype(F32)
            count = mine.shape[0] // 2
            held.append(total[:count].astype(BF16))
            away.append(total[count:].astype(BF16))
        self.held, self.away = held, away
        self.orders = [o[1:] for o in self.orders]

    def spread(self):
        n_grp, z = lax.axis_size("grp"), lax.axis_index("grp")
        self.held, self.away = [], []
        for mine, new in zip(self.last, self.arrived):
            total = (mine.astype(F32) + new.astype(F32))[0]
            total = total.reshape(n_grp, total.shape[0] // n_grp, total.shape[1])
            self.held.append(lax.dynamic_index_in_dim(total, z, 0, keepdims=False))
            self.away.append(
                [
                    lax.dynamic_index_in_dim(total, flip(z, k), 0, keepdims=False).astype(BF16)
                    for k in range(1, n_grp)
                ]
            )

    def middle(self):
        for _ in self.bits[1:]:
            self.halve()
            self.send()
        self.last = self.held

    def send_spread(self):
        self.arrived = [
            [swap(v, "grp", k + 1) for k, v in enumerate(pieces)] for pieces in self.away
        ]

    def result(self):
        sums = []
        for mine, pieces in zip(self.held, self.arrived):
            for piece in pieces:
                mine = mine + piece.astype(F32)
            sums.append(mine)
        return jnp.concatenate(sums, axis=1)

    def finish(self):
        self.send()
        self.middle()
        self.spread()
        self.send_spread()
        return self.result()


def sum_everywhere(values):
    for axis in ("grp", "fsdp"):
        mask = 1
        while mask < lax.axis_size(axis):
            values = values + swap(values, axis, mask)
            mask *= 2
    return values


def norm_rows(features):
    row_scale = lax.rsqrt(jnp.mean(features * features, axis=-1, keepdims=True) + EPSILON)
    return (features * row_scale, row_scale)


def norm_back(grad_normed, normed, row_scale):
    average_addend = jnp.mean(grad_normed * normed, axis=-1, keepdims=True)
    return row_scale * (grad_normed - normed * average_addend)


def contract_cols(first_op, second_op):
    return lax.dot_general(
        first_op, second_op, (((1,), (1,)), ((), ())), preferred_element_type=F32
    )


def exchange(by_group):
    z = lax.axis_index("grp")
    parts = []
    for k in range(by_group.shape[0]):
        part = lax.dynamic_index_in_dim(by_group, flip(z, k), 0, keepdims=False)
        parts.append(swap(part, "grp", k) if k else part)
    return jnp.stack(parts)


def exchange_back(by_distance):
    z = lax.axis_index("grp")
    parts = [by_distance[0]]
    for k in range(1, by_distance.shape[0]):
        parts.append(swap(by_distance[k], "grp", k))
    stacked = jnp.stack(parts)
    return [
        lax.dynamic_index_in_dim(stacked, flip(z, g), 0, keepdims=False)
        for g in range(by_distance.shape[0])
    ]


def flip_traced(value, mask):
    return jnp.bitwise_xor(value, mask)


def on_device(
    tokens,
    block_order,
    cont_lengths,
    gain_attn,
    w_qkv,
    w_forget,
    b_forget,
    w_out,
    gain_ffn,
    w_gate_up,
    w_down,
    grad_out,
):
    tok, width = tokens.shape
    heads = w_forget.shape[1]
    head_size = width // heads
    blocks = lax.axis_size("grp")
    z = lax.axis_index("grp")
    own_heads = heads // blocks
    pairs = own_heads // 2
    group_width = width // blocks
    slots = block_order[0]
    rel = flip_traced(slots, z)

    positions = jnp.arange(tok, dtype=jnp.int32)
    causal = positions[None, :] <= positions[:, None]
    seg_ends = jnp.cumsum(cont_lengths[0], axis=1)
    segment = jnp.sum((positions[None, :, None] >= seg_ends[:, None, :]).astype(jnp.int32), axis=2)
    within = jnp.logical_and(segment[:, :, None] == segment[:, None, :], causal[None])
    seen = jnp.concatenate([causal[None], within], axis=0)
    masks = jnp.where(seen.transpose(0, 2, 1), 0.0, NEG).astype(F32)
    summing = jnp.concatenate([causal[None], seen], axis=0).astype(F32)

    forget_pad = 128 - heads
    qkv_full, forget_full = gather_rows(
        [w_qkv, jnp.pad(w_forget, ((0, 0), (0, forget_pad)))], 1
    )
    inputs = tokens.astype(F32)
    normed_one, scale_one = norm_rows(inputs)
    acts = (normed_one * gain_attn).astype(BF16)
    grad_out_other = swap(grad_out, "fsdp", 1)
    acts_rows = split_rows(acts)
    logits = jnp.dot(acts, forget_full, preferred_element_type=F32)[:, :heads] + b_forget
    log_keep = jax.nn.log_sigmoid(logits)
    mixed = jnp.dot(acts, qkv_full, preferred_element_type=F32).astype(BF16)

    by_group = mixed.reshape(tok, 3, blocks, group_width).transpose(2, 1, 0, 3)
    x = exchange(by_group)
    logs = exchange(log_keep.T.reshape(blocks, own_heads, tok))

    gu_in, out_in, _ = lax.optimization_barrier((w_gate_up, w_out, mixed[:8, :128]))
    gate_up_full, out_full = gather_rows([gu_in, out_in], 2)

    logs_block = jnp.stack(
        [lax.dynamic_index_in_dim(logs, rel[b], 0, keepdims=False) for b in range(blocks)]
    )
    local = jnp.einsum("bhj,bij->bhi", logs_block, summing, precision=HIGHEST)
    second = local[1] + local[0][:, -1:]
    decay = jnp.concatenate([local[:1], second[None], local[2:]], axis=0)
    decay_cols = decay.reshape(blocks, pairs, 2, tok).transpose(1, 0, 3, 2)
    decay_cols = jnp.pad(decay_cols, ((0, 0), (0, 0), (0, 0), (0, 6)))
    x, gate_up_full, out_full, down_in = lax.optimization_barrier(
        (x, gate_up_full, out_full, w_down)
    )
    down_full = lax.all_gather(down_in, ("fsdp", "grp"), axis=0, tiled=True)
    head_out, lse = attend(rel, x, decay_cols, masks, head_size)
    attn_o = jnp.concatenate(exchange_back(head_out), axis=1)

    attn_rows = split_rows(attn_o)
    resid = inputs + jnp.dot(attn_o, out_full, preferred_element_type=F32)
    normed_two, scale_two = norm_rows(resid)
    acts_two = (normed_two * gain_ffn).astype(BF16)
    acts_two_rows = split_rows(acts_two)
    ffn_width = down_full.shape[0]
    both = jnp.dot(acts_two, gate_up_full, preferred_element_type=F32)
    gate = both[:, :ffn_width]
    up_part = both[:, ffn_width:]
    sigma = jax.nn.sigmoid(gate)
    swish = gate * sigma
    inner_act = (swish * up_part).astype(BF16)
    half = width // 2
    sum_down = RowSum(
        split_rows(inner_act),
        [(grad_out, grad_out_other, 0, half), (grad_out, grad_out_other, half, half)],
    )
    inner_act, resid = sum_down.after(inner_act, resid)
    sum_down.send()
    result = resid + jnp.dot(inner_act, down_full, preferred_element_type=F32)
    output = result.astype(BF16)

    grad_inner = contract_cols(grad_out, down_full)
    slope = sigma * (1.0 + gate * (1.0 - sigma))
    grad_both = jnp.concatenate(
        [grad_inner * up_part * slope, grad_inner * swish], axis=1
    ).astype(BF16)
    sum_down.middle()
    grad_both_other = swap(grad_both, "fsdp", 1)
    (grad_both,) = sum_down.after(grad_both)
    grad_acts_two = contract_cols(grad_both, gate_up_full)
    gain_two_grad = jnp.sum(grad_acts_two * normed_two, axis=0)
    grad_resid = grad_out.astype(F32) + norm_back(
        grad_acts_two * gain_ffn, normed_two, scale_two
    )
    grad_branch = grad_resid.astype(BF16)
    grad_branch_other = swap(grad_branch, "fsdp", 1)
    grad_heads = contract_cols(grad_branch, out_full).astype(BF16)
    sum_down.spread()
    (grad_heads,) = sum_down.after(grad_heads)
    grad_o = exchange(grad_heads.reshape(tok, blocks, group_width).transpose(1, 0, 2))
    sum_gate_up = RowSum(
        acts_two_rows,
        [
            (grad_both, grad_both_other, 0, ffn_width),
            (grad_both, grad_both_other, ffn_width, ffn_width),
        ],
    )
    sum_gate_up.after()
    sum_gate_up.send()
    sum_down.send_spread()
    sum_out = RowSum(
        attn_rows,
        [
            (grad_branch, grad_branch_other, 0, half),
            (grad_branch, grad_branch_other, half, half),
        ],
    )
    (grad_o,) = sum_out.after(grad_o)
    sum_out.send()

    grad_x, grad_q_decay, grad_k_decay = attend_back(
        rel, x, grad_o, decay_cols, masks, lse, head_size
    )
    sum_gate_up.middle()
    sum_out.middle()
    (grad_x,) = sum_gate_up.after(grad_x)
    (grad_x,) = sum_out.after(grad_x)
    grad_mixed = jnp.stack(exchange_back(grad_x))
    grad_mixed = grad_mixed.transpose(2, 1, 0, 3).reshape(tok, 3 * width)
    grad_q_decay = grad_q_decay[:, :, :blocks].transpose(2, 0, 1, 3).reshape(blocks, own_heads, tok)
    grad_k_decay = grad_k_decay[:, :, :, :2].transpose(1, 0, 3, 2).reshape(blocks, own_heads, tok)
    grad_decay = grad_q_decay - grad_k_decay
    after_second = jnp.sum(grad_q_decay[2:], axis=(0, 2))[None, :, None]
    after_first = after_second + jnp.sum(grad_decay[1], axis=1)[None, :, None]
    after = jnp.concatenate(
        [after_first, after_second, jnp.zeros((blocks - 2, own_heads, 1), F32)], axis=0
    )
    grad_logs = jnp.einsum("bhi,bij->bhj", grad_decay, summing, precision=HIGHEST) + after
    order_back = jnp.stack(
        [
            jnp.sum(jnp.arange(blocks, dtype=jnp.int32) * (rel == k).astype(jnp.int32))
            for k in range(blocks)
        ]
    )
    logs_back = jnp.stack(
        [
            lax.dynamic_index_in_dim(grad_logs, order_back[k], 0, keepdims=False)
            for k in range(blocks)
        ]
    )
    log_grad = jnp.concatenate(exchange_back(logs_back), axis=0)
    grad_logits = log_grad.T * jax.nn.sigmoid(-logits)
    grad_logits = grad_logits.astype(BF16)

    sum_gate_up.spread()
    sum_gate_up.send_spread()
    sum_out.spread()
    sum_out.send_spread()
    part = 3 * width // 2
    narrow = jnp.pad(grad_logits, ((0, 0), (0, forget_pad)))
    last = jnp.concatenate([grad_mixed[:, part:], narrow], axis=1)
    sum_qkv = RowSum(
        acts_rows,
        [
            (grad_mixed, swap(grad_mixed, "fsdp", 1), 0, part),
            (last, swap(last, "fsdp", 1), 0, part + 128),
        ],
    )
    sum_qkv.after()
    grad_wide = sum_qkv.finish()
    grad_qkv, grad_forget = grad_wide[:, : 3 * width], grad_wide[:, 3 * width :][:, :heads]
    grad_acts = contract_cols(grad_mixed, qkv_full) + contract_cols(
        grad_logits, forget_full[:, :heads]
    )
    gain_one_grad = jnp.sum(grad_acts * normed_one, axis=0)
    bias_grad = jnp.sum(grad_logits.astype(F32), axis=0)
    grad_inputs = grad_resid + norm_back(grad_acts * gain_attn, normed_one, scale_one)
    small = sum_everywhere(jnp.concatenate([gain_one_grad, gain_two_grad, bias_grad]))
    return (
        output,
        grad_inputs.astype(BF16),
        small[:width],
        grad_qkv,
        grad_forget,
        small[2 * width :],
        sum_out.result(),
        small[width : 2 * width],
        sum_gate_up.result(),
        sum_down.result(),
    )


def solution(mesh):
    both = P(("fsdp", "grp"), None)
    in_specs = (
        both,
        P("fsdp", None),
        P("fsdp", None, None),
        P(),
        both,
        both,
        P(),
        both,
        P(),
        both,
        both,
        both,
    )
    out_specs = (both, both, P(), both, both, P(), both, P(), both, both)
    return jax.shard_map(
        on_device, mesh=mesh, in_specs=in_specs, out_specs=out_specs, check_vma=False
    )
```

```python
import functools
import itertools

import jax
import jax.numpy as jnp
from jax import lax
from jax.experimental import pallas as pl
from jax.experimental.pallas import tpu as pltpu
from jax.sharding import PartitionSpec as P

EPSILON = 1e-05
NEG = -1e30
HIGHEST = lax.Precision.HIGHEST
MESH = pl.DeviceIdType.MESH
F32 = jnp.float32
BF16 = jnp.bfloat16


def flip_bit(value, bit):
    return value + bit - 2 * bit * ((value // bit) % 2)


def flip(value, mask):
    bit = 1
    while bit <= mask:
        if mask & bit:
            value = flip_bit(value, bit)
        bit *= 2
    return value


def swap(value, axis, mask):
    return lax.ppermute(value, axis, [(i, i ^ mask) for i in range(lax.axis_size(axis))])


def gather_parts(shapes):
    return [(w, h) for w, s in enumerate(shapes) for h in (0, 1) if h == 0 or s[1] % 256 == 0]


class Gather:
    def __init__(self, ins, outs, send_sem, recv_sem, local_sem, n_fsdp, n_grp):
        self.ins, self.outs = ins, outs
        self.send_sem, self.recv_sem = send_sem, recv_sem
        self.f, self.z, self.n_grp = lax.axis_index("fsdp"), lax.axis_index("grp"), n_grp
        self.bits = [1 << i for i in range(1, n_fsdp.bit_length() - 1)]
        self.parts = gather_parts([r.shape for r in ins])
        self.orders = [self.bits if h == 0 else self.bits[::-1] for _, h in self.parts]
        self.across = {b: {"fsdp": flip(self.f, b), "grp": self.z} for b in self.bits + [1]}
        self.up = {"fsdp": self.f, "grp": self.z + 1}
        self.down = {"fsdp": self.f, "grp": self.z - 1}
        self.count, self.sent, self.local = 0, [], []
        for w in range(len(ins)):
            self.local.append(
                pltpu.make_async_copy(
                    ins[w], outs[w].at[self.f * n_grp + self.z], local_sem.at[w]
                )
            )
        self.steps = self._steps()

    def _columns(self, part):
        w, h = self.parts[part]
        width = self.ins[w].shape[1]
        return pl.ds(0, width) if width % 256 else pl.ds(h * (width // 2), width // 2)

    def _piece(self, part, fk, place):
        row = flip(self.f, fk) * self.n_grp + place
        return self.outs[self.parts[part][0]].at[row, :, self._columns(part)]

    def _send(self, part, fk, place, to, to_fk, own=False):
        index = self.count
        self.count += 1

        def copy():
            source = self._piece(part, fk, place)
            if own:
                source = self.ins[self.parts[part][0]].at[:, self._columns(part)]
            return pltpu.make_async_remote_copy(
                src_ref=source,
                dst_ref=self._piece(part, fk, place),
                send_sem=self.send_sem.at[index],
                recv_sem=self.recv_sem.at[part, to_fk, place],
                device_id=to,
                device_id_type=MESH,
            )

        copy().start()
        return copy

    def _wait(self, part, fk, place):
        piece = self._piece(part, fk, place)
        pltpu.make_async_remote_copy(
            src_ref=piece,
            dst_ref=piece,
            send_sem=self.send_sem.at[0],
            recv_sem=self.recv_sem.at[part, fk, place],
            device_id=self.across[1],
            device_id_type=MESH,
        ).wait_recv()

    def _forward(self, part, stage, fk, place, own=False):
        return [
            self._send(part, fk, place, self.across[b], fk ^ b, own)
            for b in self.orders[part][stage:] + [1]
        ]

    def _when(self, condition, action):
        copies = []
        pl.when(condition)(lambda: copies.extend(action()))
        self.sent.append((condition, copies))

    def start(self):
        for copy in self.local:
            copy.start()
        last = self.n_grp - 1
        for part in range(len(self.parts)):
            self._when(
                self.z < last, lambda: [self._send(part, 0, self.z, self.up, 0, True)]
            )
            self._when(self.z > 0, lambda: [self._send(part, 0, self.z, self.down, 0, True)])
            self.sent.append((None, self._forward(part, 0, 0, self.z, True)))

    def _line_step(self, part, j):
        z, last = self.z, self.n_grp - 1
        below, above = z - j, z + j

        def arrive(place):
            self._wait(part, 0, place)
            return self._forward(part, 0, 0, place)

        self._when(z >= j, lambda: arrive(below))
        if j < last:
            self._when(
                jnp.logical_and(z >= j, z < last),
                lambda: [self._send(part, 0, below, self.up, 0)],
            )
        self._when(above <= last, lambda: arrive(above))
        if j < last:
            self._when(
                jnp.logical_and(above <= last, z > 0),
                lambda: [self._send(part, 0, above, self.down, 0)],
            )

    def _cross_step(self, part, stage, fk, place):
        self._wait(part, fk, place)
        self.sent.append((None, self._forward(part, stage + 1, fk, place)))

    def _steps(self):
        count = len(self.parts)
        steps = []
        for j in range(1, self.n_grp):
            for part in range(count):
                steps.append(functools.partial(self._line_step, part, j))
        have = [[0] for _ in range(count)]
        for stage in range(len(self.bits)):
            for a in range(len(have[0])):
                for place in range(self.n_grp):
                    for part in range(count):
                        fk = have[part][a] ^ self.orders[part][stage]
                        steps.append(
                            functools.partial(self._cross_step, part, stage, fk, place)
                        )
            have = [
                known + [v ^ self.orders[part][stage] for v in known]
                for part, known in enumerate(have)
            ]
        for a in range(len(have[0])):
            for place in range(self.n_grp):
                for part in range(count):
                    steps.append(functools.partial(self._wait, part, have[part][a] ^ 1, place))
        return steps

    def run(self, until=None):
        done = len(self.all_steps) - len(self.steps) if hasattr(self, "all_steps") else 0
        if done == 0:
            self.all_steps = list(self.steps)
        stop = len(self.all_steps) if until is None else int(until * len(self.all_steps))
        for step in self.all_steps[done:stop]:
            step()
        self.steps = self.all_steps[max(stop, done) :]

    def finish(self):
        self.run()
        for copy in self.local:
            copy.wait()
        for condition, copies in self.sent:
            if condition is None:
                for copy in copies:
                    copy().wait_send()
            else:

                def wait_sent():
                    for copy in copies:
                        copy().wait_send()

                pl.when(condition)(wait_sent)


def gather_scratch(weights, n_fsdp, n_grp):
    parts = len(gather_parts([w.shape for w in weights]))
    bits = n_fsdp.bit_length() - 2
    crossing = n_fsdp // 2 - 1 + n_fsdp // 2
    sends = 2 + (n_grp - 1) * 2 * (bits + 1) + 2 * (n_grp - 2) + n_grp * crossing + bits + 1
    return [
        pltpu.SemaphoreType.DMA((parts * sends,)),
        pltpu.SemaphoreType.DMA((parts, n_fsdp, n_grp)),
        pltpu.SemaphoreType.DMA((len(weights),)),
    ]


def gathered(weights, n_fsdp, n_grp):
    return [jax.ShapeDtypeStruct((n_fsdp * n_grp,) + w.shape, w.dtype) for w in weights]


def meet(n_fsdp, n_grp, line_only):
    f, z = lax.axis_index("fsdp"), lax.axis_index("grp")
    barrier = pltpu.get_barrier_semaphore()
    bits = [1 << i for i in range(n_fsdp.bit_length() - 1)]
    peers = [{"fsdp": flip(f, b), "grp": z} for b in bits]
    peers += [{"fsdp": f, "grp": flip(z, k)} for k in range(1, n_grp)]
    for peer in peers:
        pl.semaphore_signal(barrier, inc=1, device_id=peer, device_id_type=MESH)
    pl.semaphore_wait(barrier, len(peers))


def gather_kernel(count, n_fsdp, n_grp, *refs):
    meet(n_fsdp, n_grp, True)
    gather = Gather(refs[:count], refs[count : 2 * count], *refs[2 * count :], n_fsdp, n_grp)
    gather.start()
    gather.finish()


def gather_rows(weights, collective_id):
    n_fsdp, n_grp = lax.axis_size("fsdp"), lax.axis_size("grp")
    count = len(weights)
    full = pl.pallas_call(
        functools.partial(gather_kernel, count, n_fsdp, n_grp),
        out_shape=gathered(weights, n_fsdp, n_grp),
        in_specs=[pl.BlockSpec(memory_space=pl.ANY)] * count,
        out_specs=[pl.BlockSpec(memory_space=pl.ANY)] * count,
        scratch_shapes=gather_scratch(weights, n_fsdp, n_grp),
        compiler_params=pltpu.CompilerParams(
            collective_id=collective_id, has_side_effects=True
        ),
        name="gather_rows",
    )(*weights)
    return [v.reshape(-1, v.shape[2]) for v in full]


def dot_lanes(a, b):
    return lax.dot_general(a, b, (((1,), (1,)), ((), ())), preferred_element_type=F32)


def dot_rows(a, b):
    return lax.dot_general(a, b, (((0,), (0,)), ((), ())), preferred_element_type=F32)


def seen_blocks(block):
    if block == 0:
        return [(0, 0)]
    if block == 1:
        return [(0, None), (1, 0)]
    return [(0, None), (1, None), (block, block - 1)]


def column(values, index):
    lanes = lax.broadcasted_iota(jnp.int32, (1, values.shape[1]), 1)
    return jnp.sum(jnp.where(lanes == index, values, 0.0), axis=1, keepdims=True)


def pick(slots_ref, place, by_block):
    result = by_block[0]
    for block in range(1, len(by_block)):
        here = jnp.full((1, result.shape[1]), slots_ref[block], jnp.int32) == place
        result = jnp.where(here, by_block[block], result)
    return result


def attend_pair(pair, blocks, head_size, slots_ref, x_ref, c_ref, mask_ref, o_ref, lse_ref):
    scale = head_size**-0.5

    def head(h, carry):
        lanes = lax.broadcasted_iota(jnp.int32, (1, 2 * head_size), 1)
        mine = lanes // head_size == h
        decays = [column(c_ref[b], 2 * pair + h) for b in range(blocks)]
        outs = []
        for block in range(blocks):
            query = jnp.where(mine, x_ref[slots_ref[block], 0] * scale, 0).astype(BF16)
            scores = []
            for other, mask in seen_blocks(block):
                s = dot_lanes(x_ref[slots_ref[other], 1], query) - decays[other]
                if mask is not None:
                    s = s + mask_ref[mask]
                scores.append(s)
            top = functools.reduce(
                jnp.maximum, [jnp.max(s, axis=0, keepdims=True) for s in scores]
            )
            total, mixed = 0.0, 0.0
            for s, (other, _) in zip(scores, seen_blocks(block)):
                weight = jnp.exp(s - top)
                total = total + jnp.sum(weight, axis=0, keepdims=True)
                mixed = mixed + dot_rows(x_ref[slots_ref[other], 2], weight.astype(BF16))
            lse_ref[pair, h, pl.ds(block, 1), :] = top + jnp.log(total)
            outs.append((mixed / total).T.astype(BF16))
        for place in range(blocks):
            o_ref[place] = jnp.where(mine, pick(slots_ref, place, outs), o_ref[place])
        return carry

    lax.fori_loop(0, 2, head, 0)


def sum_decay(blocks, slots_ref, log_ref, seen_ref, c_ref):
    total = 0.0
    for block in range(blocks):
        logs = log_ref[slots_ref[block]]
        high = logs.astype(BF16)
        rest = logs - high.astype(F32)
        middle = rest.astype(BF16)
        low = (rest - middle.astype(F32)).astype(BF16)
        seen = seen_ref[max(block - 1, 0)]
        local = dot_lanes(seen, high) + dot_lanes(seen, middle) + dot_lanes(seen, low)
        c_ref[block] = local + total if block < 2 else local
        if block == 0:
            total = local[local.shape[0] - 1 :, :]


class GroupExchange:
    def __init__(self, n_grp, send_sem, recv_sem):
        self.n_grp, self.send_sem, self.recv_sem = n_grp, send_sem, recv_sem
        self.f, self.z = lax.axis_index("fsdp"), lax.axis_index("grp")
        self.sent, self.landed = [], {}

    def send(self, key, index, source_of, target):
        self.landed[key] = (index, target)
        for k in range(1, self.n_grp):
            place = flip(self.z, k)
            copy = pltpu.make_async_remote_copy(
                src_ref=source_of(place),
                dst_ref=target(self.z),
                send_sem=self.send_sem.at[index, k],
                recv_sem=self.recv_sem.at[index, k],
                device_id={"fsdp": self.f, "grp": place},
                device_id_type=MESH,
            )
            copy.start()
            self.sent.append(copy)

    def wait(self, key):
        index, target = self.landed[key]
        for k in range(1, self.n_grp):
            place = flip(self.z, k)
            pltpu.make_async_remote_copy(
                src_ref=target(place),
                dst_ref=target(place),
                send_sem=self.send_sem.at[index, k],
                recv_sem=self.recv_sem.at[index, k],
                device_id={"fsdp": self.f, "grp": place},
                device_id_type=MESH,
            ).wait_recv()

    def finish(self):
        for copy in self.sent:
            copy.wait_send()


def forward_kernel(count, pairs, head_size, n_fsdp, n_grp, *refs):
    weights, refs = refs[:count], refs[count:]
    slots_ref, mixed_ref, log_ref, mask_ref, seen_ref = refs[:5]
    full, refs = refs[5 : 5 + count], refs[5 + count :]
    o_out, x_out, lse_ref, c_ref = refs[:4]
    gather_sems, refs = refs[4:7], refs[7:]
    x_refs, refs = refs[:pairs], refs[pairs:]
    o_refs, refs = refs[:pairs], refs[pairs:]
    logs_ref, send_sem, recv_sem, copy_sem = refs
    blocks = n_grp
    pair_width = 2 * head_size
    group_width = pairs * pair_width
    width = blocks * group_width
    z = lax.axis_index("grp")

    meet(n_fsdp, n_grp, False)
    gather = Gather(weights, full, *gather_sems, n_fsdp, n_grp)
    swap_heads = GroupExchange(n_grp, send_sem, recv_sem)
    started = itertools.count()

    def keep(source, target):
        copy = pltpu.make_async_copy(source, target, copy_sem.at[next(started)])
        copy.start()
        return copy

    def heads_of(part, place, pair):
        start = part * width + place * group_width + pair * pair_width
        return mixed_ref.at[:, pl.ds(pl.multiple_of(start, 128), pair_width)]

    own_logs = keep(log_ref.at[z], logs_ref.at[z])
    swap_heads.send("logs", 0, lambda place: log_ref.at[place], lambda place: logs_ref.at[place])
    own, late = [], []
    for pair in range(pairs):
        for part in range(3):
            swap_heads.send(
                (pair, part),
                1 + 4 * pair + part,
                lambda place, pair=pair, part=part: heads_of(part, place, pair),
                lambda place, pair=pair, part=part: x_refs[pair].at[place, part],
            )
            own.append(keep(heads_of(part, z, pair), x_refs[pair].at[z, part]))
        if pair == 0:
            gather.start()
    gather.run(0.1)
    own_logs.wait()
    swap_heads.wait("logs")
    sum_decay(blocks, slots_ref, logs_ref, seen_ref, c_ref)
    for pair in range(pairs):
        gather.run(0.16 + 0.12 * pair)
        for part in range(3):
            own[3 * pair + part].wait()
            swap_heads.wait((pair, part))
        attend_pair(
            pair, blocks, head_size, slots_ref, x_refs[pair], c_ref, mask_ref, o_refs[pair], lse_ref
        )
        late.append(keep(x_refs[pair], x_out.at[pair]))

        def columns(place, pair=pair):
            start = place * group_width + pair * pair_width
            return o_out.at[:, pl.ds(pl.multiple_of(start, 128), pair_width)]

        swap_heads.send(
            (pair, 3), 4 + 4 * pair, lambda place: o_refs[pair].at[place], columns
        )
        late.append(keep(o_refs[pair].at[z], columns(z)))
    gather.finish()
    for pair in range(pairs):
        swap_heads.wait((pair, 3))
    swap_heads.finish()
    for copy in late:
        copy.wait()


def forward_attention(weights, slots, mixed, logs, masks, seen, head_size, collective_id):
    n_fsdp, n_grp = lax.axis_size("fsdp"), lax.axis_size("grp")
    count = len(weights)
    tok, width = mixed.shape[0], mixed.shape[1] // 3
    pair_width = 2 * head_size
    pairs = width // n_grp // pair_width
    anywhere = pl.BlockSpec(memory_space=pl.ANY)
    vmem = pl.BlockSpec(memory_space=pltpu.VMEM)
    out = pl.pallas_call(
        functools.partial(forward_kernel, count, pairs, head_size, n_fsdp, n_grp),
        out_shape=gathered(weights, n_fsdp, n_grp)
        + [
            jax.ShapeDtypeStruct((tok, width), BF16),
            jax.ShapeDtypeStruct((pairs, n_grp, 3, tok, pair_width), BF16),
            jax.ShapeDtypeStruct((pairs, 2, 8, tok), F32),
            jax.ShapeDtypeStruct((n_grp, tok, logs.shape[1]), F32),
        ],
        in_specs=[anywhere] * count
        + [pl.BlockSpec(memory_space=pltpu.SMEM), anywhere, anywhere, vmem, vmem],
        out_specs=[anywhere] * count + [anywhere, anywhere, vmem, vmem],
        scratch_shapes=gather_scratch(weights, n_fsdp, n_grp)
        + [pltpu.VMEM((n_grp, 3, tok, pair_width), BF16)] * pairs
        + [pltpu.VMEM((n_grp, tok, pair_width), BF16)] * pairs
        + [
            pltpu.VMEM(logs.shape, F32),
            pltpu.SemaphoreType.DMA((1 + 4 * pairs, n_grp)),
            pltpu.SemaphoreType.DMA((1 + 4 * pairs, n_grp)),
            pltpu.SemaphoreType.DMA((1 + 5 * pairs,)),
        ],
        compiler_params=pltpu.CompilerParams(
            collective_id=collective_id, has_side_effects=True, vmem_limit_bytes=48 << 20
        ),
        name="forward_attention",
    )(*weights, slots, mixed, logs, masks, seen)
    return [v.reshape(-1, v.shape[2]) for v in out[:count]], out[count:]


def attend_back_pair(
    pair,
    blocks,
    head_size,
    slots_ref,
    x_ref,
    do_ref,
    c_ref,
    mask_ref,
    lse_ref,
    dx_ref,
    query_decay_ref,
    key_decay_ref,
):
    scale = head_size**-0.5

    def head(h, carry):
        lanes = lax.broadcasted_iota(jnp.int32, (1, 2 * head_size), 1)
        mine = lanes // head_size == h
        index = 2 * pair + h
        mine_decay = lax.broadcasted_iota(jnp.int32, (1, c_ref.shape[2]), 1) == index
        decays = [column(c_ref[b], index) for b in range(blocks)]
        query_grads = [None] * blocks
        key_grads, value_grads = [None] * blocks, [None] * blocks
        decay_grads = [None] * blocks

        def add(store, at, value):
            store[at] = value if store[at] is None else store[at] + value

        for block in range(blocks):
            query = jnp.where(mine, x_ref[slots_ref[block], 0] * scale, 0).astype(BF16)
            grad_o = jnp.where(mine, do_ref[slots_ref[block]], 0).astype(BF16)
            lse = lse_ref[pair, h, pl.ds(block, 1), :]
            weights, grads, delta = [], [], 0.0
            for other, mask in seen_blocks(block):
                s = dot_lanes(x_ref[slots_ref[other], 1], query) - decays[other]
                if mask is not None:
                    s = s + mask_ref[mask]
                weight = jnp.exp(s - lse)
                grad = dot_lanes(x_ref[slots_ref[other], 2], grad_o)
                delta = delta + jnp.sum(weight * grad, axis=0, keepdims=True)
                weights.append(weight)
                grads.append(grad)
            query_grad, query_decay = 0.0, 0.0
            for weight, grad, (other, _) in zip(weights, grads, seen_blocks(block)):
                ds = weight * (grad - delta)
                query_decay = query_decay + jnp.sum(ds, axis=0, keepdims=True)
                add(decay_grads, other, jnp.sum(ds, axis=1, keepdims=True))
                low = ds.astype(BF16)
                query_grad = query_grad + dot_rows(x_ref[slots_ref[other], 1], low)
                add(key_grads, other, jnp.dot(low, query, preferred_element_type=F32))
                add(
                    value_grads,
                    other,
                    jnp.dot(weight.astype(BF16), grad_o, preferred_element_type=F32),
                )
            query_grads[block] = (query_grad * scale).T
            turned = jnp.broadcast_to(query_decay, (c_ref.shape[2], query_decay.shape[1])).T
            query_decay_ref[block] = jnp.where(mine_decay, turned, query_decay_ref[block])
        for block in range(blocks):
            key_decay_ref[block] = jnp.where(
                mine_decay, decay_grads[block], key_decay_ref[block]
            )
        for part, by_block in enumerate((query_grads, key_grads, value_grads)):
            low = [v.astype(BF16) for v in by_block]
            for place in range(blocks):
                dx_ref[place, part] = jnp.where(
                    mine, pick(slots_ref, place, low), dx_ref[place, part]
                )
        return carry

    lax.fori_loop(0, 2, head, 0)


def split3(values):
    high = values.astype(BF16)
    rest = values - high.astype(F32)
    middle = rest.astype(BF16)
    return high, middle, (rest - middle.astype(F32)).astype(BF16)


def sum_decay_back(blocks, slots_ref, seen_ref, query_decay_ref, key_decay_ref, logs_ref):
    after = 0.0
    for block in range(2, blocks):
        after = after + jnp.sum(query_decay_ref[block], axis=0, keepdims=True)
    by_block = [None] * blocks
    for block in reversed(range(blocks)):
        grad = query_decay_ref[block] - key_decay_ref[block]
        seen = seen_ref[max(block - 1, 0)]
        value = sum(dot_rows(seen, part) for part in split3(grad))
        by_block[block] = value if block >= 2 else value + after
        if block == 1:
            after = after + jnp.sum(grad, axis=0, keepdims=True)
    for place in range(blocks):
        logs_ref[place] = pick(slots_ref, place, by_block)


def halving_orders(n_fsdp):
    bits = [1 << i for i in range(n_fsdp.bit_length() - 2)]
    return bits[::-1], bits


def kept_pieces(order):
    keep = [0]
    for bit in reversed(order[1:]):
        keep = keep + [k ^ bit for k in keep]
    return keep


class Scatter:
    AHEAD = 6

    def __init__(self, parts, send_sem, recv_sem, line_sem, local_sem, n_fsdp, n_grp):
        self.parts, self.n_grp = parts, n_grp
        self.send_sem, self.recv_sem = send_sem, recv_sem
        self.line_sem, self.local_sem = line_sem, local_sem
        self.f, self.z = lax.axis_index("fsdp"), lax.axis_index("grp")
        orders = halving_orders(n_fsdp)
        self.orders = [orders[i % 2] for i in range(len(parts))]
        self.keeps = [kept_pieces(o) for o in self.orders]
        self.up = {"fsdp": self.f, "grp": self.z + 1}
        self.down = {"fsdp": self.f, "grp": self.z - 1}
        self.across = {b: {"fsdp": flip(self.f, 2 * b), "grp": self.z} for b in orders[1]}
        self.sent, self.count = [], [0] * len(parts)

    def stage_of(self, part, k):
        order = self.orders[part]
        return next((i for i, b in enumerate(order) if k & b), len(order))

    def slot(self, part, k, stage):
        slots = [(v, j) for v in self.keeps[part] for j in range(self.stage_of(part, v))]
        return slots.index((k, stage))

    def _send(self, part, source, target, recv_sem, to):
        index = self.count[part]
        self.count[part] += 1

        def copy():
            return pltpu.make_async_remote_copy(
                src_ref=source(),
                dst_ref=target(),
                send_sem=self.send_sem.at[part, index],
                recv_sem=recv_sem(),
                device_id=to,
                device_id_type=MESH,
            )

        copy().start()
        return copy

    def _cross(self, part, place, k, stage, source):
        bit = self.orders[part][stage]
        slot = self.slot(part, k ^ bit, stage)
        copy = self._send(
            part,
            lambda: source,
            lambda: self.parts[part][3].at[slot, place],
            lambda: self.recv_sem.at[part, slot, place],
            self.across[bit],
        )
        self.sent.append((None, [copy]))

    def _arrived(self, target, recv_sem):
        pltpu.make_async_remote_copy(
            src_ref=target,
            dst_ref=target,
            send_sem=self.send_sem.at[0, 0],
            recv_sem=recv_sem,
            device_id=self.across[1],
            device_id_type=MESH,
        ).wait_recv()

    def _load(self, part, place, i):
        kept, held = self.parts[part][1:3]
        return pltpu.make_async_copy(
            kept.at[i, place], held.at[i, place], self.local_sem.at[part, i, place]
        )

    def _begin(self, part, place):
        away = self.parts[part][0]
        for i, k in reversed(list(enumerate(self.keeps[part]))):
            self._cross(part, place, k ^ self.orders[part][0], 0, away.at[i, place])
            self._load(part, place, i).start()

    def _add_arrived(self, part, place, k):
        held, arrived = self.parts[part][2], self.parts[part][3]
        i = self.keeps[part].index(k)
        self._load(part, place, i).wait()
        for stage in range(self.stage_of(part, k)):
            slot = self.slot(part, k, stage)
            self._arrived(arrived.at[slot, place], self.recv_sem.at[part, slot, place])
        total = held[i, place]
        for stage in range(self.stage_of(part, k)):
            total = total + arrived[self.slot(part, k, stage), place]
        held[i, place] = total
        return held.at[i, place]

    def _halve(self, part, place, k):
        source = self._add_arrived(part, place, k)
        self._cross(part, place, k, self.stage_of(part, k), source)

    def _when(self, condition, action):
        copies = []
        pl.when(condition)(lambda: copies.extend(action()))
        self.sent.append((condition, copies))

    def _line(self, part, place, hop):
        last = self.n_grp - 1
        held = self.parts[part][2]
        ways = []
        if hop < place:
            ways.append((self.z == hop, 4, 0, self.up))
        if last - hop > place:
            ways.append((self.z == last - hop, 5, 1, self.down))
        for condition, which, way, to in ways:
            passing = self.parts[part][which]

            def action(passing=passing, way=way, to=to):
                target = lambda: passing.at[place]
                sem = lambda: self.line_sem.at[part, way, place]
                if hop == 0:
                    return [self._send(part, lambda: held.at[0, place], target, sem, to)]
                self._arrived(target(), sem())
                passing[place] = passing[place] + held[0, place]
                return [self._send(part, target, target, sem, to)]

            self._when(condition, action)

    def _result(self, part):
        held, below, above, result, columns = (self.parts[part][i] for i in (2, 4, 5, 6, 7))
        z, last = self.z, self.n_grp - 1
        result[:, columns] = held[0, z].astype(F32)

        def add(passing, index):
            self._arrived(passing.at[z], self.line_sem.at[part, index, z])
            result[:, columns] = result[:, columns] + passing[z].astype(F32)

        pl.when(z > 0)(lambda: add(below, 0))
        pl.when(z < last)(lambda: add(above, 1))

    def waves(self):
        bind = functools.partial
        low, high, places = 0, self.n_grp - 1, []
        while low <= high:
            places += [high] if low == high else [high, low]
            low, high = low + 1, high - 1
        units = []
        for first in range(0, len(self.parts), 2):
            group = range(first, min(first + 2, len(self.parts)))
            units += [(part, place) for place in places for part in group]
        ahead, stages = self.AHEAD, len(self.orders[0])
        length = len(units) + ahead + 2 * stages + 2 * self.n_grp
        waves = [[] for _ in range(length)]
        final = {}
        for n, (part, place) in enumerate(units):
            waves[max(0, n + 1 - ahead)].append(bind(self._begin, part, place))
            at = n + 1
            for stage in range(1, stages):
                for k in self.keeps[part]:
                    if self.stage_of(part, k) == stage:
                        waves[at].append(bind(self._halve, part, place, k))
                at += 2
            waves[at].append(bind(self._add_arrived, part, place, 0))
            for hop in range(self.n_grp - 1):
                waves[at + 2 * hop].append(bind(self._line, part, place, hop))
            final[part] = at + 2 * (self.n_grp - 1)
        for part, at in final.items():
            waves[at].append(bind(self._result, part))
        return waves

    def finish(self):
        for condition, copies in self.sent:
            if condition is None:
                for copy in copies:
                    copy().wait_send()
            else:

                def wait_sent():
                    for copy in copies:
                        copy().wait_send()

                pl.when(condition)(wait_sent)


def scatter_scratch(aways, n_fsdp, n_grp):
    m = n_fsdp.bit_length() - 2
    keep = n_fsdp // 4
    slots = m + sum(i << (m - 1 - i) for i in range(1, m))
    parts = len(aways)
    shapes = [
        pltpu.SemaphoreType.DMA((parts, n_grp * (2 * keep + 2 * n_grp))),
        pltpu.SemaphoreType.DMA((parts, slots, n_grp)),
        pltpu.SemaphoreType.DMA((parts, 2, n_grp)),
        pltpu.SemaphoreType.DMA((parts, keep, n_grp)),
    ]
    for away in aways:
        rows, width = away.shape[2:]
        for leading in ((keep, n_grp), (slots, n_grp), (n_grp,), (n_grp,)):
            shapes.append(pltpu.VMEM(leading + (rows, width), BF16))
    return shapes


def scatter_parts(aways, kepts, buffers, results):
    parts = []
    places = [(ref, columns) for ref, ranges in results for columns in ranges]
    for i, (away, kept) in enumerate(zip(aways, kepts)):
        parts.append((away, kept, *buffers[4 * i : 4 * i + 4], *places[i]))
    return parts


def column_ranges(widths):
    start, ranges = 0, []
    for width in widths:
        ranges.append(pl.ds(start, width))
        start += width
    return ranges


def scatter_kernel(widths, n_fsdp, n_grp, *refs):
    count = sum(len(w) for w in widths)
    aways, kepts, refs = refs[:count], refs[count : 2 * count], refs[2 * count :]
    results, sems, buffers = refs[: len(widths)], refs[len(widths) :][:4], refs[len(widths) + 4 :]
    meet(n_fsdp, n_grp, True)
    places = [(ref, column_ranges(w)) for ref, w in zip(results, widths)]
    scatter = Scatter(scatter_parts(aways, kepts, buffers, places), *sems, n_fsdp, n_grp)
    for wave in scatter.waves():
        for step in wave:
            step()
    scatter.finish()


def scatter_rows(weights, collective_id):
    n_fsdp, n_grp = lax.axis_size("fsdp"), lax.axis_size("grp")
    aways = [away for parts in weights for away, _ in parts]
    kepts = [kept for parts in weights for _, kept in parts]
    widths = [[away.shape[3] for away, _ in parts] for parts in weights]
    return pl.pallas_call(
        functools.partial(scatter_kernel, widths, n_fsdp, n_grp),
        out_shape=[
            jax.ShapeDtypeStruct((parts[0][0].shape[2], sum(w)), F32)
            for parts, w in zip(weights, widths)
        ],
        in_specs=[pl.BlockSpec(memory_space=pl.ANY)] * (2 * len(aways)),
        out_specs=[pl.BlockSpec(memory_space=pltpu.VMEM)] * len(weights),
        scratch_shapes=scatter_scratch(aways, n_fsdp, n_grp),
        compiler_params=pltpu.CompilerParams(
            collective_id=collective_id, has_side_effects=True, vmem_limit_bytes=58 << 20
        ),
        name="scatter_rows",
    )(*aways, *kepts)


def backward_kernel(widths, pairs, head_size, n_fsdp, n_grp, *refs):
    count = sum(len(w) for w in widths)
    aways, kepts, refs = refs[:count], refs[count : 2 * count], refs[2 * count :]
    slots_ref, grad_ref, x_hbm, c_ref, mask_ref, seen_ref, lse_ref = refs[:7]
    results, refs = refs[7 : 7 + len(widths)], refs[7 + len(widths) :]
    mixed_out, logs_out = refs[:2]
    sems, buffers, refs = refs[2:6], refs[6 : 6 + 4 * count], refs[6 + 4 * count :]
    x_refs, refs = refs[:pairs], refs[pairs:]
    do_refs, refs = refs[:pairs], refs[pairs:]
    dx_refs, refs = refs[:pairs], refs[pairs:]
    query_decay_ref, key_decay_ref, logs_ref, send_sem, recv_sem, copy_sem = refs
    blocks = n_grp
    pair_width = 2 * head_size
    group_width = pairs * pair_width
    width = blocks * group_width
    z = lax.axis_index("grp")

    meet(n_fsdp, n_grp, False)
    places = [(ref, column_ranges(w)) for ref, w in zip(results, widths)]
    scatter = Scatter(scatter_parts(aways, kepts, buffers, places), *sems, n_fsdp, n_grp)
    swap_heads = GroupExchange(n_grp, send_sem, recv_sem)
    started = itertools.count()

    def keep(source, target):
        copy = pltpu.make_async_copy(source, target, copy_sem.at[next(started)])
        copy.start()
        return copy

    def heads_of(ref, part, place, pair):
        start = part * width + place * group_width + pair * pair_width
        return ref.at[:, pl.ds(pl.multiple_of(start, 128), pair_width)]

    own, late = [], []
    for pair in range(pairs):
        swap_heads.send(
            (pair, "do"),
            4 * pair,
            lambda place, pair=pair: heads_of(grad_ref, 0, place, pair),
            lambda place, pair=pair: do_refs[pair].at[place],
        )
        own.append(keep(heads_of(grad_ref, 0, z, pair), do_refs[pair].at[z]))
        own.append(keep(x_hbm.at[pair], x_refs[pair]))
    waves = iter(scatter.waves())

    def advance(count=None):
        for wave in itertools.islice(waves, count):
            for step in wave:
                step()

    advance(1)
    for pair in range(pairs):
        own[2 * pair].wait()
        own[2 * pair + 1].wait()
        swap_heads.wait((pair, "do"))
        attend_back_pair(
            pair,
            blocks,
            head_size,
            slots_ref,
            x_refs[pair],
            do_refs[pair],
            c_ref,
            mask_ref,
            lse_ref,
            dx_refs[pair],
            query_decay_ref,
            key_decay_ref,
        )
        for part in range(3):
            swap_heads.send(
                (pair, part),
                1 + 4 * pair + part,
                lambda place, pair=pair, part=part: dx_refs[pair].at[place, part],
                lambda place, pair=pair, part=part: heads_of(mixed_out, part, place, pair),
            )
            late.append(keep(dx_refs[pair].at[z, part], heads_of(mixed_out, part, z, pair)))
        advance(3)
    sum_decay_back(blocks, slots_ref, seen_ref, query_decay_ref, key_decay_ref, logs_ref)
    swap_heads.send(
        "logs",
        4 * pairs,
        lambda place: logs_ref.at[place],
        lambda place: logs_out.at[place],
    )
    late.append(keep(logs_ref.at[z], logs_out.at[z]))
    advance()
    for pair in range(pairs):
        for part in range(3):
            swap_heads.wait((pair, part))
    swap_heads.wait("logs")
    scatter.finish()
    swap_heads.finish()
    for copy in late:
        copy.wait()


def backward_attention(weights, slots, grad, x, decay, masks, seen, lse, head_size, collective_id):
    n_fsdp, n_grp = lax.axis_size("fsdp"), lax.axis_size("grp")
    aways = [away for parts in weights for away, _ in parts]
    kepts = [kept for parts in weights for _, kept in parts]
    widths = [[away.shape[3] for away, _ in parts] for parts in weights]
    pairs, _, _, tok, pair_width = x.shape
    lanes = decay.shape[2]
    anywhere = pl.BlockSpec(memory_space=pl.ANY)
    vmem = pl.BlockSpec(memory_space=pltpu.VMEM)
    out = pl.pallas_call(
        functools.partial(backward_kernel, widths, pairs, head_size, n_fsdp, n_grp),
        out_shape=[
            jax.ShapeDtypeStruct((parts[0][0].shape[2], sum(w)), F32)
            for parts, w in zip(weights, widths)
        ]
        + [
            jax.ShapeDtypeStruct((tok, 3 * grad.shape[1]), BF16),
            jax.ShapeDtypeStruct((n_grp, tok, lanes), F32),
        ],
        in_specs=[anywhere] * (2 * len(aways))
        + [pl.BlockSpec(memory_space=pltpu.SMEM), anywhere, anywhere]
        + [vmem] * 4,
        out_specs=[vmem] * len(weights) + [anywhere] * 2,
        scratch_shapes=scatter_scratch(aways, n_fsdp, n_grp)
        + [pltpu.VMEM((n_grp, 3, tok, pair_width), BF16)] * pairs
        + [pltpu.VMEM((n_grp, tok, pair_width), BF16)] * pairs
        + [pltpu.VMEM((n_grp, 3, tok, pair_width), BF16)] * pairs
        + [pltpu.VMEM((n_grp, tok, lanes), F32)] * 3
        + [
            pltpu.SemaphoreType.DMA((1 + 4 * pairs, n_grp)),
            pltpu.SemaphoreType.DMA((1 + 4 * pairs, n_grp)),
            pltpu.SemaphoreType.DMA((1 + 5 * pairs,)),
        ],
        compiler_params=pltpu.CompilerParams(
            collective_id=collective_id, has_side_effects=True, vmem_limit_bytes=62 << 20
        ),
        name="backward_attention",
    )(*aways, *kepts, slots, grad, x, decay, masks, seen, lse)
    return out[: len(weights)], out[len(weights)], out[len(weights) + 1]


def weight_grad_kernel(count, own_ids, other_ids, l_ref, l_other_ref, r_ref, r_other_ref, *outs):
    def side(ref, ids):
        return jnp.concatenate([ref[ids[k]] for k in range(2 * count)], axis=0)

    total = jnp.dot(side(l_ref, own_ids), r_ref[...], preferred_element_type=F32)
    total = total + jnp.dot(
        side(l_other_ref, other_ids), r_other_ref[...], preferred_element_type=F32
    )
    total = total.astype(BF16).reshape(2 * count, -1, total.shape[1])
    outs[0][...] = total[:count]
    outs[1][...] = total[count:]


def weight_grad(own_ids, other_ids, l_own, l_other, r_own, r_other, start, width):
    count = own_ids.shape[0] // 2
    _, rows, tok = l_own.shape
    limit = 1536 if rows * count < 1024 else 512
    tile = max(t for t in range(128, limit + 1, 128) if width % t == 0 and start % t == 0)
    steps, first = width // tile, start // tile
    whole = lambda v: pl.BlockSpec(v.shape, lambda n, own, other: (0, 0, 0))
    r_spec = pl.BlockSpec((tok, tile), lambda n, own, other: (0, first + n))
    out_spec = pl.BlockSpec((count, rows, tile), lambda n, own, other: (0, 0, n))
    return pl.pallas_call(
        functools.partial(weight_grad_kernel, count),
        out_shape=[jax.ShapeDtypeStruct((count, rows, width), BF16)] * 2,
        grid_spec=pltpu.PrefetchScalarGridSpec(
            num_scalar_prefetch=2,
            grid=(steps,),
            in_specs=[whole(l_own), whole(l_other), r_spec, r_spec],
            out_specs=[out_spec, out_spec],
        ),
        compiler_params=pltpu.CompilerParams(vmem_limit_bytes=48 << 20),
        cost_estimate=pl.CostEstimate(
            flops=8 * count * rows * tok * width,
            bytes_accessed=2 * (2 * count * rows * width + 2 * tok * width),
            transcendentals=0,
        ),
        name="weight_grad",
    )(own_ids, other_ids, l_own, l_other, r_own, r_other)


def split_rows(left):
    n_fsdp = lax.axis_size("fsdp")
    turned = left.T.reshape(n_fsdp, left.shape[1] // n_fsdp, left.shape[0])
    parity = lax.axis_index("fsdp") % 2
    halves = turned.reshape(n_fsdp // 2, 2, *turned.shape[1:])
    away = lax.dynamic_index_in_dim(halves, 1 - parity, 1, keepdims=False)
    return turned, swap(away, "fsdp", 1)


def partial_rows(left, columns):
    n_fsdp, n_grp = lax.axis_size("fsdp"), lax.axis_size("grp")
    f = lax.axis_index("fsdp")
    parts = []
    for part, (right, right_other, start, width) in enumerate(columns):
        order = halving_orders(n_fsdp)[part % 2]
        keep = kept_pieces(order)
        ids = jnp.stack([flip(f // 2, k) for k in [k ^ order[0] for k in keep] + keep])
        pair = weight_grad(
            2 * ids + f % 2, ids, left[0], left[1], right, right_other, start, width
        )
        parts.append(
            tuple(v.reshape(v.shape[0], n_grp, v.shape[1] // n_grp, width) for v in pair)
        )
    return parts


def sum_everywhere(values):
    for axis in ("grp", "fsdp"):
        mask = 1
        while mask < lax.axis_size(axis):
            values = values + swap(values, axis, mask)
            mask *= 2
    return values


def norm_rows(features):
    row_scale = lax.rsqrt(jnp.mean(features * features, axis=-1, keepdims=True) + EPSILON)
    return (features * row_scale, row_scale)


def norm_back(grad_normed, normed, row_scale):
    average_addend = jnp.mean(grad_normed * normed, axis=-1, keepdims=True)
    return row_scale * (grad_normed - normed * average_addend)


def contract_cols(first_op, second_op):
    return lax.dot_general(
        first_op, second_op, (((1,), (1,)), ((), ())), preferred_element_type=F32
    )


def on_device(
    tokens,
    block_order,
    cont_lengths,
    gain_attn,
    w_qkv,
    w_forget,
    b_forget,
    w_out,
    gain_ffn,
    w_gate_up,
    w_down,
    grad_out,
):
    tok, width = tokens.shape
    heads = w_forget.shape[1]
    head_size = width // heads
    blocks = lax.axis_size("grp")
    own_heads = heads // blocks
    pairs = own_heads // 2
    group_width = width // blocks
    slots = block_order[0]

    positions = jnp.arange(tok, dtype=jnp.int32)
    causal = positions[None, :] <= positions[:, None]
    seg_ends = jnp.cumsum(cont_lengths[0], axis=1)
    segment = jnp.sum((positions[None, :, None] >= seg_ends[:, None, :]).astype(jnp.int32), axis=2)
    within = jnp.logical_and(segment[:, :, None] == segment[:, None, :], causal[None])
    seen = jnp.concatenate([causal[None], within], axis=0)
    masks = jnp.where(seen.transpose(0, 2, 1), 0.0, NEG).astype(F32)
    seen_low = seen.astype(BF16)

    forget_pad = 128 - heads
    qkv_full, forget_full = gather_rows(
        [w_qkv, jnp.pad(w_forget, ((0, 0), (0, forget_pad)))], 1
    )
    inputs = tokens.astype(F32)
    normed_one, scale_one = norm_rows(inputs)
    acts = (normed_one * gain_attn).astype(BF16)
    grad_out_other = swap(grad_out, "fsdp", 1)
    acts_rows = split_rows(acts)
    logits = jnp.dot(acts, forget_full, preferred_element_type=F32)[:, :heads] + b_forget
    log_keep = jax.nn.log_sigmoid(logits)
    mixed = jnp.dot(acts, qkv_full, preferred_element_type=F32).astype(BF16)

    logs = jnp.pad(
        log_keep.T.reshape(blocks, own_heads, tok), ((0, 0), (0, 8 - own_heads), (0, 0))
    )
    (out_full, gate_up_full, down_full), (attn_o, x, lse, decay) = forward_attention(
        [w_out, w_gate_up, w_down], slots, mixed, logs, masks, seen_low, head_size, 2
    )

    attn_rows = split_rows(attn_o)
    resid = inputs + jnp.dot(attn_o, out_full, preferred_element_type=F32)
    normed_two, scale_two = norm_rows(resid)
    acts_two = (normed_two * gain_ffn).astype(BF16)
    acts_two_rows = split_rows(acts_two)
    ffn_width = down_full.shape[0]
    both = jnp.dot(acts_two, gate_up_full, preferred_element_type=F32)
    gate = both[:, :ffn_width]
    up_part = both[:, ffn_width:]
    sigma = jax.nn.sigmoid(gate)
    swish = gate * sigma
    inner_act = (swish * up_part).astype(BF16)
    half = width // 2
    down_rows = split_rows(inner_act)
    result = resid + jnp.dot(inner_act, down_full, preferred_element_type=F32)
    output = result.astype(BF16)

    grad_inner = contract_cols(grad_out, down_full)
    slope = sigma * (1.0 + gate * (1.0 - sigma))
    grad_both = jnp.concatenate(
        [grad_inner * up_part * slope, grad_inner * swish], axis=1
    ).astype(BF16)
    grad_both_other = swap(grad_both, "fsdp", 1)
    grad_acts_two = contract_cols(grad_both, gate_up_full)
    gain_two_grad = jnp.sum(grad_acts_two * normed_two, axis=0)
    grad_resid = grad_out.astype(F32) + norm_back(
        grad_acts_two * gain_ffn, normed_two, scale_two
    )
    grad_branch = grad_resid.astype(BF16)
    grad_branch_other = swap(grad_branch, "fsdp", 1)
    grad_heads = contract_cols(grad_branch, out_full).astype(BF16)
    part_down = partial_rows(
        down_rows, [(grad_out, grad_out_other, 0, half), (grad_out, grad_out_other, half, half)]
    )
    part_gate_up = partial_rows(
        acts_two_rows,
        [
            (grad_both, grad_both_other, 0, ffn_width),
            (grad_both, grad_both_other, ffn_width, ffn_width),
        ],
    )
    part_out = partial_rows(
        attn_rows,
        [
            (grad_branch, grad_branch_other, 0, half),
            (grad_branch, grad_branch_other, half, half),
        ],
    )

    (grad_down, grad_gate_up, grad_out_w), grad_mixed, log_grad = backward_attention(
        [part_down, part_gate_up, part_out],
        slots,
        grad_heads,
        x,
        decay,
        masks,
        seen_low,
        lse,
        head_size,
        3,
    )
    log_grad = log_grad[:, :, :own_heads].transpose(1, 0, 2).reshape(tok, heads)
    grad_logits = (log_grad * jax.nn.sigmoid(-logits)).astype(BF16)
    part = 3 * width // 2
    narrow = jnp.pad(grad_logits, ((0, 0), (0, forget_pad)))
    last = jnp.concatenate([grad_mixed[:, part:], narrow], axis=1)
    part_qkv = partial_rows(
        acts_rows,
        [
            (grad_mixed, swap(grad_mixed, "fsdp", 1), 0, part),
            (last, swap(last, "fsdp", 1), 0, part + 128),
        ],
    )
    (grad_wide,) = scatter_rows([part_qkv], 4)
    grad_qkv, grad_forget = grad_wide[:, : 3 * width], grad_wide[:, 3 * width :][:, :heads]
    grad_acts = contract_cols(grad_mixed, qkv_full) + contract_cols(
        grad_logits, forget_full[:, :heads]
    )
    gain_one_grad = jnp.sum(grad_acts * normed_one, axis=0)
    bias_grad = jnp.sum(grad_logits.astype(F32), axis=0)
    grad_inputs = grad_resid + norm_back(grad_acts * gain_attn, normed_one, scale_one)
    small = sum_everywhere(jnp.concatenate([gain_one_grad, gain_two_grad, bias_grad]))
    return (
        output,
        grad_inputs.astype(BF16),
        small[:width],
        grad_qkv,
        grad_forget,
        small[2 * width :],
        grad_out_w,
        small[width : 2 * width],
        grad_gate_up,
        grad_down,
    )


def solution(mesh):
    both = P(("fsdp", "grp"), None)
    in_specs = (
        both,
        P("fsdp", None),
        P("fsdp", None, None),
        P(),
        both,
        both,
        P(),
        both,
        P(),
        both,
        both,
        both,
    )
    out_specs = (both, both, P(), both, both, P(), both, P(), both, both)
    return jax.shard_map(
        on_device, mesh=mesh, in_specs=in_specs, out_specs=out_specs, check_vma=False
    )
```

```python
import functools
import itertools

import jax
import jax.numpy as jnp
from jax import lax
from jax.experimental import pallas as pl
from jax.experimental.pallas import tpu as pltpu
from jax.sharding import PartitionSpec as P

EPSILON = 1e-05
NEG = -1e30
AHEAD = 6
MESH = pl.DeviceIdType.MESH
F32 = jnp.float32
BF16 = jnp.bfloat16


def flip_bit(value, bit):
    return value + bit - 2 * bit * ((value // bit) % 2)


def flip(value, mask):
    bit = 1
    while bit <= mask:
        if mask & bit:
            value = flip_bit(value, bit)
        bit *= 2
    return value


def swap(value, axis, mask):
    return lax.ppermute(value, axis, [(i, i ^ mask) for i in range(lax.axis_size(axis))])


def gather_parts(shapes):
    return [(w, h) for w, s in enumerate(shapes) for h in (0, 1) if h == 0 or s[1] % 256 == 0]


class Gather:
    def __init__(self, kinds, ins, outs, send_sem, recv_sem, local_sem, n_fsdp, n_grp):
        self.kinds, self.ins, self.outs = kinds, ins, outs
        self.send_sem, self.recv_sem = send_sem, recv_sem
        self.f, self.z, self.n_grp = lax.axis_index("fsdp"), lax.axis_index("grp"), n_grp
        self.bits = [1 << i for i in range(1, n_fsdp.bit_length() - 1)]
        self.parts = gather_parts([r.shape[-2:] for r in ins])
        self.orders = [self.bits if h == 0 else self.bits[::-1] for _, h in self.parts]
        self.across = {b: {"fsdp": flip(self.f, b), "grp": self.z} for b in self.bits + [1]}
        self.up = {"fsdp": self.f, "grp": self.z + 1}
        self.down = {"fsdp": self.f, "grp": self.z - 1}
        self.count, self.sent, self.local = 0, [], []
        for w in range(len(ins)):
            target = {
                "full": self.f * n_grp + self.z,
                "line": self.z,
                "lined": pl.ds(self.f * n_grp, n_grp),
            }[kinds[w]]
            self.local.append(
                pltpu.make_async_copy(ins[w], outs[w].at[target], local_sem.at[w])
            )
        self.steps, self.done = self._steps(), 0

    def _columns(self, part):
        w, h = self.parts[part]
        width = self.ins[w].shape[-1]
        return pl.ds(0, width) if width % 256 else pl.ds(h * (width // 2), width // 2)

    def kind(self, part):
        return self.kinds[self.parts[part][0]]

    def _piece(self, part, fk, place):
        row = place if self.kind(part) == "line" else flip(self.f, fk) * self.n_grp + place
        return self.outs[self.parts[part][0]].at[row, :, self._columns(part)]

    def _send(self, part, fk, place, to, to_fk, own=False):
        index = self.count
        self.count += 1

        def copy():
            source = self._piece(part, fk, place)
            if own:
                source = self.ins[self.parts[part][0]]
                source = source.at[place] if self.kind(part) == "lined" else source
                source = source.at[:, self._columns(part)]
            return pltpu.make_async_remote_copy(
                src_ref=source,
                dst_ref=self._piece(part, fk, place),
                send_sem=self.send_sem.at[index],
                recv_sem=self.recv_sem.at[part, to_fk, place],
                device_id=to,
                device_id_type=MESH,
            )

        copy().start()
        return copy

    def _wait(self, part, fk, place):
        piece = self._piece(part, fk, place)
        pltpu.make_async_remote_copy(
            src_ref=piece,
            dst_ref=piece,
            send_sem=self.send_sem.at[0],
            recv_sem=self.recv_sem.at[part, fk, place],
            device_id=self.across[1],
            device_id_type=MESH,
        ).wait_recv()

    def _forward(self, part, stage, fk, place, own=False):
        if self.kind(part) == "line":
            return []
        return [
            self._send(part, fk, place, self.across[b], fk ^ b, own)
            for b in self.orders[part][stage:] + [1]
        ]

    def _when(self, condition, action):
        copies = []
        pl.when(condition)(lambda: copies.extend(action()))
        self.sent.append((condition, copies))

    def start(self):
        for copy in self.local:
            copy.start()
        last = self.n_grp - 1
        for part in range(len(self.parts)):
            if self.kind(part) == "lined":
                for place in range(self.n_grp):
                    self.sent.append((None, self._forward(part, 0, 0, place, True)))
                continue
            self._when(
                self.z < last, lambda: [self._send(part, 0, self.z, self.up, 0, True)]
            )
            self._when(self.z > 0, lambda: [self._send(part, 0, self.z, self.down, 0, True)])
            self.sent.append((None, self._forward(part, 0, 0, self.z, True)))

    def _line_step(self, part, j):
        z, last = self.z, self.n_grp - 1
        below, above = z - j, z + j

        def arrive(place):
            self._wait(part, 0, place)
            return self._forward(part, 0, 0, place)

        self._when(z >= j, lambda: arrive(below))
        if j < last:
            self._when(
                jnp.logical_and(z >= j, z < last),
                lambda: [self._send(part, 0, below, self.up, 0)],
            )
        self._when(above <= last, lambda: arrive(above))
        if j < last:
            self._when(
                jnp.logical_and(above <= last, z > 0),
                lambda: [self._send(part, 0, above, self.down, 0)],
            )

    def _cross_step(self, part, stage, fk, place):
        self._wait(part, fk, place)
        self.sent.append((None, self._forward(part, stage + 1, fk, place)))

    def _steps(self):
        lines = [p for p in range(len(self.parts)) if self.kind(p) != "lined"]
        crossing = [p for p in range(len(self.parts)) if self.kind(p) != "line"]
        early = [p for p in crossing if self.kind(p) == "lined"]
        bind = functools.partial

        def cross(parts, stage):
            known = [[0] for _ in parts]
            for i in range(stage):
                known = [
                    k + [v ^ self.orders[p][i] for v in k] for p, k in zip(parts, known)
                ]
            return [
                bind(self._cross_step, p, stage, k[a] ^ self.orders[p][stage], place)
                for a in range(len(known[0]) if parts else 0)
                for place in range(self.n_grp)
                for p, k in zip(parts, known)
            ]

        ahead = cross(early, 0)
        steps, self.marks = [], []
        for j in range(1, self.n_grp):
            steps += [bind(self._line_step, part, j) for part in lines]
            self.marks.append(len(steps))
            share = -(-len(ahead) // (self.n_grp - j))
            steps, ahead = steps + ahead[:share], ahead[share:]
        for stage in range(len(self.bits)):
            steps += cross([p for p in crossing if stage or p not in early], stage)
        everything = [0]
        for bit in self.bits:
            everything = everything + [v ^ bit for v in everything]
        for fk in everything:
            for place in range(self.n_grp):
                for p in crossing:
                    steps.append(bind(self._wait, p, fk ^ 1, place))
        return steps

    def run(self, until=None):
        until = len(self.steps) if until is None else until
        for step in self.steps[self.done : until]:
            step()
        self.done = max(self.done, until)

    def finish(self):
        self.run()
        for copy in self.local:
            copy.wait()
        for condition, copies in self.sent:
            if condition is None:
                for copy in copies:
                    copy().wait_send()
            else:

                def wait_sent():
                    for copy in copies:
                        copy().wait_send()

                pl.when(condition)(wait_sent)


def gather_scratch(weights, n_fsdp, n_grp):
    parts = len(gather_parts([w.shape[-2:] for w in weights]))
    bits = n_fsdp.bit_length() - 2
    crossing = n_fsdp // 2 - 1 + n_fsdp // 2
    sends = 2 + (n_grp - 1) * 2 * (bits + 1) + 2 * (n_grp - 2) + n_grp * crossing + bits + 1
    return [
        pltpu.SemaphoreType.DMA((parts * sends,)),
        pltpu.SemaphoreType.DMA((parts, n_fsdp, n_grp)),
        pltpu.SemaphoreType.DMA((len(weights),)),
    ]


def gathered(kinds, weights, n_fsdp, n_grp):
    return [
        jax.ShapeDtypeStruct(
            (n_grp if kind == "line" else n_fsdp * n_grp,) + w.shape[-2:], w.dtype
        )
        for kind, w in zip(kinds, weights)
    ]


def meet(n_fsdp, n_grp, line_only):
    f, z = lax.axis_index("fsdp"), lax.axis_index("grp")
    barrier = pltpu.get_barrier_semaphore()
    bits = [1 << i for i in range(n_fsdp.bit_length() - 1)]
    peers = [{"fsdp": flip(f, b), "grp": z} for b in bits]
    peers += [{"fsdp": f, "grp": flip(z, k)} for k in range(1, n_grp)]
    for peer in peers:
        pl.semaphore_signal(barrier, inc=1, device_id=peer, device_id_type=MESH)
    pl.semaphore_wait(barrier, len(peers))


def gather_kernel(kinds, n_fsdp, n_grp, *refs):
    meet(n_fsdp, n_grp, True)
    count = len(kinds)
    ins, outs, sems = refs[:count], refs[count : 2 * count], refs[2 * count :]
    first = [i for i, kind in enumerate(kinds) if kind == "full"]
    second = [i for i, kind in enumerate(kinds) if kind == "line"]
    gathers = [
        Gather(
            [kinds[i] for i in chosen],
            [ins[i] for i in chosen],
            [outs[i] for i in chosen],
            *sems[3 * n : 3 * n + 3],
            n_fsdp,
            n_grp,
        )
        for n, chosen in enumerate((first, second))
    ]
    gathers[0].start()
    gathers[0].run(gathers[0].marks[-2])
    gathers[1].start()
    gathers[0].run(gathers[0].marks[-1])
    for n in range(len(gathers[1].steps)):
        share = (len(gathers[0].steps) - gathers[0].marks[-1]) * (n + 1)
        gathers[0].run(gathers[0].marks[-1] + share // (2 * len(gathers[1].steps)))
        gathers[1].run(n + 1)
    for gather in gathers:
        gather.finish()


def gather_rows(kinds, weights, collective_id):
    n_fsdp, n_grp = lax.axis_size("fsdp"), lax.axis_size("grp")
    count = len(weights)
    return pl.pallas_call(
        functools.partial(gather_kernel, kinds, n_fsdp, n_grp),
        out_shape=gathered(kinds, weights, n_fsdp, n_grp),
        in_specs=[pl.BlockSpec(memory_space=pl.ANY)] * count,
        out_specs=[pl.BlockSpec(memory_space=pl.ANY)] * count,
        scratch_shapes=[
            v
            for kind in ("full", "line")
            for v in gather_scratch([w for k, w in zip(kinds, weights) if k == kind], n_fsdp, n_grp)
        ],
        compiler_params=pltpu.CompilerParams(
            collective_id=collective_id, has_side_effects=True
        ),
        name="gather_rows",
    )(*weights)


def dot_lanes(a, b):
    return lax.dot_general(a, b, (((1,), (1,)), ((), ())), preferred_element_type=F32)


def dot_rows(a, b):
    return lax.dot_general(a, b, (((0,), (0,)), ((), ())), preferred_element_type=F32)


def seen_blocks(block):
    if block == 0:
        return [(0, 0)]
    if block == 1:
        return [(0, None), (1, 0)]
    return [(0, None), (1, None), (block, block - 1)]


def column(values, index):
    lanes = lax.broadcasted_iota(jnp.int32, (1, values.shape[1]), 1)
    return jnp.sum(jnp.where(lanes == index, values, 0.0), axis=1, keepdims=True)


def pick(slots_ref, place, by_block):
    result = by_block[0]
    for block in range(1, len(by_block)):
        here = jnp.full((1, result.shape[1]), slots_ref[block], jnp.int32) == place
        result = jnp.where(here, by_block[block], result)
    return result


def attend_head(
    pair, h, blocks, head_size, slots_ref, x_ref, c_ref, mask_ref, o_ref, lse_ref
):
    scale = head_size**-0.5

    def head():
        lanes = lax.broadcasted_iota(jnp.int32, (1, 2 * head_size), 1)
        mine = lanes // head_size == h
        decays = [column(c_ref[b], 2 * pair + h) for b in range(blocks)]
        outs = []
        for block in range(blocks):
            query = jnp.where(mine, x_ref[slots_ref[block], 0] * scale, 0).astype(BF16)
            scores = []
            for other, mask in seen_blocks(block):
                s = dot_lanes(x_ref[slots_ref[other], 1], query) - decays[other]
                if mask is not None:
                    s = s + mask_ref[mask]
                scores.append(s)
            top = functools.reduce(
                jnp.maximum, [jnp.max(s, axis=0, keepdims=True) for s in scores]
            )
            total, mixed = 0.0, 0.0
            for s, (other, _) in zip(scores, seen_blocks(block)):
                weight = jnp.exp(s - top)
                total = total + jnp.sum(weight, axis=0, keepdims=True)
                mixed = mixed + dot_rows(x_ref[slots_ref[other], 2], weight.astype(BF16))
            lse_ref[pair, h, pl.ds(block, 1), :] = top + jnp.log(total)
            outs.append((mixed / total).T.astype(BF16))
        for place in range(blocks):
            o_ref[place] = jnp.where(mine, pick(slots_ref, place, outs), o_ref[place])

    head()


def sum_decay(blocks, slots_ref, log_ref, seen_ref, c_ref):
    total = 0.0
    for block in range(blocks):
        logs = log_ref[slots_ref[block]]
        high = logs.astype(BF16)
        rest = logs - high.astype(F32)
        middle = rest.astype(BF16)
        low = (rest - middle.astype(F32)).astype(BF16)
        seen = seen_ref[max(block - 1, 0)]
        local = dot_lanes(seen, high) + dot_lanes(seen, middle) + dot_lanes(seen, low)
        c_ref[block] = local + total if block < 2 else local
        if block == 0:
            total = local[local.shape[0] - 1 :, :]


class GroupExchange:
    def __init__(self, n_grp, send_sem, recv_sem):
        self.n_grp, self.send_sem, self.recv_sem = n_grp, send_sem, recv_sem
        self.f, self.z = lax.axis_index("fsdp"), lax.axis_index("grp")
        self.sent, self.landed = [], {}

    def send(self, key, index, source_of, target):
        self.landed[key] = (index, target)
        for k in range(1, self.n_grp):
            place = flip(self.z, k)
            copy = pltpu.make_async_remote_copy(
                src_ref=source_of(place),
                dst_ref=target(self.z),
                send_sem=self.send_sem.at[index, k],
                recv_sem=self.recv_sem.at[index, k],
                device_id={"fsdp": self.f, "grp": place},
                device_id_type=MESH,
            )
            copy.start()
            self.sent.append(copy)

    def wait(self, key):
        index, target = self.landed[key]
        for k in range(1, self.n_grp):
            place = flip(self.z, k)
            pltpu.make_async_remote_copy(
                src_ref=target(place),
                dst_ref=target(place),
                send_sem=self.send_sem.at[index, k],
                recv_sem=self.recv_sem.at[index, k],
                device_id={"fsdp": self.f, "grp": place},
                device_id_type=MESH,
            ).wait_recv()

    def finish(self):
        for copy in self.sent:
            copy.wait_send()


def forward_kernel(kinds, pairs, head_size, n_fsdp, n_grp, *refs):
    count = len(kinds)
    weights, refs = refs[:count], refs[count:]
    slots_ref, mixed_ref, log_ref, mask_ref, seen_ref = refs[:5]
    full, refs = refs[5 : 5 + count], refs[5 + count :]
    o_out, x_out, lse_ref, c_ref = refs[:4]
    gather_sems, refs = refs[4:7], refs[7:]
    x_refs, refs = refs[:pairs], refs[pairs:]
    o_refs, refs = refs[:pairs], refs[pairs:]
    logs_ref, send_sem, recv_sem, copy_sem = refs
    blocks = n_grp
    pair_width = 2 * head_size
    group_width = pairs * pair_width
    width = blocks * group_width
    z = lax.axis_index("grp")

    meet(n_fsdp, n_grp, False)
    gather = Gather(kinds, weights, full, *gather_sems, n_fsdp, n_grp)
    swap_heads = GroupExchange(n_grp, send_sem, recv_sem)
    started = itertools.count()

    def keep(source, target):
        copy = pltpu.make_async_copy(source, target, copy_sem.at[next(started)])
        copy.start()
        return copy

    def heads_of(part, place, pair):
        start = part * width + place * group_width + pair * pair_width
        return mixed_ref.at[:, pl.ds(pl.multiple_of(start, 128), pair_width)]

    own = []

    def send_pair(pair):
        for part in range(3):
            swap_heads.send(
                (pair, part),
                1 + 4 * pair + part,
                lambda place, pair=pair, part=part: heads_of(part, place, pair),
                lambda place, pair=pair, part=part: x_refs[pair].at[place, part],
            )
            own.append(keep(heads_of(part, z, pair), x_refs[pair].at[z, part]))

    late = []
    own_logs = keep(log_ref.at[z], logs_ref.at[z])
    swap_heads.send("logs", 0, lambda place: log_ref.at[place], lambda place: logs_ref.at[place])
    gather.start()
    send_pair(0)
    for pair in range(1, pairs):
        if pair <= len(gather.marks):
            gather.run(gather.marks[pair - 1])
        send_pair(pair)
    own_logs.wait()
    swap_heads.wait("logs")
    sum_decay(blocks, slots_ref, logs_ref, seen_ref, c_ref)
    last_wait = len(gather.steps) * 3 // 5
    share = -(-(last_wait - gather.done) // (2 * pairs))
    for pair in range(pairs):
        for part in range(3):
            own[3 * pair + part].wait()
            swap_heads.wait((pair, part))
        for h in range(2):
            attend_head(
                pair, h, blocks, head_size, slots_ref, x_refs[pair], c_ref, mask_ref,
                o_refs[pair], lse_ref,
            )
            if h == 0:
                late.append(keep(x_refs[pair], x_out.at[pair]))
                gather.run(gather.done + share)

        def columns(place, pair=pair):
            start = place * group_width + pair * pair_width
            return o_out.at[:, pl.ds(pl.multiple_of(start, 128), pair_width)]

        swap_heads.send(
            (pair, 3), 4 + 4 * pair, lambda place: o_refs[pair].at[place], columns
        )
        late.append(keep(o_refs[pair].at[z], columns(z)))
        gather.run(gather.done + share)
    gather.finish()
    for pair in range(pairs):
        swap_heads.wait((pair, 3))
    swap_heads.finish()
    for copy in late:
        copy.wait()


def forward_attention(kinds, weights, slots, mixed, logs, masks, seen, head_size, collective_id):
    n_fsdp, n_grp = lax.axis_size("fsdp"), lax.axis_size("grp")
    count = len(weights)
    tok, width = mixed.shape[0], mixed.shape[1] // 3
    pair_width = 2 * head_size
    pairs = width // n_grp // pair_width
    anywhere = pl.BlockSpec(memory_space=pl.ANY)
    vmem = pl.BlockSpec(memory_space=pltpu.VMEM)
    out = pl.pallas_call(
        functools.partial(forward_kernel, kinds, pairs, head_size, n_fsdp, n_grp),
        out_shape=gathered(kinds, weights, n_fsdp, n_grp)
        + [
            jax.ShapeDtypeStruct((tok, width), BF16),
            jax.ShapeDtypeStruct((pairs, n_grp, 3, tok, pair_width), BF16),
            jax.ShapeDtypeStruct((pairs, 2, 8, tok), F32),
            jax.ShapeDtypeStruct((n_grp, tok, logs.shape[1]), F32),
        ],
        in_specs=[anywhere] * count
        + [pl.BlockSpec(memory_space=pltpu.SMEM), anywhere, anywhere, vmem, vmem],
        out_specs=[anywhere] * count + [anywhere, anywhere, vmem, vmem],
        scratch_shapes=gather_scratch(weights, n_fsdp, n_grp)
        + [pltpu.VMEM((n_grp, 3, tok, pair_width), BF16)] * pairs
        + [pltpu.VMEM((n_grp, tok, pair_width), BF16)] * pairs
        + [
            pltpu.VMEM(logs.shape, F32),
            pltpu.SemaphoreType.DMA((1 + 4 * pairs, n_grp)),
            pltpu.SemaphoreType.DMA((1 + 4 * pairs, n_grp)),
            pltpu.SemaphoreType.DMA((1 + 5 * pairs,)),
        ],
        compiler_params=pltpu.CompilerParams(
            collective_id=collective_id, has_side_effects=True, vmem_limit_bytes=48 << 20
        ),
        name="forward_attention",
    )(*weights, slots, mixed, logs, masks, seen)
    return [v.reshape(-1, v.shape[2]) for v in out[:count]], out[count:]


def attend_back_pair(
    pair,
    blocks,
    head_size,
    slots_ref,
    x_ref,
    do_ref,
    c_ref,
    mask_ref,
    lse_ref,
    dx_ref,
    query_decay_ref,
    key_decay_ref,
):
    scale = head_size**-0.5

    def head(h, carry):
        lanes = lax.broadcasted_iota(jnp.int32, (1, 2 * head_size), 1)
        mine = lanes // head_size == h
        index = 2 * pair + h
        mine_decay = lax.broadcasted_iota(jnp.int32, (1, c_ref.shape[2]), 1) == index
        decays = [column(c_ref[b], index) for b in range(blocks)]
        query_grads = [None] * blocks
        key_grads, value_grads = [None] * blocks, [None] * blocks
        decay_grads = [None] * blocks

        def add(store, at, value):
            store[at] = value if store[at] is None else store[at] + value

        for block in range(blocks):
            query = jnp.where(mine, x_ref[slots_ref[block], 0] * scale, 0).astype(BF16)
            grad_o = jnp.where(mine, do_ref[slots_ref[block]], 0).astype(BF16)
            lse = lse_ref[pair, h, pl.ds(block, 1), :]
            weights, grads, delta = [], [], 0.0
            for other, mask in seen_blocks(block):
                s = dot_lanes(x_ref[slots_ref[other], 1], query) - decays[other]
                if mask is not None:
                    s = s + mask_ref[mask]
                weight = jnp.exp(s - lse)
                grad = dot_lanes(x_ref[slots_ref[other], 2], grad_o)
                delta = delta + jnp.sum(weight * grad, axis=0, keepdims=True)
                weights.append(weight)
                grads.append(grad)
            query_grad, query_decay = 0.0, 0.0
            for weight, grad, (other, _) in zip(weights, grads, seen_blocks(block)):
                ds = weight * (grad - delta)
                query_decay = query_decay + jnp.sum(ds, axis=0, keepdims=True)
                add(decay_grads, other, jnp.sum(ds, axis=1, keepdims=True))
                low = ds.astype(BF16)
                query_grad = query_grad + dot_rows(x_ref[slots_ref[other], 1], low)
                add(key_grads, other, jnp.dot(low, query, preferred_element_type=F32))
                add(
                    value_grads,
                    other,
                    jnp.dot(weight.astype(BF16), grad_o, preferred_element_type=F32),
                )
            query_grads[block] = (query_grad * scale).T
            turned = jnp.broadcast_to(query_decay, (c_ref.shape[2], query_decay.shape[1])).T
            query_decay_ref[block] = jnp.where(mine_decay, turned, query_decay_ref[block])
        for block in range(blocks):
            key_decay_ref[block] = jnp.where(
                mine_decay, decay_grads[block], key_decay_ref[block]
            )
        for part, by_block in enumerate((query_grads, key_grads, value_grads)):
            low = [v.astype(BF16) for v in by_block]
            for place in range(blocks):
                dx_ref[place, part] = jnp.where(
                    mine, pick(slots_ref, place, low), dx_ref[place, part]
                )
        return carry

    lax.fori_loop(0, 2, head, 0)


def split3(values):
    high = values.astype(BF16)
    rest = values - high.astype(F32)
    middle = rest.astype(BF16)
    return high, middle, (rest - middle.astype(F32)).astype(BF16)


def sum_decay_back(blocks, slots_ref, seen_ref, query_decay_ref, key_decay_ref, logs_ref):
    after = 0.0
    for block in range(2, blocks):
        after = after + jnp.sum(query_decay_ref[block], axis=0, keepdims=True)
    by_block = [None] * blocks
    for block in reversed(range(blocks)):
        grad = query_decay_ref[block] - key_decay_ref[block]
        seen = seen_ref[max(block - 1, 0)]
        value = sum(dot_rows(seen, part) for part in split3(grad))
        by_block[block] = value if block >= 2 else value + after
        if block == 1:
            after = after + jnp.sum(grad, axis=0, keepdims=True)
    for place in range(blocks):
        logs_ref[place] = pick(slots_ref, place, by_block)


def halving_orders(n_fsdp):
    bits = [1 << i for i in range(n_fsdp.bit_length() - 2)]
    return bits[::-1], bits


def kept_pieces(order):
    keep = [0]
    for bit in reversed(order[1:]):
        keep = keep + [k ^ bit for k in keep]
    return keep


class Scatter:
    def __init__(
        self, parts, groups, received, ahead, send_sem, recv_sem, line_sem, local_sem, n_fsdp, n_grp
    ):
        self.parts, self.groups, self.n_grp = parts, groups, n_grp
        self.received, self.ahead = received, ahead
        self.saved = []
        self.send_sem, self.recv_sem = send_sem, recv_sem
        self.line_sem, self.local_sem = line_sem, local_sem
        self.f, self.z = lax.axis_index("fsdp"), lax.axis_index("grp")
        orders = halving_orders(n_fsdp)
        self.orders = [orders[i % 2] for i in range(len(parts))]
        self.keeps = [kept_pieces(o) for o in self.orders]
        self.up = {"fsdp": self.f, "grp": self.z + 1}
        self.down = {"fsdp": self.f, "grp": self.z - 1}
        self.across = {b: {"fsdp": flip(self.f, 2 * b), "grp": self.z} for b in orders[1]}
        self.sent, self.count = [], [0] * len(parts)

    def stage_of(self, part, k):
        order = self.orders[part]
        return next((i for i, b in enumerate(order) if k & b), len(order))

    def slot(self, part, k, stage):
        slots = [(v, j) for v in self.keeps[part] for j in range(self.stage_of(part, v))]
        return slots.index((k, stage))

    def _send(self, part, source, target, recv_sem, to):
        index = self.count[part]
        self.count[part] += 1

        def copy():
            return pltpu.make_async_remote_copy(
                src_ref=source(),
                dst_ref=target(),
                send_sem=self.send_sem.at[part, index],
                recv_sem=recv_sem(),
                device_id=to,
                device_id_type=MESH,
            )

        copy().start()
        return copy

    def _cross(self, part, place, k, stage, source):
        bit = self.orders[part][stage]
        slot = self.slot(part, k ^ bit, stage)
        copy = self._send(
            part,
            lambda: source,
            lambda: self.parts[part][3].at[slot, place],
            lambda: self.recv_sem.at[part, slot, place],
            self.across[bit],
        )
        self.sent.append((None, [copy]))

    def _arrived(self, target, recv_sem):
        pltpu.make_async_remote_copy(
            src_ref=target,
            dst_ref=target,
            send_sem=self.send_sem.at[0, 0],
            recv_sem=recv_sem,
            device_id=self.across[1],
            device_id_type=MESH,
        ).wait_recv()

    def _load(self, part, place, i):
        kept, held = self.parts[part][1:3]
        return pltpu.make_async_copy(
            kept.at[i, place], held.at[i, place], self.local_sem.at[part, i, place]
        )

    def _fill(self, part, place, i):
        away, arrived = self.parts[part][0], self.parts[part][3]
        slot = self.slot(part, self.keeps[part][i], 0)
        return pltpu.make_async_copy(
            away.at[i, place], arrived.at[slot, place], self.recv_sem.at[part, slot, place]
        )

    def _begin(self, part, place):
        away = self.parts[part][0]
        for i, k in reversed(list(enumerate(self.keeps[part]))):
            if part in self.received:
                self._fill(part, place, i).start()
            else:
                self._cross(part, place, k ^ self.orders[part][0], 0, away.at[i, place])
            if self.parts[part][1] is not None:
                self._load(part, place, i).start()

    def _add_arrived(self, part, place, k):
        held, arrived = self.parts[part][2], self.parts[part][3]
        i = self.keeps[part].index(k)
        if self.parts[part][1] is not None:
            self._load(part, place, i).wait()
        for stage in range(self.stage_of(part, k)):
            slot = self.slot(part, k, stage)
            if stage == 0 and part in self.received:
                self._fill(part, place, i).wait()
            else:
                self._arrived(arrived.at[slot, place], self.recv_sem.at[part, slot, place])
        total = held[i, place]
        for stage in range(self.stage_of(part, k)):
            total = total + arrived[self.slot(part, k, stage), place]
        held[i, place] = total
        return held.at[i, place]

    def _save(self, part, place):
        source = self._add_arrived(part, place, 0)
        if self.parts[part][4] is None:
            copy = pltpu.make_async_copy(
                source, self.parts[part][6].at[place], self.local_sem.at[part, 0, place]
            )
            copy.start()
            self.saved.append(copy)

    def _halve(self, part, place, k):
        source = self._add_arrived(part, place, k)
        self._cross(part, place, k, self.stage_of(part, k), source)

    def _when(self, condition, action):
        copies = []
        pl.when(condition)(lambda: copies.extend(action()))
        self.sent.append((condition, copies))

    def _line(self, part, place, hop):
        last = self.n_grp - 1
        held = self.parts[part][2]
        ways = []
        if hop < place:
            ways.append((self.z == hop, 4, 0, self.up))
        if last - hop > place:
            ways.append((self.z == last - hop, 5, 1, self.down))
        for condition, which, way, to in ways:
            passing = self.parts[part][which]

            def action(passing=passing, way=way, to=to):
                target = lambda: passing.at[place]
                sem = lambda: self.line_sem.at[part, way, place]
                if hop == 0:
                    return [self._send(part, lambda: held.at[0, place], target, sem, to)]
                self._arrived(target(), sem())
                passing[place] = passing[place] + held[0, place]
                return [self._send(part, target, target, sem, to)]

            self._when(condition, action)

    def _result(self, part):
        held, below, above, result, columns = (self.parts[part][i] for i in (2, 4, 5, 6, 7))
        z, last = self.z, self.n_grp - 1
        result[:, columns] = held[0, z].astype(F32)

        def add(passing, index):
            self._arrived(passing.at[z], self.line_sem.at[part, index, z])
            result[:, columns] = result[:, columns] + passing[z].astype(F32)

        pl.when(z > 0)(lambda: add(below, 0))
        pl.when(z < last)(lambda: add(above, 1))

    def waves(self):
        bind = functools.partial
        low, high, places = 0, self.n_grp - 1, []
        while low <= high:
            places += [high] if low == high else [high, low]
            low, high = low + 1, high - 1
        units = []
        for i, count in enumerate(self.groups):
            first = sum(self.groups[:i])
            group = range(first, first + count)
            units += [(part, place) for place in places for part in group]
        ahead, stages = self.ahead, len(self.orders[0])
        length = len(units) + ahead + 2 * stages + 4 * self.n_grp
        waves = [[] for _ in range(length)]
        final = {}
        for n, (part, place) in enumerate(units):
            waves[max(0, n + 1 - ahead)].append(bind(self._begin, part, place))
            at = n + 1
            for stage in range(1, stages):
                for k in self.keeps[part]:
                    if self.stage_of(part, k) == stage:
                        waves[at].append(bind(self._halve, part, place, k))
                at += 2
            waves[at].append(bind(self._save, part, place))
            if self.parts[part][4] is None:
                continue
            for hop in range(self.n_grp - 1):
                waves[at + 2 * hop].append(bind(self._line, part, place, hop))
            final[part] = at + 2 * (self.n_grp - 1)
        for part, at in final.items():
            waves[at].append(bind(self._result, part))
        return waves

    def finish(self):
        for copy in self.saved:
            copy.wait()
        for condition, copies in self.sent:
            if condition is None:
                for copy in copies:
                    copy().wait_send()
            else:

                def wait_sent():
                    for copy in copies:
                        copy().wait_send()

                pl.when(condition)(wait_sent)


def scatter_buffers(kind, rows, width, n_fsdp, n_grp):
    m = n_fsdp.bit_length() - 2
    keep = n_fsdp // 4
    slots = m + sum(i << (m - 1 - i) for i in range(1, m))
    leading = {
        "full": [(keep, n_grp), (slots, n_grp), (n_grp,), (n_grp,)],
        "cross": [(keep, n_grp), (slots, n_grp)],
    }[kind]
    return [pltpu.VMEM(v + (rows, width), BF16) for v in leading]


def scatter_scratch(kinds, sizes, n_fsdp, n_grp, parts=None):
    m = n_fsdp.bit_length() - 2
    keep = n_fsdp // 4
    slots = m + sum(i << (m - 1 - i) for i in range(1, m))
    parts = parts or len(kinds)
    shapes = [
        pltpu.SemaphoreType.DMA((parts, n_grp * (2 * keep + 2 * n_grp))),
        pltpu.SemaphoreType.DMA((parts, slots, n_grp)),
        pltpu.SemaphoreType.DMA((parts, 2, n_grp)),
        pltpu.SemaphoreType.DMA((parts, keep, n_grp)),
    ]
    for kind, (rows, width) in zip(kinds, sizes):
        shapes += scatter_buffers(kind, rows, width, n_fsdp, n_grp)
    return shapes


def scatter_parts(kinds, aways, kepts, buffers, results):
    parts, buffers = [], list(buffers)
    for kind, away, kept, result in zip(kinds, aways, kepts, results):
        count = {"full": 4, "cross": 2}[kind]
        mine, buffers = buffers[:count], buffers[count:]
        if kind == "cross":
            mine = mine + [None, None]
        parts.append((away, kept, *mine, *result))
    return parts, buffers


def column_ranges(widths):
    start, ranges = 0, []
    for width in widths:
        ranges.append(pl.ds(start, width))
        start += width
    return ranges


def last_kernel(widths, lines, n_fsdp, n_grp, *refs):
    mixed_ref, narrow_ref, l_ref, l_other_ref, w_hbm, forget_ref = refs[:6]
    tokens_ref, scale_ref, gain_ref, resid_ref, small_ref = refs[6:11]
    count, more = len(widths), sum(len(w) for w in lines)
    lined, refs = refs[11 : 11 + more], refs[11 + more :]
    wide_ref, narrow_result, grad_ref, dgain_refs = refs[0], refs[1], refs[2], refs[3:6]
    results, refs = refs[6 : 6 + len(lines)], refs[6 + len(lines) :]
    sems, refs = refs[:4], refs[4:]
    ranges = column_ranges(widths)
    gathered_refs, aways, refs = refs[:more], refs[more : more + count], refs[more + count :]
    places = [(wide_ref, c) for c in ranges[:-1]] + [(narrow_result, pl.ds(0, widths[-1]))]
    parts, refs = scatter_parts(["full"] * count, aways, [None] * count, refs, places)
    mixed_other, narrow_other, rows_ref, w_ref, act_ref, incoming, send_sem, recv_sem, w_sem, own_sem, group_send, group_recv, total_ref = refs
    f, z = lax.axis_index("fsdp"), lax.axis_index("grp")
    tok, width = act_ref.shape
    pieces = n_fsdp // 2

    meet(n_fsdp, n_grp, False)

    def exchange(source, target, index, peer):
        return pltpu.make_async_remote_copy(
            src_ref=source,
            dst_ref=target,
            send_sem=send_sem.at[index],
            recv_sem=recv_sem.at[index],
            device_id=peer,
            device_id_type=MESH,
        )

    sibling = {"fsdp": flip(f, 1), "grp": z}
    others = []
    for i in range(count):
        if i < count - 1:
            pair = (mixed_ref.at[:, ranges[i]], mixed_other.at[:, ranges[i]])
        else:
            pair = (narrow_ref, narrow_other)
        others.append(exchange(*pair, i, sibling))
        others[-1].start()

    chunk = w_ref.shape[2]
    chunks = w_hbm.shape[1] // chunk

    def fetch(i):
        return pltpu.make_async_copy(
            w_hbm.at[:, pl.ds(i * chunk, chunk)], w_ref.at[i % 2], w_sem.at[i % 2]
        )

    fetch(0).start()
    for k in range(pieces):
        row = flip(f // 2, k) * 2 + f % 2
        rows_ref[k, :, :tok] = l_ref[row]
        rows_ref[k, :, tok:] = l_other_ref[row]

    scatter = Scatter(parts, [count], (), AHEAD, *sems, n_fsdp, n_grp)
    waves = iter(scatter.waves())

    def advance(steps=None):
        for wave in itertools.islice(waves, steps):
            for step in wave:
                step()

    direct = GroupExchange(n_grp, group_send, group_recv)
    own = []
    for i, (source, target) in enumerate(zip(lined, gathered_refs)):
        direct.send(
            i, i, lambda place, source=source: source.at[place],
            lambda place, target=target: target.at[place],
        )
        own.append(pltpu.make_async_copy(source.at[z], target.at[z], own_sem.at[i]))
        own[-1].start()

    def products(part, ks, target):
        if part < count - 1:
            right = (mixed_ref[:, ranges[part]], mixed_other[:, ranges[part]])
        else:
            right = (narrow_ref[...], narrow_other[...])
        right = jnp.concatenate(right, axis=0)
        left = jnp.concatenate([rows_ref[k] for k in ks], axis=0)
        value = jnp.dot(left, right, preferred_element_type=F32).astype(BF16)
        target[...] = value.reshape(target.shape)

    for part in range(count):
        others[part].wait_recv()
        first = scatter.orders[part][0]
        products(part, [k ^ first for k in scatter.keeps[part]], aways[part])
    advance(1)
    for part in range(count):
        products(part, scatter.keeps[part], parts[part][2])
    act_ref[...] = dot_lanes(narrow_ref[...], forget_ref[...])
    for i in range(chunks):
        if i + 1 < chunks:
            fetch(i + 1).start()
        fetch(i).wait()
        act_ref[...] += dot_lanes(mixed_ref[:, pl.ds(i * chunk, chunk)], w_ref[i % 2])
        advance(1)

    block = next(t for t in (64, 32, 16, 8) if tok % t == 0)
    total_ref[0] = small_ref[...]

    def finish_rows(i, carry):
        rows = pl.ds(pl.multiple_of(i * block, block), block)
        scale = scale_ref[rows, :]
        normed = tokens_ref[rows, :].astype(F32) * scale
        act = act_ref[rows, :]
        total_ref[0, :, :width] += jnp.sum(act * normed, axis=0, keepdims=True)
        scaled = act * gain_ref[...]
        average = jnp.mean(scaled * normed, axis=1, keepdims=True)
        grad_ref[rows, :] = (
            resid_ref[rows, :] + scale * (scaled - normed * average)
        ).astype(BF16)
        return carry

    lax.fori_loop(0, tok // block, finish_rows, 0)
    peers = [{"fsdp": f, "grp": flip(z, 1 << i)} for i in range(n_grp.bit_length() - 1)]
    peers += [{"fsdp": flip(f, 1 << i), "grp": z} for i in range(n_fsdp.bit_length() - 1)]
    sent = []
    for i, peer in enumerate(peers):
        copy = exchange(total_ref.at[i], incoming.at[i], count + i, peer)
        copy.start()
        sent.append(copy)
        advance(1)
        copy.wait_recv()
        total_ref[i + 1] = total_ref[i] + incoming[i]
    total = total_ref[len(peers)]
    for ref, start in zip(dgain_refs, (0, width, 2 * width)):
        ref[...] = total[:, start : start + ref.shape[1]]
    advance()
    i = 0
    for ref, line in zip(results, lines):
        for columns in column_ranges(line):
            own[i].wait()
            direct.wait(i)
            value = gathered_refs[i][0].astype(F32)
            for place in range(1, n_grp):
                value = value + gathered_refs[i][place].astype(F32)
            ref[:, columns] = value
            i += 1
    scatter.finish()
    direct.finish()
    for copy in others + sent:
        copy.wait_send()


def last_gradients(
    acts, mixed, narrow, w_qkv, forget, tokens, scale, gain, resid, small, lines, collective_id
):
    n_fsdp, n_grp = lax.axis_size("fsdp"), lax.axis_size("grp")
    tok, wide = mixed.shape
    width = tokens.shape[1]
    own_rows = width // (n_fsdp * n_grp)
    split = 4 if wide % 512 == 0 else 2
    more = sum(len(w) for w in lines)
    widths = [wide // split] * split + [narrow.shape[1]]
    keep = n_fsdp // 4
    rounds = n_fsdp.bit_length() + n_grp.bit_length() - 2
    aways = [jax.ShapeDtypeStruct((keep, n_grp, own_rows, w), BF16) for w in widths]
    chunk = next(t for t in (512, 384, 256, 128) if wide % t == 0)
    vmem = pl.BlockSpec(memory_space=pltpu.VMEM)
    anywhere = pl.BlockSpec(memory_space=pl.ANY)
    return pl.pallas_call(
        functools.partial(
            last_kernel, widths, [[v.shape[2] for v in w] for w in lines], n_fsdp, n_grp
        ),
        out_shape=[
            jax.ShapeDtypeStruct((own_rows, wide), F32),
            jax.ShapeDtypeStruct((own_rows, widths[-1]), F32),
            jax.ShapeDtypeStruct(tokens.shape, BF16),
            jax.ShapeDtypeStruct((1, width), F32),
            jax.ShapeDtypeStruct((1, width), F32),
            jax.ShapeDtypeStruct((1, widths[-1]), F32),
        ]
        + [
            jax.ShapeDtypeStruct((w[0].shape[1], sum(v.shape[2] for v in w)), F32) for w in lines
        ],
        in_specs=[vmem] * 4
        + [anywhere]
        + [vmem] * 6
        + [anywhere] * sum(len(w) for w in lines),
        out_specs=[vmem] * (6 + len(lines)),
        scratch_shapes=scatter_scratch([], [], n_fsdp, n_grp, len(widths))
        + [pltpu.VMEM(v.shape, BF16) for w in lines for v in w]
        + [pltpu.VMEM(a.shape, BF16) for a in aways]
        + [v for a in aways for v in scatter_buffers("full", *a.shape[2:], n_fsdp, n_grp)]
        + [
            pltpu.VMEM(mixed.shape, BF16),
            pltpu.VMEM(narrow.shape, BF16),
            pltpu.VMEM((n_fsdp // 2, n_grp * own_rows, 2 * tok), BF16),
            pltpu.VMEM((2, width, chunk), BF16),
            pltpu.VMEM((tok, width), F32),
            pltpu.VMEM((rounds, 1, small.shape[1]), F32),
            pltpu.SemaphoreType.DMA((len(widths) + rounds,)),
            pltpu.SemaphoreType.DMA((len(widths) + rounds,)),
            pltpu.SemaphoreType.DMA((2,)),
            pltpu.SemaphoreType.DMA((max(1, more),)),
            pltpu.SemaphoreType.DMA((max(1, more), n_grp)),
            pltpu.SemaphoreType.DMA((max(1, more), n_grp)),
            pltpu.VMEM((rounds + 1, 1, small.shape[1]), F32),
        ],
        compiler_params=pltpu.CompilerParams(
            collective_id=collective_id, has_side_effects=True, vmem_limit_bytes=58 << 20
        ),
        name="last_gradients",
    )(
        mixed, narrow, acts[0], acts[1], w_qkv, forget, tokens, scale, gain, resid, small,
        *(v for w in lines for v in w),
    )


def backward_kernel(kinds, widths, received, pairs, head_size, n_fsdp, n_grp, *refs):
    count = sum(len(w) for w in widths)
    aways, kepts, refs = refs[:count], refs[count : 2 * count], refs[2 * count :]
    slots_ref, grad_ref, x_hbm, c_ref, mask_ref, seen_ref, lse_ref = refs[:7]
    refs = refs[7:]
    results, part_kinds = [], []
    for kind, w in zip(kinds, widths):
        if kind == "full":
            results += [(refs[0], columns) for columns in column_ranges(w)]
            refs = refs[1:]
        else:
            results += [(ref, None) for ref in refs[: len(w)]]
            refs = refs[len(w) :]
        part_kinds += [kind] * len(w)
    mixed_out, logs_out = refs[:2]
    sems = refs[2:6]
    parts, refs = scatter_parts(part_kinds, aways, kepts, refs[6:], results)
    x_refs, refs = refs[:pairs], refs[pairs:]
    do_refs, refs = refs[:pairs], refs[pairs:]
    dx_refs, refs = refs[:pairs], refs[pairs:]
    query_decay_ref, key_decay_ref, logs_ref, send_sem, recv_sem, copy_sem = refs
    blocks = n_grp
    pair_width = 2 * head_size
    group_width = pairs * pair_width
    width = blocks * group_width
    z = lax.axis_index("grp")

    meet(n_fsdp, n_grp, False)
    scatter = Scatter(parts, [len(w) for w in widths], received, AHEAD, *sems, n_fsdp, n_grp)
    swap_heads = GroupExchange(n_grp, send_sem, recv_sem)
    started = itertools.count()

    def keep(source, target):
        copy = pltpu.make_async_copy(source, target, copy_sem.at[next(started)])
        copy.start()
        return copy

    def heads_of(ref, part, place, pair):
        start = part * width + place * group_width + pair * pair_width
        return ref.at[:, pl.ds(pl.multiple_of(start, 128), pair_width)]

    own, late = [], []
    for pair in range(pairs):
        swap_heads.send(
            (pair, "do"),
            4 * pair,
            lambda place, pair=pair: heads_of(grad_ref, 0, place, pair),
            lambda place, pair=pair: do_refs[pair].at[place],
        )
        own.append(keep(heads_of(grad_ref, 0, z, pair), do_refs[pair].at[z]))
        own.append(keep(x_hbm.at[pair], x_refs[pair]))
    waves = iter(scatter.waves())

    def advance(count=None):
        for wave in itertools.islice(waves, count):
            for step in wave:
                step()

    advance(1)
    for pair in range(pairs):
        own[2 * pair].wait()
        own[2 * pair + 1].wait()
        swap_heads.wait((pair, "do"))
        attend_back_pair(
            pair,
            blocks,
            head_size,
            slots_ref,
            x_refs[pair],
            do_refs[pair],
            c_ref,
            mask_ref,
            lse_ref,
            dx_refs[pair],
            query_decay_ref,
            key_decay_ref,
        )
        for part in range(3):
            swap_heads.send(
                (pair, part),
                1 + 4 * pair + part,
                lambda place, pair=pair, part=part: dx_refs[pair].at[place, part],
                lambda place, pair=pair, part=part: heads_of(mixed_out, part, place, pair),
            )
            late.append(keep(dx_refs[pair].at[z, part], heads_of(mixed_out, part, z, pair)))
        advance(3)
    sum_decay_back(blocks, slots_ref, seen_ref, query_decay_ref, key_decay_ref, logs_ref)
    swap_heads.send(
        "logs",
        4 * pairs,
        lambda place: logs_ref.at[place],
        lambda place: logs_out.at[place],
    )
    late.append(keep(logs_ref.at[z], logs_out.at[z]))
    advance()
    for pair in range(pairs):
        for part in range(3):
            swap_heads.wait((pair, part))
    swap_heads.wait("logs")
    scatter.finish()
    swap_heads.finish()
    for copy in late:
        copy.wait()


def backward_attention(
    kinds, weights, received, slots, grad, x, decay, masks, seen, lse, head_size, collective_id
):
    n_fsdp, n_grp = lax.axis_size("fsdp"), lax.axis_size("grp")
    aways = [away for parts in weights for away, _ in parts]
    kepts = [kept for parts in weights for _, kept in parts]
    widths = [[away.shape[3] for away, _ in parts] for parts in weights]
    pairs, _, _, tok, pair_width = x.shape
    lanes = decay.shape[2]
    anywhere = pl.BlockSpec(memory_space=pl.ANY)
    vmem = pl.BlockSpec(memory_space=pltpu.VMEM)
    shapes, specs = [], []
    for kind, parts, w in zip(kinds, weights, widths):
        own_rows = parts[0][0].shape[2]
        if kind == "full":
            shapes.append(jax.ShapeDtypeStruct((own_rows, sum(w)), F32))
            specs.append(vmem)
        else:
            shapes += [jax.ShapeDtypeStruct((n_grp, own_rows, v), BF16) for v in w]
            specs += [anywhere] * len(w)
    part_kinds = [kind for kind, w in zip(kinds, widths) for _ in w]
    out = pl.pallas_call(
        functools.partial(
            backward_kernel, kinds, widths, received, pairs, head_size, n_fsdp, n_grp
        ),
        out_shape=shapes
        + [
            jax.ShapeDtypeStruct((tok, 3 * grad.shape[1]), BF16),
            jax.ShapeDtypeStruct((n_grp, tok, lanes), F32),
        ],
        in_specs=[anywhere] * (2 * len(aways))
        + [pl.BlockSpec(memory_space=pltpu.SMEM), anywhere, anywhere]
        + [vmem] * 4,
        out_specs=specs + [anywhere] * 2,
        scratch_shapes=scatter_scratch(
            part_kinds, [v.shape[2:] for v in aways], n_fsdp, n_grp
        )
        + [pltpu.VMEM((n_grp, 3, tok, pair_width), BF16)] * pairs
        + [pltpu.VMEM((n_grp, tok, pair_width), BF16)] * pairs
        + [pltpu.VMEM((n_grp, 3, tok, pair_width), BF16)] * pairs
        + [pltpu.VMEM((n_grp, tok, lanes), F32)] * 3
        + [
            pltpu.SemaphoreType.DMA((1 + 4 * pairs, n_grp)),
            pltpu.SemaphoreType.DMA((1 + 4 * pairs, n_grp)),
            pltpu.SemaphoreType.DMA((1 + 5 * pairs,)),
        ],
        compiler_params=pltpu.CompilerParams(
            collective_id=collective_id, has_side_effects=True, vmem_limit_bytes=62 << 20
        ),
        name="backward_attention",
    )(*aways, *kepts, slots, grad, x, decay, masks, seen, lse)
    return out[:-2], out[-2], out[-1]


def feed_forward_kernel(
    o_ref,
    tokens_ref,
    grad_ref,
    gain_ref,
    w_out_ref,
    gate_ref,
    up_ref,
    down_ref,
    inner_ref,
    dgate_ref,
    dup_ref,
    o_turned_ref,
    act_turned_ref,
    out_ref,
    dresid_ref,
    dbranch_ref,
    do_ref,
    dgain_ref,
    resid_ref,
    act_ref,
    sum_ref,
    dact_ref,
):
    tok = o_ref.shape[0]
    block = next(t for t in (128, 64, 32, 16, 8) if tok % t == 0)

    def rows_of(i):
        return pl.ds(pl.multiple_of(i * block, block), block)

    def norm(rows):
        resid = resid_ref[rows, :]
        scale = lax.rsqrt(jnp.mean(resid * resid, axis=1, keepdims=True) + EPSILON)
        return resid, resid * scale, scale

    @pl.when(pl.program_id(0) == 0)
    def _():
        def begin(i, carry):
            rows = rows_of(i)
            resid_ref[rows, :] = tokens_ref[rows, :].astype(F32) + jnp.dot(
                o_ref[rows, :], w_out_ref[...], preferred_element_type=F32
            )
            _, normed, _ = norm(rows)
            act_ref[rows, :] = (normed * gain_ref[...]).astype(BF16)
            return carry

        lax.fori_loop(0, tok // block, begin, 0)
        sum_ref[...] = jnp.zeros_like(sum_ref)
        dact_ref[...] = jnp.zeros_like(dact_ref)
        o_turned_ref[...] = o_ref[...].T
        act_turned_ref[...] = act_ref[...].T

    act = act_ref[...]
    gate = jnp.dot(act, gate_ref[...], preferred_element_type=F32)
    up = jnp.dot(act, up_ref[...], preferred_element_type=F32)
    grad_inner = dot_lanes(grad_ref[...], down_ref[...])
    sigma = jax.nn.sigmoid(gate)
    swish = gate * sigma
    inner = (swish * up).astype(BF16)
    dgate = (grad_inner * up * (sigma * (1.0 + gate * (1.0 - sigma)))).astype(BF16)
    dup = (grad_inner * swish).astype(BF16)
    inner_ref[...] = inner.T
    dgate_ref[...] = dgate
    dup_ref[...] = dup
    sum_ref[...] += jnp.dot(inner, down_ref[...], preferred_element_type=F32)
    dact_ref[...] += dot_lanes(dgate, gate_ref[...]) + dot_lanes(dup, up_ref[...])

    @pl.when(pl.program_id(0) == pl.num_programs(0) - 1)
    def _():
        dgain_ref[...] = jnp.zeros_like(dgain_ref)

        def end(i, carry):
            rows = rows_of(i)
            resid, normed, scale = norm(rows)
            out_ref[rows, :] = (resid + sum_ref[rows, :]).astype(BF16)
            dact = dact_ref[rows, :]
            dgain_ref[...] += jnp.sum(dact * normed, axis=0, keepdims=True)
            scaled = dact * gain_ref[...]
            average = jnp.mean(scaled * normed, axis=1, keepdims=True)
            dresid = grad_ref[rows, :].astype(F32) + scale * (scaled - normed * average)
            dresid_ref[rows, :] = dresid
            dbranch = dresid.astype(BF16)
            dbranch_ref[rows, :] = dbranch
            do_ref[rows, :] = dot_lanes(dbranch, w_out_ref[...]).astype(BF16)
            return carry

        lax.fori_loop(0, tok // block, end, 0)


def feed_forward(attn_o, tokens, grad, gain, w_out, gate_up, down):
    tok, width = tokens.shape
    hidden = down.shape[0]
    tile = 512
    steps = hidden // tile
    once = lambda rows, columns: pl.BlockSpec(
        (rows, columns), lambda j: (0, 0), pipeline_mode=pl.Buffered(1)
    )
    rows = once(tok, width)
    columns = pl.BlockSpec((tok, tile), lambda j: (0, j))
    low = lambda *shape: jax.ShapeDtypeStruct(shape, BF16)
    return pl.pallas_call(
        feed_forward_kernel,
        out_shape=[
            low(hidden, tok),
            low(tok, hidden),
            low(tok, hidden),
            low(width, tok),
            low(width, tok),
            low(tok, width),
            jax.ShapeDtypeStruct((tok, width), F32),
            low(tok, width),
            low(tok, width),
            jax.ShapeDtypeStruct((1, width), F32),
        ],
        grid=(steps,),
        in_specs=[
            rows,
            rows,
            rows,
            once(1, width),
            once(width, width),
            pl.BlockSpec((width, tile), lambda j: (0, j)),
            pl.BlockSpec((width, tile), lambda j: (0, steps + j)),
            pl.BlockSpec((tile, width), lambda j: (j, 0)),
        ],
        out_specs=[
            pl.BlockSpec((tile, tok), lambda j: (j, 0)),
            columns,
            columns,
            once(width, tok),
            once(width, tok),
            rows,
            rows,
            rows,
            rows,
            once(1, width),
        ],
        scratch_shapes=[
            pltpu.VMEM((tok, width), F32),
            pltpu.VMEM((tok, width), BF16),
            pltpu.VMEM((tok, width), F32),
            pltpu.VMEM((tok, width), F32),
        ],
        compiler_params=pltpu.CompilerParams(vmem_limit_bytes=60 << 20),
        cost_estimate=pl.CostEstimate(
            flops=12 * tok * width * hidden,
            bytes_accessed=6 * width * hidden,
            transcendentals=tok * hidden,
        ),
        name="feed_forward",
    )(attn_o, tokens, grad, gain, w_out, gate_up, gate_up, down)


def weight_grad_kernel(count, ids, *refs):
    own, other, (r_ref, r_other_ref, *outs) = (
        refs[: 2 * count],
        refs[2 * count : 4 * count],
        refs[4 * count :],
    )
    rows = [jnp.concatenate([ref[0] for ref in side], axis=0) for side in (own, other)]
    total = jnp.dot(
        jnp.concatenate(rows, axis=1),
        jnp.concatenate([r_ref[...], r_other_ref[...]], axis=0),
        preferred_element_type=F32,
    )
    total = total.astype(BF16).reshape(2 * count, -1, total.shape[1])
    outs[0][...] = total[:count]
    outs[1][...] = total[count:]


def weight_grad(ids, l_own, l_other, r_own, r_other, start, width):
    count = ids.shape[0] // 2
    _, rows, tok = l_own.shape
    limit = 1024 if rows * count < 1024 else 384
    tile = max(t for t in range(128, limit + 1, 128) if width % t == 0 and start % t == 0)
    steps, first = width // tile, start // tile
    pieces = [
        pl.BlockSpec(
            (1, rows, tok), lambda n, ids, k=k: (ids[k], 0, 0), pipeline_mode=pl.Buffered(1)
        )
        for k in range(2 * count)
    ]
    r_spec = pl.BlockSpec((tok, tile), lambda n, ids: (0, first + n))
    out_spec = pl.BlockSpec((count, rows, tile), lambda n, ids: (0, 0, n))
    return pl.pallas_call(
        functools.partial(weight_grad_kernel, count),
        out_shape=[jax.ShapeDtypeStruct((count, rows, width), BF16)] * 2,
        grid_spec=pltpu.PrefetchScalarGridSpec(
            num_scalar_prefetch=1,
            grid=(steps,),
            in_specs=pieces * 2 + [r_spec, r_spec],
            out_specs=[out_spec, out_spec],
        ),
        compiler_params=pltpu.CompilerParams(vmem_limit_bytes=60 << 20),
        cost_estimate=pl.CostEstimate(
            flops=8 * count * rows * tok * width,
            bytes_accessed=2 * (2 * count * rows * width + 2 * tok * width),
            transcendentals=0,
        ),
        name="weight_grad",
    )(ids, *[l_own] * (2 * count), *[l_other] * (2 * count), r_own, r_other)


def both_cores(turned):
    n_fsdp = lax.axis_size("fsdp")
    turned = turned.reshape(n_fsdp, turned.shape[0] // n_fsdp, turned.shape[1])
    return turned, swap(turned, "fsdp", 1)


def partial_rows(left, columns):
    n_fsdp, n_grp = lax.axis_size("fsdp"), lax.axis_size("grp")
    f = lax.axis_index("fsdp")
    parts = []
    for part, (right, right_other, start, width) in enumerate(columns):
        order = halving_orders(n_fsdp)[part % 2]
        keep = kept_pieces(order)
        ids = jnp.stack([flip(f // 2, k) for k in [k ^ order[0] for k in keep] + keep])
        pair = weight_grad(
            2 * ids + f % 2, left[0], left[1], right, right_other, start, width
        )
        parts.append(
            tuple(v.reshape(v.shape[0], n_grp, v.shape[1] // n_grp, width) for v in pair)
        )
    return parts


def norm_rows(features):
    row_scale = lax.rsqrt(jnp.mean(features * features, axis=-1, keepdims=True) + EPSILON)
    return (features * row_scale, row_scale)


def norm_back(grad_normed, normed, row_scale):
    average_addend = jnp.mean(grad_normed * normed, axis=-1, keepdims=True)
    return row_scale * (grad_normed - normed * average_addend)


def contract_cols(first_op, second_op):
    return lax.dot_general(
        first_op, second_op, (((1,), (1,)), ((), ())), preferred_element_type=F32
    )


def on_device(
    tokens,
    block_order,
    cont_lengths,
    gain_attn,
    w_qkv,
    w_forget,
    b_forget,
    w_out,
    gain_ffn,
    w_gate_up,
    w_down,
    grad_out,
):
    tok, width = tokens.shape
    heads = w_forget.shape[1]
    head_size = width // heads
    blocks = lax.axis_size("grp")
    own_heads = heads // blocks
    pairs = own_heads // 2
    group_width = width // blocks
    slots = block_order[0]

    positions = jnp.arange(tok, dtype=jnp.int32)
    causal = positions[None, :] <= positions[:, None]
    seg_ends = jnp.cumsum(cont_lengths[0], axis=1)
    segment = jnp.sum((positions[None, :, None] >= seg_ends[:, None, :]).astype(jnp.int32), axis=2)
    within = jnp.logical_and(segment[:, :, None] == segment[:, None, :], causal[None])
    seen = jnp.concatenate([causal[None], within], axis=0)
    masks = jnp.where(seen.transpose(0, 2, 1), 0.0, NEG).astype(F32)
    seen_low = seen.astype(BF16)

    forget_pad = 128 - heads
    qkv_full, forget_full, out_line, down_line = gather_rows(
        ("full", "full", "line", "line"),
        [w_qkv, jnp.pad(w_forget, ((0, 0), (0, forget_pad))), w_out, w_down],
        1,
    )
    qkv_full, forget_full = (v.reshape(-1, v.shape[2]) for v in (qkv_full, forget_full))
    inputs = tokens.astype(F32)
    normed_one, scale_one = norm_rows(inputs)
    acts = (normed_one * gain_attn).astype(BF16)
    grad_out_other = swap(grad_out, "fsdp", 1)
    acts_rows = both_cores(acts.T)
    logits = jnp.dot(acts, forget_full, preferred_element_type=F32)[:, :heads] + b_forget
    log_keep = jax.nn.log_sigmoid(logits)
    mixed = jnp.dot(acts, qkv_full, preferred_element_type=F32).astype(BF16)

    logs = jnp.pad(
        log_keep.T.reshape(blocks, own_heads, tok), ((0, 0), (0, 8 - own_heads), (0, 0))
    )
    (out_full, gate_up_full, down_full), (attn_o, x, lse, decay) = forward_attention(
        ("lined", "full", "lined"), [out_line, w_gate_up, down_line], slots, mixed, logs, masks, seen_low, head_size, 2
    )

    half, hidden = width // 2, down_full.shape[0]
    (
        inner_turned,
        grad_gate,
        grad_up,
        attn_turned,
        acts_two_turned,
        output,
        grad_resid,
        grad_branch,
        grad_heads,
        gain_two_grad,
    ) = feed_forward(attn_o, tokens, grad_out, gain_ffn[None], out_full, gate_up_full, down_full)
    down_rows = both_cores(inner_turned)
    acts_two_rows = both_cores(acts_two_turned)
    attn_rows = both_cores(attn_turned)
    grad_branch_other = swap(grad_branch, "fsdp", 1)
    part_down = partial_rows(
        down_rows, [(grad_out, grad_out_other, 0, half), (grad_out, grad_out_other, half, half)]
    )
    orders = halving_orders(lax.axis_size("fsdp"))
    part_down, grad_gate, grad_up, grad_branch = lax.optimization_barrier(
        (part_down, grad_gate, grad_up, grad_branch)
    )
    part_down = [
        (swap(away, "fsdp", 2 * order[0]), kept)
        for (away, kept), order in zip(part_down, orders)
    ]
    part_gate_up = partial_rows(
        acts_two_rows,
        [(v, swap(v, "fsdp", 1), 0, hidden) for v in (grad_gate, grad_up)],
    )
    part_out = partial_rows(
        attn_rows,
        [
            (grad_branch, grad_branch_other, 0, half),
            (grad_branch, grad_branch_other, half, half),
        ],
    )

    sums, grad_mixed, log_grad = backward_attention(
        ("cross", "full", "cross"),
        [part_down, part_gate_up, part_out],
        range(len(part_down)),
        slots,
        grad_heads,
        x,
        decay,
        masks,
        seen_low,
        lse,
        head_size,
        3,
    )
    log_grad = log_grad[:, :, :own_heads].transpose(1, 0, 2).reshape(tok, heads)
    grad_logits = (log_grad * jax.nn.sigmoid(-logits)).astype(BF16)
    narrow = jnp.pad(grad_logits, ((0, 0), (0, forget_pad)))
    bias_grad = jnp.sum(narrow.astype(F32), axis=0)
    (
        grad_qkv,
        grad_forget,
        grad_tokens,
        grad_gain,
        grad_gain_two,
        grad_bias,
        grad_down,
        grad_out_w,
    ) = last_gradients(
        acts_rows,
        grad_mixed,
        narrow,
        qkv_full,
        forget_full,
        tokens,
        scale_one,
        gain_attn[None],
        grad_resid,
        jnp.concatenate([jnp.zeros((width,), F32), gain_two_grad[0], bias_grad])[None],
        [sums[:2], sums[3:]],
        4,
    )
    return (
        output,
        grad_tokens,
        grad_gain[0],
        grad_qkv,
        grad_forget[:, :heads],
        grad_bias[0, :heads],
        grad_out_w,
        grad_gain_two[0],
        sums[2],
        grad_down,
    )


def solution(mesh):
    both = P(("fsdp", "grp"), None)
    in_specs = (
        both,
        P("fsdp", None),
        P("fsdp", None, None),
        P(),
        both,
        both,
        P(),
        both,
        P(),
        both,
        both,
        both,
    )
    out_specs = (both, both, P(), both, both, P(), both, P(), both, both)
    return jax.shard_map(
        on_device, mesh=mesh, in_specs=in_specs, out_specs=out_specs, check_vma=False
    )
```

```python
import functools
import itertools

import jax
import jax.numpy as jnp
from jax import lax
from jax.experimental import pallas as pl
from jax.experimental.pallas import tpu as pltpu
from jax.sharding import PartitionSpec as P

EPSILON = 1e-05
NEG = -1e30
AHEAD = 6
MESH = pl.DeviceIdType.MESH
F32 = jnp.float32
BF16 = jnp.bfloat16


def flip_bit(value, bit):
    return value + bit - 2 * bit * ((value // bit) % 2)


def flip(value, mask):
    bit = 1
    while bit <= mask:
        if mask & bit:
            value = flip_bit(value, bit)
        bit *= 2
    return value


def swap(value, axis, mask):
    return lax.ppermute(value, axis, [(i, i ^ mask) for i in range(lax.axis_size(axis))])


def gather_parts(shapes):
    return [(w, h) for w, s in enumerate(shapes) for h in (0, 1) if h == 0 or s[1] % 256 == 0]


class Gather:
    def __init__(self, kinds, ins, outs, send_sem, recv_sem, local_sem, n_fsdp, n_grp):
        self.kinds, self.ins, self.outs = kinds, ins, outs
        self.send_sem, self.recv_sem = send_sem, recv_sem
        self.f, self.z, self.n_grp = lax.axis_index("fsdp"), lax.axis_index("grp"), n_grp
        self.bits = [1 << i for i in range(1, n_fsdp.bit_length() - 1)]
        self.parts = gather_parts([r.shape[-2:] for r in ins])
        self.orders = [self.bits if h == 0 else self.bits[::-1] for _, h in self.parts]
        self.across = {b: {"fsdp": flip(self.f, b), "grp": self.z} for b in self.bits + [1]}
        self.up = {"fsdp": self.f, "grp": self.z + 1}
        self.down = {"fsdp": self.f, "grp": self.z - 1}
        self.count, self.sent, self.local = 0, [], []
        for w in range(len(ins)):
            target = {
                "full": self.f * n_grp + self.z,
                "line": self.z,
                "lined": pl.ds(self.f * n_grp, n_grp),
            }[kinds[w]]
            self.local.append(
                pltpu.make_async_copy(ins[w], outs[w].at[target], local_sem.at[w])
            )
        self.steps, self.done = self._steps(), 0

    def _columns(self, part):
        w, h = self.parts[part]
        width = self.ins[w].shape[-1]
        return pl.ds(0, width) if width % 256 else pl.ds(h * (width // 2), width // 2)

    def kind(self, part):
        return self.kinds[self.parts[part][0]]

    def _piece(self, part, fk, place):
        row = place if self.kind(part) == "line" else flip(self.f, fk) * self.n_grp + place
        return self.outs[self.parts[part][0]].at[row, :, self._columns(part)]

    def _send(self, part, fk, place, to, to_fk, own=False):
        index = self.count
        self.count += 1

        def copy():
            source = self._piece(part, fk, place)
            if own:
                source = self.ins[self.parts[part][0]]
                source = source.at[place] if self.kind(part) == "lined" else source
                source = source.at[:, self._columns(part)]
            return pltpu.make_async_remote_copy(
                src_ref=source,
                dst_ref=self._piece(part, fk, place),
                send_sem=self.send_sem.at[index],
                recv_sem=self.recv_sem.at[part, to_fk, place],
                device_id=to,
                device_id_type=MESH,
            )

        copy().start()
        return copy

    def _wait(self, part, fk, place):
        piece = self._piece(part, fk, place)
        pltpu.make_async_remote_copy(
            src_ref=piece,
            dst_ref=piece,
            send_sem=self.send_sem.at[0],
            recv_sem=self.recv_sem.at[part, fk, place],
            device_id=self.across[1],
            device_id_type=MESH,
        ).wait_recv()

    def _forward(self, part, stage, fk, place, own=False):
        if self.kind(part) == "line":
            return []
        return [
            self._send(part, fk, place, self.across[b], fk ^ b, own)
            for b in self.orders[part][stage:] + [1]
        ]

    def _when(self, condition, action):
        copies = []
        pl.when(condition)(lambda: copies.extend(action()))
        self.sent.append((condition, copies))

    def start(self):
        for copy in self.local:
            copy.start()
        last = self.n_grp - 1
        for part in range(len(self.parts)):
            if self.kind(part) == "lined":
                for place in range(self.n_grp):
                    self.sent.append((None, self._forward(part, 0, 0, place, True)))
                continue
            self._when(
                self.z < last, lambda: [self._send(part, 0, self.z, self.up, 0, True)]
            )
            self._when(self.z > 0, lambda: [self._send(part, 0, self.z, self.down, 0, True)])
            self.sent.append((None, self._forward(part, 0, 0, self.z, True)))

    def _line_step(self, part, j):
        z, last = self.z, self.n_grp - 1
        below, above = z - j, z + j

        def arrive(place):
            self._wait(part, 0, place)
            return self._forward(part, 0, 0, place)

        self._when(z >= j, lambda: arrive(below))
        if j < last:
            self._when(
                jnp.logical_and(z >= j, z < last),
                lambda: [self._send(part, 0, below, self.up, 0)],
            )
        self._when(above <= last, lambda: arrive(above))
        if j < last:
            self._when(
                jnp.logical_and(above <= last, z > 0),
                lambda: [self._send(part, 0, above, self.down, 0)],
            )

    def _cross_step(self, part, stage, fk, place):
        self._wait(part, fk, place)
        self.sent.append((None, self._forward(part, stage + 1, fk, place)))

    def _steps(self):
        lines = [p for p in range(len(self.parts)) if self.kind(p) != "lined"]
        crossing = [p for p in range(len(self.parts)) if self.kind(p) != "line"]
        early = [p for p in crossing if self.kind(p) == "lined"]
        bind = functools.partial

        def cross(parts, stage):
            known = [[0] for _ in parts]
            for i in range(stage):
                known = [
                    k + [v ^ self.orders[p][i] for v in k] for p, k in zip(parts, known)
                ]
            return [
                bind(self._cross_step, p, stage, k[a] ^ self.orders[p][stage], place)
                for a in range(len(known[0]) if parts else 0)
                for place in range(self.n_grp)
                for p, k in zip(parts, known)
            ]

        ahead = cross(early, 0)
        steps, self.marks = [], []
        for j in range(1, self.n_grp):
            steps += [bind(self._line_step, part, j) for part in lines]
            self.marks.append(len(steps))
            share = -(-len(ahead) // (self.n_grp - j))
            steps, ahead = steps + ahead[:share], ahead[share:]
        for stage in range(len(self.bits)):
            steps += cross([p for p in crossing if stage or p not in early], stage)
        everything = [0]
        for bit in self.bits:
            everything = everything + [v ^ bit for v in everything]
        for fk in everything:
            for place in range(self.n_grp):
                for p in crossing:
                    steps.append(bind(self._wait, p, fk ^ 1, place))
        return steps

    def run(self, until=None):
        until = len(self.steps) if until is None else until
        for step in self.steps[self.done : until]:
            step()
        self.done = max(self.done, until)

    def finish(self):
        self.run()
        for copy in self.local:
            copy.wait()
        for condition, copies in self.sent:
            if condition is None:
                for copy in copies:
                    copy().wait_send()
            else:

                def wait_sent():
                    for copy in copies:
                        copy().wait_send()

                pl.when(condition)(wait_sent)


def gather_scratch(weights, n_fsdp, n_grp):
    parts = len(gather_parts([w.shape[-2:] for w in weights]))
    bits = n_fsdp.bit_length() - 2
    crossing = n_fsdp // 2 - 1 + n_fsdp // 2
    sends = 2 + (n_grp - 1) * 2 * (bits + 1) + 2 * (n_grp - 2) + n_grp * crossing + bits + 1
    return [
        pltpu.SemaphoreType.DMA((parts * sends,)),
        pltpu.SemaphoreType.DMA((parts, n_fsdp, n_grp)),
        pltpu.SemaphoreType.DMA((len(weights),)),
    ]


def gathered(kinds, weights, n_fsdp, n_grp):
    return [
        jax.ShapeDtypeStruct(
            (n_grp if kind == "line" else n_fsdp * n_grp,) + w.shape[-2:], w.dtype
        )
        for kind, w in zip(kinds, weights)
    ]


def meet(n_fsdp, n_grp, line_only):
    f, z = lax.axis_index("fsdp"), lax.axis_index("grp")
    barrier = pltpu.get_barrier_semaphore()
    bits = [1 << i for i in range(n_fsdp.bit_length() - 1)]
    peers = [{"fsdp": flip(f, b), "grp": z} for b in bits]
    peers += [{"fsdp": f, "grp": flip(z, k)} for k in range(1, n_grp)]
    for peer in peers:
        pl.semaphore_signal(barrier, inc=1, device_id=peer, device_id_type=MESH)
    pl.semaphore_wait(barrier, len(peers))


def gather_kernel(kinds, n_fsdp, n_grp, *refs):
    meet(n_fsdp, n_grp, True)
    count = len(kinds)
    ins, outs, sems = refs[:count], refs[count : 2 * count], refs[2 * count :]
    first = [i for i, kind in enumerate(kinds) if kind == "full"]
    second = [i for i, kind in enumerate(kinds) if kind == "line"]
    gathers = [
        Gather(
            [kinds[i] for i in chosen],
            [ins[i] for i in chosen],
            [outs[i] for i in chosen],
            *sems[3 * n : 3 * n + 3],
            n_fsdp,
            n_grp,
        )
        for n, chosen in enumerate((first, second))
    ]
    gathers[0].start()
    gathers[0].run(gathers[0].marks[-2])
    gathers[1].start()
    gathers[0].run(gathers[0].marks[-1])
    for n in range(len(gathers[1].steps)):
        share = (len(gathers[0].steps) - gathers[0].marks[-1]) * (n + 1)
        gathers[0].run(gathers[0].marks[-1] + share // (2 * len(gathers[1].steps)))
        gathers[1].run(n + 1)
    for gather in gathers:
        gather.finish()


def gather_rows(kinds, weights, collective_id):
    n_fsdp, n_grp = lax.axis_size("fsdp"), lax.axis_size("grp")
    count = len(weights)
    return pl.pallas_call(
        functools.partial(gather_kernel, kinds, n_fsdp, n_grp),
        out_shape=gathered(kinds, weights, n_fsdp, n_grp),
        in_specs=[pl.BlockSpec(memory_space=pl.ANY)] * count,
        out_specs=[pl.BlockSpec(memory_space=pl.ANY)] * count,
        scratch_shapes=[
            v
            for kind in ("full", "line")
            for v in gather_scratch([w for k, w in zip(kinds, weights) if k == kind], n_fsdp, n_grp)
        ],
        compiler_params=pltpu.CompilerParams(
            collective_id=collective_id, has_side_effects=True
        ),
        name="gather_rows",
    )(*weights)


def dot_lanes(a, b):
    return lax.dot_general(a, b, (((1,), (1,)), ((), ())), preferred_element_type=F32)


def dot_rows(a, b):
    return lax.dot_general(a, b, (((0,), (0,)), ((), ())), preferred_element_type=F32)


def seen_blocks(block):
    if block == 0:
        return [(0, 0)]
    if block == 1:
        return [(0, None), (1, 0)]
    return [(0, None), (1, None), (block, block - 1)]


def column(values, index):
    lanes = lax.broadcasted_iota(jnp.int32, (1, values.shape[1]), 1)
    return jnp.sum(jnp.where(lanes == index, values, 0.0), axis=1, keepdims=True)


def pick(slots_ref, place, by_block):
    result = by_block[0]
    for block in range(1, len(by_block)):
        here = jnp.full((1, result.shape[1]), slots_ref[block], jnp.int32) == place
        result = jnp.where(here, by_block[block], result)
    return result


def attend_head(
    pair, h, blocks, head_size, slots_ref, x_ref, c_ref, mask_ref, o_ref, lse_ref
):
    scale = head_size**-0.5

    def head():
        lanes = lax.broadcasted_iota(jnp.int32, (1, 2 * head_size), 1)
        mine = lanes // head_size == h
        decays = [column(c_ref[b], 2 * pair + h) for b in range(blocks)]
        outs = []
        for block in range(blocks):
            query = jnp.where(mine, x_ref[slots_ref[block], 0] * scale, 0).astype(BF16)
            scores = []
            for other, mask in seen_blocks(block):
                s = dot_lanes(x_ref[slots_ref[other], 1], query) - decays[other]
                if mask is not None:
                    s = s + mask_ref[mask]
                scores.append(s)
            top = functools.reduce(
                jnp.maximum, [jnp.max(s, axis=0, keepdims=True) for s in scores]
            )
            total, mixed = 0.0, 0.0
            for s, (other, _) in zip(scores, seen_blocks(block)):
                weight = jnp.exp(s - top)
                total = total + jnp.sum(weight, axis=0, keepdims=True)
                mixed = mixed + dot_rows(x_ref[slots_ref[other], 2], weight.astype(BF16))
            lse_ref[pair, h, pl.ds(block, 1), :] = top + jnp.log(total)
            outs.append((mixed / total).T.astype(BF16))
        for place in range(blocks):
            o_ref[place] = jnp.where(mine, pick(slots_ref, place, outs), o_ref[place])

    head()


def sum_decay(blocks, slots_ref, log_ref, seen_ref, c_ref):
    total = 0.0
    for block in range(blocks):
        logs = log_ref[slots_ref[block]]
        high = logs.astype(BF16)
        rest = logs - high.astype(F32)
        middle = rest.astype(BF16)
        low = (rest - middle.astype(F32)).astype(BF16)
        seen = seen_ref[max(block - 1, 0)]
        local = dot_lanes(seen, high) + dot_lanes(seen, middle) + dot_lanes(seen, low)
        c_ref[block] = local + total if block < 2 else local
        if block == 0:
            total = local[local.shape[0] - 1 :, :]


class GroupExchange:
    def __init__(self, n_grp, send_sem, recv_sem):
        self.n_grp, self.send_sem, self.recv_sem = n_grp, send_sem, recv_sem
        self.f, self.z = lax.axis_index("fsdp"), lax.axis_index("grp")
        self.sent, self.landed = [], {}

    def send(self, key, index, source_of, target):
        self.landed[key] = (index, target)
        for k in range(1, self.n_grp):
            place = flip(self.z, k)
            copy = pltpu.make_async_remote_copy(
                src_ref=source_of(place),
                dst_ref=target(self.z),
                send_sem=self.send_sem.at[index, k],
                recv_sem=self.recv_sem.at[index, k],
                device_id={"fsdp": self.f, "grp": place},
                device_id_type=MESH,
            )
            copy.start()
            self.sent.append(copy)

    def wait(self, key):
        index, target = self.landed[key]
        for k in range(1, self.n_grp):
            place = flip(self.z, k)
            pltpu.make_async_remote_copy(
                src_ref=target(place),
                dst_ref=target(place),
                send_sem=self.send_sem.at[index, k],
                recv_sem=self.recv_sem.at[index, k],
                device_id={"fsdp": self.f, "grp": place},
                device_id_type=MESH,
            ).wait_recv()

    def finish(self):
        for copy in self.sent:
            copy.wait_send()


def forward_kernel(kinds, pairs, head_size, n_fsdp, n_grp, *refs):
    count = len(kinds)
    weights, refs = refs[:count], refs[count:]
    slots_ref, mixed_ref, log_ref, mask_ref, seen_ref = refs[:5]
    full, refs = refs[5 : 5 + count], refs[5 + count :]
    o_out, x_out, lse_ref, c_ref = refs[:4]
    gather_sems, refs = refs[4:7], refs[7:]
    x_refs, refs = refs[:pairs], refs[pairs:]
    o_refs, refs = refs[:pairs], refs[pairs:]
    logs_ref, send_sem, recv_sem, copy_sem = refs
    blocks = n_grp
    pair_width = 2 * head_size
    group_width = pairs * pair_width
    width = blocks * group_width
    z = lax.axis_index("grp")

    meet(n_fsdp, n_grp, False)
    gather = Gather(kinds, weights, full, *gather_sems, n_fsdp, n_grp)
    swap_heads = GroupExchange(n_grp, send_sem, recv_sem)
    started = itertools.count()

    def keep(source, target):
        copy = pltpu.make_async_copy(source, target, copy_sem.at[next(started)])
        copy.start()
        return copy

    def heads_of(part, place, pair):
        start = part * width + place * group_width + pair * pair_width
        return mixed_ref.at[:, pl.ds(pl.multiple_of(start, 128), pair_width)]

    own = []

    def send_pair(pair):
        for part in range(3):
            swap_heads.send(
                (pair, part),
                1 + 4 * pair + part,
                lambda place, pair=pair, part=part: heads_of(part, place, pair),
                lambda place, pair=pair, part=part: x_refs[pair].at[place, part],
            )
            own.append(keep(heads_of(part, z, pair), x_refs[pair].at[z, part]))

    late = []
    own_logs = keep(log_ref.at[z], logs_ref.at[z])
    swap_heads.send("logs", 0, lambda place: log_ref.at[place], lambda place: logs_ref.at[place])
    gather.start()
    send_pair(0)
    for pair in range(1, pairs):
        if pair <= len(gather.marks):
            gather.run(gather.marks[pair - 1])
        send_pair(pair)
    own_logs.wait()
    swap_heads.wait("logs")
    sum_decay(blocks, slots_ref, logs_ref, seen_ref, c_ref)
    last_wait = len(gather.steps) * 3 // 5
    share = -(-(last_wait - gather.done) // (2 * pairs))
    for pair in range(pairs):
        for part in range(3):
            own[3 * pair + part].wait()
            swap_heads.wait((pair, part))
        for h in range(2):
            attend_head(
                pair, h, blocks, head_size, slots_ref, x_refs[pair], c_ref, mask_ref,
                o_refs[pair], lse_ref,
            )
            if h == 0:
                late.append(keep(x_refs[pair], x_out.at[pair]))
                gather.run(gather.done + share)

        def columns(place, pair=pair):
            start = place * group_width + pair * pair_width
            return o_out.at[:, pl.ds(pl.multiple_of(start, 128), pair_width)]

        swap_heads.send(
            (pair, 3), 4 + 4 * pair, lambda place: o_refs[pair].at[place], columns
        )
        late.append(keep(o_refs[pair].at[z], columns(z)))
        gather.run(gather.done + share)
    gather.finish()
    for pair in range(pairs):
        swap_heads.wait((pair, 3))
    swap_heads.finish()
    for copy in late:
        copy.wait()


def forward_attention(kinds, weights, slots, mixed, logs, masks, seen, head_size, collective_id):
    n_fsdp, n_grp = lax.axis_size("fsdp"), lax.axis_size("grp")
    count = len(weights)
    tok, width = mixed.shape[0], mixed.shape[1] // 3
    pair_width = 2 * head_size
    pairs = width // n_grp // pair_width
    anywhere = pl.BlockSpec(memory_space=pl.ANY)
    vmem = pl.BlockSpec(memory_space=pltpu.VMEM)
    out = pl.pallas_call(
        functools.partial(forward_kernel, kinds, pairs, head_size, n_fsdp, n_grp),
        out_shape=gathered(kinds, weights, n_fsdp, n_grp)
        + [
            jax.ShapeDtypeStruct((tok, width), BF16),
            jax.ShapeDtypeStruct((pairs, n_grp, 3, tok, pair_width), BF16),
            jax.ShapeDtypeStruct((pairs, 2, 8, tok), F32),
            jax.ShapeDtypeStruct((n_grp, tok, logs.shape[1]), F32),
        ],
        in_specs=[anywhere] * count
        + [pl.BlockSpec(memory_space=pltpu.SMEM), anywhere, anywhere, vmem, vmem],
        out_specs=[anywhere] * count + [anywhere, anywhere, vmem, vmem],
        scratch_shapes=gather_scratch(weights, n_fsdp, n_grp)
        + [pltpu.VMEM((n_grp, 3, tok, pair_width), BF16)] * pairs
        + [pltpu.VMEM((n_grp, tok, pair_width), BF16)] * pairs
        + [
            pltpu.VMEM(logs.shape, F32),
            pltpu.SemaphoreType.DMA((1 + 4 * pairs, n_grp)),
            pltpu.SemaphoreType.DMA((1 + 4 * pairs, n_grp)),
            pltpu.SemaphoreType.DMA((1 + 5 * pairs,)),
        ],
        compiler_params=pltpu.CompilerParams(
            collective_id=collective_id, has_side_effects=True, vmem_limit_bytes=48 << 20
        ),
        name="forward_attention",
    )(*weights, slots, mixed, logs, masks, seen)
    return [v.reshape(-1, v.shape[2]) for v in out[:count]], out[count:]


def attend_back_pair(
    pair,
    blocks,
    head_size,
    slots_ref,
    x_ref,
    do_ref,
    c_ref,
    mask_ref,
    lse_ref,
    dx_ref,
    query_decay_ref,
    key_decay_ref,
):
    scale = head_size**-0.5

    def head(h, carry):
        lanes = lax.broadcasted_iota(jnp.int32, (1, 2 * head_size), 1)
        mine = lanes // head_size == h
        index = 2 * pair + h
        mine_decay = lax.broadcasted_iota(jnp.int32, (1, c_ref.shape[2]), 1) == index
        decays = [column(c_ref[b], index) for b in range(blocks)]
        query_grads = [None] * blocks
        key_grads, value_grads = [None] * blocks, [None] * blocks
        decay_grads = [None] * blocks

        def add(store, at, value):
            store[at] = value if store[at] is None else store[at] + value

        for block in range(blocks):
            query = jnp.where(mine, x_ref[slots_ref[block], 0] * scale, 0).astype(BF16)
            grad_o = jnp.where(mine, do_ref[slots_ref[block]], 0).astype(BF16)
            lse = lse_ref[pair, h, pl.ds(block, 1), :]
            weights, grads, delta = [], [], 0.0
            for other, mask in seen_blocks(block):
                s = dot_lanes(x_ref[slots_ref[other], 1], query) - decays[other]
                if mask is not None:
                    s = s + mask_ref[mask]
                weight = jnp.exp(s - lse)
                grad = dot_lanes(x_ref[slots_ref[other], 2], grad_o)
                delta = delta + jnp.sum(weight * grad, axis=0, keepdims=True)
                weights.append(weight)
                grads.append(grad)
            query_grad, query_decay = 0.0, 0.0
            for weight, grad, (other, _) in zip(weights, grads, seen_blocks(block)):
                ds = weight * (grad - delta)
                query_decay = query_decay + jnp.sum(ds, axis=0, keepdims=True)
                add(decay_grads, other, jnp.sum(ds, axis=1, keepdims=True))
                low = ds.astype(BF16)
                query_grad = query_grad + dot_rows(x_ref[slots_ref[other], 1], low)
                add(key_grads, other, jnp.dot(low, query, preferred_element_type=F32))
                add(
                    value_grads,
                    other,
                    jnp.dot(weight.astype(BF16), grad_o, preferred_element_type=F32),
                )
            query_grads[block] = (query_grad * scale).T
            turned = jnp.broadcast_to(query_decay, (c_ref.shape[2], query_decay.shape[1])).T
            query_decay_ref[block] = jnp.where(mine_decay, turned, query_decay_ref[block])
        for block in range(blocks):
            key_decay_ref[block] = jnp.where(
                mine_decay, decay_grads[block], key_decay_ref[block]
            )
        for part, by_block in enumerate((query_grads, key_grads, value_grads)):
            low = [v.astype(BF16) for v in by_block]
            for place in range(blocks):
                dx_ref[place, part] = jnp.where(
                    mine, pick(slots_ref, place, low), dx_ref[place, part]
                )
        return carry

    lax.fori_loop(0, 2, head, 0)


def split3(values):
    high = values.astype(BF16)
    rest = values - high.astype(F32)
    middle = rest.astype(BF16)
    return high, middle, (rest - middle.astype(F32)).astype(BF16)


def sum_decay_back(blocks, slots_ref, seen_ref, query_decay_ref, key_decay_ref, logs_ref):
    after = 0.0
    for block in range(2, blocks):
        after = after + jnp.sum(query_decay_ref[block], axis=0, keepdims=True)
    by_block = [None] * blocks
    for block in reversed(range(blocks)):
        grad = query_decay_ref[block] - key_decay_ref[block]
        seen = seen_ref[max(block - 1, 0)]
        value = sum(dot_rows(seen, part) for part in split3(grad))
        by_block[block] = value if block >= 2 else value + after
        if block == 1:
            after = after + jnp.sum(grad, axis=0, keepdims=True)
    for place in range(blocks):
        logs_ref[place] = pick(slots_ref, place, by_block)


def halving_orders(n_fsdp):
    bits = [1 << i for i in range(n_fsdp.bit_length() - 2)]
    return bits[::-1], bits


def kept_pieces(order):
    keep = [0]
    for bit in reversed(order[1:]):
        keep = keep + [k ^ bit for k in keep]
    return keep


class Scatter:
    def __init__(
        self, parts, groups, received, ahead, send_sem, recv_sem, line_sem, local_sem, n_fsdp, n_grp
    ):
        self.parts, self.groups, self.n_grp = parts, groups, n_grp
        self.received, self.ahead = received, ahead
        self.saved = []
        self.send_sem, self.recv_sem = send_sem, recv_sem
        self.line_sem, self.local_sem = line_sem, local_sem
        self.f, self.z = lax.axis_index("fsdp"), lax.axis_index("grp")
        orders = halving_orders(n_fsdp)
        self.orders = [orders[i % 2] for i in range(len(parts))]
        self.keeps = [kept_pieces(o) for o in self.orders]
        self.up = {"fsdp": self.f, "grp": self.z + 1}
        self.down = {"fsdp": self.f, "grp": self.z - 1}
        self.across = {b: {"fsdp": flip(self.f, 2 * b), "grp": self.z} for b in orders[1]}
        self.sent, self.count = [], [0] * len(parts)

    def stage_of(self, part, k):
        order = self.orders[part]
        return next((i for i, b in enumerate(order) if k & b), len(order))

    def slot(self, part, k, stage):
        slots = [(v, j) for v in self.keeps[part] for j in range(self.stage_of(part, v))]
        return slots.index((k, stage))

    def _send(self, part, source, target, recv_sem, to):
        index = self.count[part]
        self.count[part] += 1

        def copy():
            return pltpu.make_async_remote_copy(
                src_ref=source(),
                dst_ref=target(),
                send_sem=self.send_sem.at[part, index],
                recv_sem=recv_sem(),
                device_id=to,
                device_id_type=MESH,
            )

        copy().start()
        return copy

    def _cross(self, part, place, k, stage, source):
        bit = self.orders[part][stage]
        slot = self.slot(part, k ^ bit, stage)
        copy = self._send(
            part,
            lambda: source,
            lambda: self.parts[part][3].at[slot, place],
            lambda: self.recv_sem.at[part, slot, place],
            self.across[bit],
        )
        self.sent.append((None, [copy]))

    def _arrived(self, target, recv_sem):
        pltpu.make_async_remote_copy(
            src_ref=target,
            dst_ref=target,
            send_sem=self.send_sem.at[0, 0],
            recv_sem=recv_sem,
            device_id=self.across[1],
            device_id_type=MESH,
        ).wait_recv()

    def _load(self, part, place, i):
        kept, held = self.parts[part][1:3]
        return pltpu.make_async_copy(
            kept.at[i, place], held.at[i, place], self.local_sem.at[part, i, place]
        )

    def _fill(self, part, place, i):
        away, arrived = self.parts[part][0], self.parts[part][3]
        slot = self.slot(part, self.keeps[part][i], 0)
        return pltpu.make_async_copy(
            away.at[i, place], arrived.at[slot, place], self.recv_sem.at[part, slot, place]
        )

    def _begin(self, part, place):
        away = self.parts[part][0]
        for i, k in reversed(list(enumerate(self.keeps[part]))):
            if part in self.received:
                self._fill(part, place, i).start()
            else:
                self._cross(part, place, k ^ self.orders[part][0], 0, away.at[i, place])
            if self.parts[part][1] is not None:
                self._load(part, place, i).start()

    def _add_arrived(self, part, place, k):
        held, arrived = self.parts[part][2], self.parts[part][3]
        i = self.keeps[part].index(k)
        if self.parts[part][1] is not None:
            self._load(part, place, i).wait()
        for stage in range(self.stage_of(part, k)):
            slot = self.slot(part, k, stage)
            if stage == 0 and part in self.received:
                self._fill(part, place, i).wait()
            else:
                self._arrived(arrived.at[slot, place], self.recv_sem.at[part, slot, place])
        total = held[i, place]
        for stage in range(self.stage_of(part, k)):
            total = total + arrived[self.slot(part, k, stage), place]
        held[i, place] = total
        return held.at[i, place]

    def _save(self, part, place):
        source = self._add_arrived(part, place, 0)
        if self.parts[part][4] is None:
            copy = pltpu.make_async_copy(
                source, self.parts[part][6].at[place], self.local_sem.at[part, 0, place]
            )
            copy.start()
            self.saved.append(copy)

    def _halve(self, part, place, k):
        source = self._add_arrived(part, place, k)
        self._cross(part, place, k, self.stage_of(part, k), source)

    def _when(self, condition, action):
        copies = []
        pl.when(condition)(lambda: copies.extend(action()))
        self.sent.append((condition, copies))

    def _line(self, part, place, hop):
        last = self.n_grp - 1
        held = self.parts[part][2]
        ways = []
        if hop < place:
            ways.append((self.z == hop, 4, 0, self.up))
        if last - hop > place:
            ways.append((self.z == last - hop, 5, 1, self.down))
        for condition, which, way, to in ways:
            passing = self.parts[part][which]

            def action(passing=passing, way=way, to=to):
                target = lambda: passing.at[place]
                sem = lambda: self.line_sem.at[part, way, place]
                if hop == 0:
                    return [self._send(part, lambda: held.at[0, place], target, sem, to)]
                self._arrived(target(), sem())
                passing[place] = passing[place] + held[0, place]
                return [self._send(part, target, target, sem, to)]

            self._when(condition, action)

    def _result(self, part):
        held, below, above, result, columns = (self.parts[part][i] for i in (2, 4, 5, 6, 7))
        z, last = self.z, self.n_grp - 1
        result[:, columns] = held[0, z].astype(F32)

        def add(passing, index):
            self._arrived(passing.at[z], self.line_sem.at[part, index, z])
            result[:, columns] = result[:, columns] + passing[z].astype(F32)

        pl.when(z > 0)(lambda: add(below, 0))
        pl.when(z < last)(lambda: add(above, 1))

    def waves(self):
        bind = functools.partial
        low, high, places = 0, self.n_grp - 1, []
        while low <= high:
            places += [high] if low == high else [high, low]
            low, high = low + 1, high - 1
        units = []
        for i, count in enumerate(self.groups):
            first = sum(self.groups[:i])
            group = range(first, first + count)
            units += [(part, place) for place in places for part in group]
        ahead, stages = self.ahead, len(self.orders[0])
        length = len(units) + ahead + 2 * stages + 4 * self.n_grp
        waves = [[] for _ in range(length)]
        final = {}
        for n, (part, place) in enumerate(units):
            waves[max(0, n + 1 - ahead)].append(bind(self._begin, part, place))
            at = n + 1
            for stage in range(1, stages):
                for k in self.keeps[part]:
                    if self.stage_of(part, k) == stage:
                        waves[at].append(bind(self._halve, part, place, k))
                at += 2
            waves[at].append(bind(self._save, part, place))
            if self.parts[part][4] is None:
                continue
            for hop in range(self.n_grp - 1):
                waves[at + 2 * hop].append(bind(self._line, part, place, hop))
            final[part] = at + 2 * (self.n_grp - 1)
        for part, at in final.items():
            waves[at].append(bind(self._result, part))
        return waves

    def finish(self):
        for copy in self.saved:
            copy.wait()
        for condition, copies in self.sent:
            if condition is None:
                for copy in copies:
                    copy().wait_send()
            else:

                def wait_sent():
                    for copy in copies:
                        copy().wait_send()

                pl.when(condition)(wait_sent)


def scatter_buffers(kind, rows, width, n_fsdp, n_grp):
    m = n_fsdp.bit_length() - 2
    keep = n_fsdp // 4
    slots = m + sum(i << (m - 1 - i) for i in range(1, m))
    leading = {
        "full": [(keep, n_grp), (slots, n_grp), (n_grp,), (n_grp,)],
        "cross": [(keep, n_grp), (slots, n_grp)],
    }[kind]
    return [pltpu.VMEM(v + (rows, width), BF16) for v in leading]


def scatter_scratch(kinds, sizes, n_fsdp, n_grp, parts=None):
    m = n_fsdp.bit_length() - 2
    keep = n_fsdp // 4
    slots = m + sum(i << (m - 1 - i) for i in range(1, m))
    parts = parts or len(kinds)
    shapes = [
        pltpu.SemaphoreType.DMA((parts, n_grp * (2 * keep + 2 * n_grp))),
        pltpu.SemaphoreType.DMA((parts, slots, n_grp)),
        pltpu.SemaphoreType.DMA((parts, 2, n_grp)),
        pltpu.SemaphoreType.DMA((parts, keep, n_grp)),
    ]
    for kind, (rows, width) in zip(kinds, sizes):
        shapes += scatter_buffers(kind, rows, width, n_fsdp, n_grp)
    return shapes


def scatter_parts(kinds, aways, kepts, buffers, results):
    parts, buffers = [], list(buffers)
    for kind, away, kept, result in zip(kinds, aways, kepts, results):
        count = {"full": 4, "cross": 2}[kind]
        mine, buffers = buffers[:count], buffers[count:]
        if kind == "cross":
            mine = mine + [None, None]
        parts.append((away, kept, *mine, *result))
    return parts, buffers


def column_ranges(widths):
    start, ranges = 0, []
    for width in widths:
        ranges.append(pl.ds(start, width))
        start += width
    return ranges


def last_kernel(widths, lines, n_fsdp, n_grp, *refs):
    mixed_ref, narrow_ref, l_ref, l_other_ref, w_hbm, forget_ref = refs[:6]
    tokens_ref, scale_ref, gain_ref, resid_ref, small_ref = refs[6:11]
    count, more = len(widths), sum(len(w) for w in lines)
    lined, refs = refs[11 : 11 + more], refs[11 + more :]
    wide_ref, narrow_result, grad_ref, dgain_refs = refs[0], refs[1], refs[2], refs[3:6]
    results, refs = refs[6 : 6 + len(lines)], refs[6 + len(lines) :]
    sems, refs = refs[:4], refs[4:]
    ranges = column_ranges(widths)
    gathered_refs, aways, refs = refs[:more], refs[more : more + count], refs[more + count :]
    places = [(wide_ref, c) for c in ranges[:-1]] + [(narrow_result, pl.ds(0, widths[-1]))]
    parts, refs = scatter_parts(["full"] * count, aways, [None] * count, refs, places)
    mixed_other, narrow_other, rows_ref, w_ref, act_ref, incoming, send_sem, recv_sem, w_sem, own_sem, group_send, group_recv, total_ref = refs
    f, z = lax.axis_index("fsdp"), lax.axis_index("grp")
    tok, width = act_ref.shape
    pieces = n_fsdp // 2

    meet(n_fsdp, n_grp, False)

    def exchange(source, target, index, peer):
        return pltpu.make_async_remote_copy(
            src_ref=source,
            dst_ref=target,
            send_sem=send_sem.at[index],
            recv_sem=recv_sem.at[index],
            device_id=peer,
            device_id_type=MESH,
        )

    sibling = {"fsdp": flip(f, 1), "grp": z}
    others = []
    for i in range(count):
        if i < count - 1:
            pair = (mixed_ref.at[:, ranges[i]], mixed_other.at[:, ranges[i]])
        else:
            pair = (narrow_ref, narrow_other)
        others.append(exchange(*pair, i, sibling))
        others[-1].start()

    chunk = w_ref.shape[2]
    chunks = w_hbm.shape[1] // chunk

    def fetch(i):
        return pltpu.make_async_copy(
            w_hbm.at[:, pl.ds(i * chunk, chunk)], w_ref.at[i % 2], w_sem.at[i % 2]
        )

    fetch(0).start()
    for k in range(pieces):
        row = flip(f // 2, k) * 2 + f % 2
        rows_ref[k, :, :tok] = l_ref[row]
        rows_ref[k, :, tok:] = l_other_ref[row]

    scatter = Scatter(parts, [count], (), AHEAD, *sems, n_fsdp, n_grp)
    waves = iter(scatter.waves())

    def advance(steps=None):
        for wave in itertools.islice(waves, steps):
            for step in wave:
                step()

    direct = GroupExchange(n_grp, group_send, group_recv)
    own = []
    for i, (source, target) in enumerate(zip(lined, gathered_refs)):
        direct.send(
            i, i, lambda place, source=source: source.at[place],
            lambda place, target=target: target.at[place],
        )
        own.append(pltpu.make_async_copy(source.at[z], target.at[z], own_sem.at[i]))
        own[-1].start()

    def products(part, ks, target):
        if part < count - 1:
            right = (mixed_ref[:, ranges[part]], mixed_other[:, ranges[part]])
        else:
            right = (narrow_ref[...], narrow_other[...])
        right = jnp.concatenate(right, axis=0)
        left = jnp.concatenate([rows_ref[k] for k in ks], axis=0)
        value = jnp.dot(left, right, preferred_element_type=F32).astype(BF16)
        target[...] = value.reshape(target.shape)

    for part in range(count):
        others[part].wait_recv()
        first = scatter.orders[part][0]
        products(part, [k ^ first for k in scatter.keeps[part]], aways[part])
    advance(1)
    for part in range(count):
        products(part, scatter.keeps[part], parts[part][2])
    act_ref[...] = dot_lanes(narrow_ref[...], forget_ref[...])
    for i in range(chunks):
        if i + 1 < chunks:
            fetch(i + 1).start()
        fetch(i).wait()
        act_ref[...] += dot_lanes(mixed_ref[:, pl.ds(i * chunk, chunk)], w_ref[i % 2])
        advance(1)

    block = next(t for t in (64, 32, 16, 8) if tok % t == 0)
    total_ref[0] = small_ref[...]

    def finish_rows(i, carry):
        rows = pl.ds(pl.multiple_of(i * block, block), block)
        scale = scale_ref[rows, :]
        normed = tokens_ref[rows, :].astype(F32) * scale
        act = act_ref[rows, :]
        total_ref[0, :, :width] += jnp.sum(act * normed, axis=0, keepdims=True)
        scaled = act * gain_ref[...]
        average = jnp.mean(scaled * normed, axis=1, keepdims=True)
        grad_ref[rows, :] = (
            resid_ref[rows, :] + scale * (scaled - normed * average)
        ).astype(BF16)
        return carry

    lax.fori_loop(0, tok // block, finish_rows, 0)
    peers = [{"fsdp": f, "grp": flip(z, 1 << i)} for i in range(n_grp.bit_length() - 1)]
    peers += [{"fsdp": flip(f, 1 << i), "grp": z} for i in range(n_fsdp.bit_length() - 1)]
    sent = []
    for i, peer in enumerate(peers):
        copy = exchange(total_ref.at[i], incoming.at[i], count + i, peer)
        copy.start()
        sent.append(copy)
        advance(1)
        copy.wait_recv()
        total_ref[i + 1] = total_ref[i] + incoming[i]
    total = total_ref[len(peers)]
    for ref, start in zip(dgain_refs, (0, width, 2 * width)):
        ref[...] = total[:, start : start + ref.shape[1]]
    advance()
    i = 0
    for ref, line in zip(results, lines):
        for columns in column_ranges(line):
            own[i].wait()
            direct.wait(i)
            value = gathered_refs[i][0].astype(F32)
            for place in range(1, n_grp):
                value = value + gathered_refs[i][place].astype(F32)
            ref[:, columns] = value
            i += 1
    scatter.finish()
    direct.finish()
    for copy in others + sent:
        copy.wait_send()


def last_gradients(
    acts, mixed, narrow, w_qkv, forget, tokens, scale, gain, resid, small, lines, collective_id
):
    n_fsdp, n_grp = lax.axis_size("fsdp"), lax.axis_size("grp")
    tok, wide = mixed.shape
    width = tokens.shape[1]
    own_rows = width // (n_fsdp * n_grp)
    split = 4 if wide % 512 == 0 else 2
    more = sum(len(w) for w in lines)
    widths = [wide // split] * split + [narrow.shape[1]]
    keep = n_fsdp // 4
    rounds = n_fsdp.bit_length() + n_grp.bit_length() - 2
    aways = [jax.ShapeDtypeStruct((keep, n_grp, own_rows, w), BF16) for w in widths]
    chunk = next(t for t in (512, 384, 256, 128) if wide % t == 0)
    vmem = pl.BlockSpec(memory_space=pltpu.VMEM)
    anywhere = pl.BlockSpec(memory_space=pl.ANY)
    return pl.pallas_call(
        functools.partial(
            last_kernel, widths, [[v.shape[2] for v in w] for w in lines], n_fsdp, n_grp
        ),
        out_shape=[
            jax.ShapeDtypeStruct((own_rows, wide), F32),
            jax.ShapeDtypeStruct((own_rows, widths[-1]), F32),
            jax.ShapeDtypeStruct(tokens.shape, BF16),
            jax.ShapeDtypeStruct((1, width), F32),
            jax.ShapeDtypeStruct((1, width), F32),
            jax.ShapeDtypeStruct((1, widths[-1]), F32),
        ]
        + [
            jax.ShapeDtypeStruct((w[0].shape[1], sum(v.shape[2] for v in w)), F32) for w in lines
        ],
        in_specs=[vmem] * 4
        + [anywhere]
        + [vmem] * 6
        + [anywhere] * sum(len(w) for w in lines),
        out_specs=[vmem] * (6 + len(lines)),
        scratch_shapes=scatter_scratch([], [], n_fsdp, n_grp, len(widths))
        + [pltpu.VMEM(v.shape, BF16) for w in lines for v in w]
        + [pltpu.VMEM(a.shape, BF16) for a in aways]
        + [v for a in aways for v in scatter_buffers("full", *a.shape[2:], n_fsdp, n_grp)]
        + [
            pltpu.VMEM(mixed.shape, BF16),
            pltpu.VMEM(narrow.shape, BF16),
            pltpu.VMEM((n_fsdp // 2, n_grp * own_rows, 2 * tok), BF16),
            pltpu.VMEM((2, width, chunk), BF16),
            pltpu.VMEM((tok, width), F32),
            pltpu.VMEM((rounds, 1, small.shape[1]), F32),
            pltpu.SemaphoreType.DMA((len(widths) + rounds,)),
            pltpu.SemaphoreType.DMA((len(widths) + rounds,)),
            pltpu.SemaphoreType.DMA((2,)),
            pltpu.SemaphoreType.DMA((max(1, more),)),
            pltpu.SemaphoreType.DMA((max(1, more), n_grp)),
            pltpu.SemaphoreType.DMA((max(1, more), n_grp)),
            pltpu.VMEM((rounds + 1, 1, small.shape[1]), F32),
        ],
        compiler_params=pltpu.CompilerParams(
            collective_id=collective_id, has_side_effects=True, vmem_limit_bytes=58 << 20
        ),
        name="last_gradients",
    )(
        mixed, narrow, acts[0], acts[1], w_qkv, forget, tokens, scale, gain, resid, small,
        *(v for w in lines for v in w),
    )


def backward_kernel(kinds, widths, received, pairs, head_size, n_fsdp, n_grp, *refs):
    count = sum(len(w) for w in widths)
    aways, kepts, refs = refs[:count], refs[count : 2 * count], refs[2 * count :]
    slots_ref, grad_ref, x_hbm, c_ref, mask_ref, seen_ref, lse_ref = refs[:7]
    refs = refs[7:]
    results, part_kinds = [], []
    for kind, w in zip(kinds, widths):
        if kind == "full":
            results += [(refs[0], columns) for columns in column_ranges(w)]
            refs = refs[1:]
        else:
            results += [(ref, None) for ref in refs[: len(w)]]
            refs = refs[len(w) :]
        part_kinds += [kind] * len(w)
    mixed_out, logs_out = refs[:2]
    sems = refs[2:6]
    parts, refs = scatter_parts(part_kinds, aways, kepts, refs[6:], results)
    x_refs, refs = refs[:pairs], refs[pairs:]
    do_refs, refs = refs[:pairs], refs[pairs:]
    dx_refs, refs = refs[:pairs], refs[pairs:]
    query_decay_ref, key_decay_ref, logs_ref, send_sem, recv_sem, copy_sem = refs
    blocks = n_grp
    pair_width = 2 * head_size
    group_width = pairs * pair_width
    width = blocks * group_width
    z = lax.axis_index("grp")

    meet(n_fsdp, n_grp, False)
    scatter = Scatter(parts, [len(w) for w in widths], received, AHEAD, *sems, n_fsdp, n_grp)
    swap_heads = GroupExchange(n_grp, send_sem, recv_sem)
    started = itertools.count()

    def keep(source, target):
        copy = pltpu.make_async_copy(source, target, copy_sem.at[next(started)])
        copy.start()
        return copy

    def heads_of(ref, part, place, pair):
        start = part * width + place * group_width + pair * pair_width
        return ref.at[:, pl.ds(pl.multiple_of(start, 128), pair_width)]

    own, late = [], []
    for pair in range(pairs):
        swap_heads.send(
            (pair, "do"),
            4 * pair,
            lambda place, pair=pair: heads_of(grad_ref, 0, place, pair),
            lambda place, pair=pair: do_refs[pair].at[place],
        )
        own.append(keep(heads_of(grad_ref, 0, z, pair), do_refs[pair].at[z]))
        own.append(keep(x_hbm.at[pair], x_refs[pair]))
    waves = iter(scatter.waves())

    def advance(count=None):
        for wave in itertools.islice(waves, count):
            for step in wave:
                step()

    advance(1)
    for pair in range(pairs):
        own[2 * pair].wait()
        own[2 * pair + 1].wait()
        swap_heads.wait((pair, "do"))
        attend_back_pair(
            pair,
            blocks,
            head_size,
            slots_ref,
            x_refs[pair],
            do_refs[pair],
            c_ref,
            mask_ref,
            lse_ref,
            dx_refs[pair],
            query_decay_ref,
            key_decay_ref,
        )
        for part in range(3):
            swap_heads.send(
                (pair, part),
                1 + 4 * pair + part,
                lambda place, pair=pair, part=part: dx_refs[pair].at[place, part],
                lambda place, pair=pair, part=part: heads_of(mixed_out, part, place, pair),
            )
            late.append(keep(dx_refs[pair].at[z, part], heads_of(mixed_out, part, z, pair)))
        advance(3)
    sum_decay_back(blocks, slots_ref, seen_ref, query_decay_ref, key_decay_ref, logs_ref)
    swap_heads.send(
        "logs",
        4 * pairs,
        lambda place: logs_ref.at[place],
        lambda place: logs_out.at[place],
    )
    late.append(keep(logs_ref.at[z], logs_out.at[z]))
    advance()
    for pair in range(pairs):
        for part in range(3):
            swap_heads.wait((pair, part))
    swap_heads.wait("logs")
    scatter.finish()
    swap_heads.finish()
    for copy in late:
        copy.wait()


def backward_attention(
    kinds, weights, received, slots, grad, x, decay, masks, seen, lse, head_size, collective_id
):
    n_fsdp, n_grp = lax.axis_size("fsdp"), lax.axis_size("grp")
    aways = [away for parts in weights for away, _ in parts]
    kepts = [kept for parts in weights for _, kept in parts]
    widths = [[away.shape[3] for away, _ in parts] for parts in weights]
    pairs, _, _, tok, pair_width = x.shape
    lanes = decay.shape[2]
    anywhere = pl.BlockSpec(memory_space=pl.ANY)
    vmem = pl.BlockSpec(memory_space=pltpu.VMEM)
    shapes, specs = [], []
    for kind, parts, w in zip(kinds, weights, widths):
        own_rows = parts[0][0].shape[2]
        if kind == "full":
            shapes.append(jax.ShapeDtypeStruct((own_rows, sum(w)), F32))
            specs.append(vmem)
        else:
            shapes += [jax.ShapeDtypeStruct((n_grp, own_rows, v), BF16) for v in w]
            specs += [anywhere] * len(w)
    part_kinds = [kind for kind, w in zip(kinds, widths) for _ in w]
    out = pl.pallas_call(
        functools.partial(
            backward_kernel, kinds, widths, received, pairs, head_size, n_fsdp, n_grp
        ),
        out_shape=shapes
        + [
            jax.ShapeDtypeStruct((tok, 3 * grad.shape[1]), BF16),
            jax.ShapeDtypeStruct((n_grp, tok, lanes), F32),
        ],
        in_specs=[anywhere] * (2 * len(aways))
        + [pl.BlockSpec(memory_space=pltpu.SMEM), anywhere, anywhere]
        + [vmem] * 4,
        out_specs=specs + [anywhere] * 2,
        scratch_shapes=scatter_scratch(
            part_kinds, [v.shape[2:] for v in aways], n_fsdp, n_grp
        )
        + [pltpu.VMEM((n_grp, 3, tok, pair_width), BF16)] * pairs
        + [pltpu.VMEM((n_grp, tok, pair_width), BF16)] * pairs
        + [pltpu.VMEM((n_grp, 3, tok, pair_width), BF16)] * pairs
        + [pltpu.VMEM((n_grp, tok, lanes), F32)] * 3
        + [
            pltpu.SemaphoreType.DMA((1 + 4 * pairs, n_grp)),
            pltpu.SemaphoreType.DMA((1 + 4 * pairs, n_grp)),
            pltpu.SemaphoreType.DMA((1 + 5 * pairs,)),
        ],
        compiler_params=pltpu.CompilerParams(
            collective_id=collective_id, has_side_effects=True, vmem_limit_bytes=62 << 20
        ),
        name="backward_attention",
    )(*aways, *kepts, slots, grad, x, decay, masks, seen, lse)
    return out[:-2], out[-2], out[-1]


def project_kernel(act_ref, w_ref, out_ref):
    out_ref[...] = jnp.dot(act_ref[...], w_ref[...], preferred_element_type=F32).astype(BF16)


def project(act, w):
    tok, width = act.shape
    columns = w.shape[1]
    tile = next(t for t in (768, 512, 384, 256, 128) if columns % t == 0)
    return pl.pallas_call(
        project_kernel,
        out_shape=jax.ShapeDtypeStruct((tok, columns), BF16),
        grid=(columns // tile,),
        in_specs=[
            pl.BlockSpec((tok, width), lambda j: (0, 0), pipeline_mode=pl.Buffered(1)),
            pl.BlockSpec((width, tile), lambda j: (0, j)),
        ],
        out_specs=pl.BlockSpec((tok, tile), lambda j: (0, j)),
        compiler_params=pltpu.CompilerParams(vmem_limit_bytes=60 << 20),
        cost_estimate=pl.CostEstimate(
            flops=2 * tok * width * columns,
            bytes_accessed=2 * (width + tok) * columns,
            transcendentals=0,
        ),
        name="project",
    )(act, w)


def feed_forward_kernel(
    o_ref,
    tokens_ref,
    grad_ref,
    gain_ref,
    w_out_ref,
    gate_ref,
    up_ref,
    down_ref,
    inner_ref,
    dgate_ref,
    dup_ref,
    o_turned_ref,
    act_turned_ref,
    out_ref,
    dresid_ref,
    dbranch_ref,
    do_ref,
    dgain_ref,
    resid_ref,
    act_ref,
    sum_ref,
    dact_ref,
):
    tok = o_ref.shape[0]
    block = next(t for t in (128, 64, 32, 16, 8) if tok % t == 0)

    def rows_of(i):
        return pl.ds(pl.multiple_of(i * block, block), block)

    def norm(rows):
        resid = resid_ref[rows, :]
        scale = lax.rsqrt(jnp.mean(resid * resid, axis=1, keepdims=True) + EPSILON)
        return resid, resid * scale, scale

    @pl.when(pl.program_id(0) == 0)
    def _():
        resid_ref[...] = jnp.dot(o_ref[...], w_out_ref[...], preferred_element_type=F32)

        def begin(i, carry):
            rows = rows_of(i)
            resid_ref[rows, :] = tokens_ref[rows, :].astype(F32) + resid_ref[rows, :]
            _, normed, _ = norm(rows)
            act_ref[rows, :] = (normed * gain_ref[...]).astype(BF16)
            return carry

        lax.fori_loop(0, tok // block, begin, 0)
        sum_ref[...] = jnp.zeros_like(sum_ref)
        dact_ref[...] = jnp.zeros_like(dact_ref)
        o_turned_ref[...] = o_ref[...].T
        act_turned_ref[...] = act_ref[...].T

    act = act_ref[...]
    gate = jnp.dot(act, gate_ref[...], preferred_element_type=F32)
    up = jnp.dot(act, up_ref[...], preferred_element_type=F32)
    grad_inner = dot_lanes(grad_ref[...], down_ref[...])
    sigma = jax.nn.sigmoid(gate)
    swish = gate * sigma
    inner = (swish * up).astype(BF16)
    dgate = (grad_inner * up * (sigma * (1.0 + gate * (1.0 - sigma)))).astype(BF16)
    dup = (grad_inner * swish).astype(BF16)
    inner_ref[...] = inner.T
    dgate_ref[...] = dgate
    dup_ref[...] = dup
    sum_ref[...] += jnp.dot(inner, down_ref[...], preferred_element_type=F32)
    dact_ref[...] += dot_lanes(dgate, gate_ref[...]) + dot_lanes(dup, up_ref[...])

    @pl.when(pl.program_id(0) == pl.num_programs(0) - 1)
    def _():
        dgain_ref[...] = jnp.zeros_like(dgain_ref)

        def end(i, carry):
            rows = rows_of(i)
            resid, normed, scale = norm(rows)
            out_ref[rows, :] = (resid + sum_ref[rows, :]).astype(BF16)
            dact = dact_ref[rows, :]
            dgain_ref[...] += jnp.sum(dact * normed, axis=0, keepdims=True)
            scaled = dact * gain_ref[...]
            average = jnp.mean(scaled * normed, axis=1, keepdims=True)
            dresid = grad_ref[rows, :].astype(F32) + scale * (scaled - normed * average)
            dresid_ref[rows, :] = dresid
            dbranch_ref[rows, :] = dresid.astype(BF16)
            return carry

        lax.fori_loop(0, tok // block, end, 0)
        do_ref[...] = dot_lanes(dbranch_ref[...], w_out_ref[...]).astype(BF16)


def feed_forward(attn_o, tokens, grad, gain, w_out, gate_up, down):
    tok, width = tokens.shape
    hidden = down.shape[0]
    tile = 512
    steps = hidden // tile
    once = lambda rows, columns: pl.BlockSpec(
        (rows, columns), lambda j: (0, 0), pipeline_mode=pl.Buffered(1)
    )
    rows = once(tok, width)
    columns = pl.BlockSpec((tok, tile), lambda j: (0, j))
    low = lambda *shape: jax.ShapeDtypeStruct(shape, BF16)
    return pl.pallas_call(
        feed_forward_kernel,
        out_shape=[
            low(hidden, tok),
            low(tok, hidden),
            low(tok, hidden),
            low(width, tok),
            low(width, tok),
            low(tok, width),
            jax.ShapeDtypeStruct((tok, width), F32),
            low(tok, width),
            low(tok, width),
            jax.ShapeDtypeStruct((1, width), F32),
        ],
        grid=(steps,),
        in_specs=[
            rows,
            rows,
            rows,
            once(1, width),
            once(width, width),
            pl.BlockSpec((width, tile), lambda j: (0, j)),
            pl.BlockSpec((width, tile), lambda j: (0, steps + j)),
            pl.BlockSpec((tile, width), lambda j: (j, 0)),
        ],
        out_specs=[
            pl.BlockSpec((tile, tok), lambda j: (j, 0)),
            columns,
            columns,
            once(width, tok),
            once(width, tok),
            rows,
            rows,
            rows,
            rows,
            once(1, width),
        ],
        scratch_shapes=[
            pltpu.VMEM((tok, width), F32),
            pltpu.VMEM((tok, width), BF16),
            pltpu.VMEM((tok, width), F32),
            pltpu.VMEM((tok, width), F32),
        ],
        compiler_params=pltpu.CompilerParams(vmem_limit_bytes=60 << 20),
        cost_estimate=pl.CostEstimate(
            flops=12 * tok * width * hidden,
            bytes_accessed=6 * width * hidden,
            transcendentals=tok * hidden,
        ),
        name="feed_forward",
    )(attn_o, tokens, grad, gain, w_out, gate_up, gate_up, down)


def weight_grad_kernel(count, ids, *refs):
    own, other, (r_ref, r_other_ref, *outs) = (
        refs[: 2 * count],
        refs[2 * count : 4 * count],
        refs[4 * count :],
    )
    rows = [jnp.concatenate([ref[0] for ref in side], axis=0) for side in (own, other)]
    total = jnp.dot(
        jnp.concatenate(rows, axis=1),
        jnp.concatenate([r_ref[...], r_other_ref[...]], axis=0),
        preferred_element_type=F32,
    )
    total = total.astype(BF16).reshape(2 * count, -1, total.shape[1])
    outs[0][...] = total[:count]
    outs[1][...] = total[count:]


def weight_grad(ids, l_own, l_other, r_own, r_other, start, width):
    count = ids.shape[0] // 2
    _, rows, tok = l_own.shape
    limit = 1024 if rows * count < 1024 else 384
    tile = max(t for t in range(128, limit + 1, 128) if width % t == 0 and start % t == 0)
    steps, first = width // tile, start // tile
    pieces = [
        pl.BlockSpec(
            (1, rows, tok), lambda n, ids, k=k: (ids[k], 0, 0), pipeline_mode=pl.Buffered(1)
        )
        for k in range(2 * count)
    ]
    r_spec = pl.BlockSpec((tok, tile), lambda n, ids: (0, first + n))
    out_spec = pl.BlockSpec((count, rows, tile), lambda n, ids: (0, 0, n))
    return pl.pallas_call(
        functools.partial(weight_grad_kernel, count),
        out_shape=[jax.ShapeDtypeStruct((count, rows, width), BF16)] * 2,
        grid_spec=pltpu.PrefetchScalarGridSpec(
            num_scalar_prefetch=1,
            grid=(steps,),
            in_specs=pieces * 2 + [r_spec, r_spec],
            out_specs=[out_spec, out_spec],
        ),
        compiler_params=pltpu.CompilerParams(vmem_limit_bytes=60 << 20),
        cost_estimate=pl.CostEstimate(
            flops=8 * count * rows * tok * width,
            bytes_accessed=2 * (2 * count * rows * width + 2 * tok * width),
            transcendentals=0,
        ),
        name="weight_grad",
    )(ids, *[l_own] * (2 * count), *[l_other] * (2 * count), r_own, r_other)


def both_cores(turned):
    n_fsdp = lax.axis_size("fsdp")
    turned = turned.reshape(n_fsdp, turned.shape[0] // n_fsdp, turned.shape[1])
    return turned, swap(turned, "fsdp", 1)


def partial_rows(left, columns):
    n_fsdp, n_grp = lax.axis_size("fsdp"), lax.axis_size("grp")
    f = lax.axis_index("fsdp")
    parts = []
    for part, (right, right_other, start, width) in enumerate(columns):
        order = halving_orders(n_fsdp)[part % 2]
        keep = kept_pieces(order)
        ids = jnp.stack([flip(f // 2, k) for k in [k ^ order[0] for k in keep] + keep])
        pair = weight_grad(
            2 * ids + f % 2, left[0], left[1], right, right_other, start, width
        )
        parts.append(
            tuple(v.reshape(v.shape[0], n_grp, v.shape[1] // n_grp, width) for v in pair)
        )
    return parts


def norm_rows(features):
    row_scale = lax.rsqrt(jnp.mean(features * features, axis=-1, keepdims=True) + EPSILON)
    return (features * row_scale, row_scale)


def norm_back(grad_normed, normed, row_scale):
    average_addend = jnp.mean(grad_normed * normed, axis=-1, keepdims=True)
    return row_scale * (grad_normed - normed * average_addend)


def contract_cols(first_op, second_op):
    return lax.dot_general(
        first_op, second_op, (((1,), (1,)), ((), ())), preferred_element_type=F32
    )


def on_device(
    tokens,
    block_order,
    cont_lengths,
    gain_attn,
    w_qkv,
    w_forget,
    b_forget,
    w_out,
    gain_ffn,
    w_gate_up,
    w_down,
    grad_out,
):
    tok, width = tokens.shape
    heads = w_forget.shape[1]
    head_size = width // heads
    blocks = lax.axis_size("grp")
    own_heads = heads // blocks
    pairs = own_heads // 2
    group_width = width // blocks
    slots = block_order[0]

    positions = jnp.arange(tok, dtype=jnp.int32)
    causal = positions[None, :] <= positions[:, None]
    seg_ends = jnp.cumsum(cont_lengths[0], axis=1)
    segment = jnp.sum((positions[None, :, None] >= seg_ends[:, None, :]).astype(jnp.int32), axis=2)
    within = jnp.logical_and(segment[:, :, None] == segment[:, None, :], causal[None])
    seen = jnp.concatenate([causal[None], within], axis=0)
    masks = jnp.where(seen.transpose(0, 2, 1), 0.0, NEG).astype(F32)
    seen_low = seen.astype(BF16)

    forget_pad = 128 - heads
    qkv_full, forget_full, out_line, down_line = gather_rows(
        ("full", "full", "line", "line"),
        [w_qkv, jnp.pad(w_forget, ((0, 0), (0, forget_pad))), w_out, w_down],
        1,
    )
    qkv_full, forget_full = (v.reshape(-1, v.shape[2]) for v in (qkv_full, forget_full))
    inputs = tokens.astype(F32)
    normed_one, scale_one = norm_rows(inputs)
    acts = (normed_one * gain_attn).astype(BF16)
    grad_out_other = swap(grad_out, "fsdp", 1)
    acts_rows = both_cores(acts.T)
    logits = jnp.dot(acts, forget_full, preferred_element_type=F32)[:, :heads] + b_forget
    log_keep = jax.nn.log_sigmoid(logits)
    mixed = project(acts, qkv_full)
    mixed, grad_out_other = lax.optimization_barrier((mixed, grad_out_other))

    logs = jnp.pad(
        log_keep.T.reshape(blocks, own_heads, tok), ((0, 0), (0, 8 - own_heads), (0, 0))
    )
    (out_full, gate_up_full, down_full), (attn_o, x, lse, decay) = forward_attention(
        ("lined", "full", "lined"), [out_line, w_gate_up, down_line], slots, mixed, logs, masks, seen_low, head_size, 2
    )

    half, hidden = width // 2, down_full.shape[0]
    (
        inner_turned,
        grad_gate,
        grad_up,
        attn_turned,
        acts_two_turned,
        output,
        grad_resid,
        grad_branch,
        grad_heads,
        gain_two_grad,
    ) = feed_forward(attn_o, tokens, grad_out, gain_ffn[None], out_full, gate_up_full, down_full)
    down_rows = both_cores(inner_turned)
    down_rows, *later = lax.optimization_barrier(
        (down_rows, grad_gate, grad_up, grad_branch, acts_two_turned, attn_turned)
    )
    grad_gate_other, grad_up_other, grad_branch_other = (swap(v, "fsdp", 1) for v in later[:3])
    acts_two_rows, attn_rows = both_cores(later[3]), both_cores(later[4])
    part_down = partial_rows(
        down_rows, [(grad_out, grad_out_other, 0, half), (grad_out, grad_out_other, half, half)]
    )
    orders = halving_orders(lax.axis_size("fsdp"))
    part_down, grad_gate, grad_up, grad_branch = lax.optimization_barrier(
        (part_down, grad_gate, grad_up, grad_branch)
    )
    part_down = [
        (swap(away, "fsdp", 2 * order[0]), kept)
        for (away, kept), order in zip(part_down, orders)
    ]
    part_gate_up = partial_rows(
        acts_two_rows,
        [(grad_gate, grad_gate_other, 0, hidden), (grad_up, grad_up_other, 0, hidden)],
    )
    part_out = partial_rows(
        attn_rows,
        [
            (grad_branch, grad_branch_other, 0, half),
            (grad_branch, grad_branch_other, half, half),
        ],
    )

    sums, grad_mixed, log_grad = backward_attention(
        ("cross", "full", "cross"),
        [part_down, part_gate_up, part_out],
        range(len(part_down)),
        slots,
        grad_heads,
        x,
        decay,
        masks,
        seen_low,
        lse,
        head_size,
        3,
    )
    log_grad = log_grad[:, :, :own_heads].transpose(1, 0, 2).reshape(tok, heads)
    grad_logits = (log_grad * jax.nn.sigmoid(-logits)).astype(BF16)
    narrow = jnp.pad(grad_logits, ((0, 0), (0, forget_pad)))
    bias_grad = jnp.sum(narrow.astype(F32), axis=0)
    (
        grad_qkv,
        grad_forget,
        grad_tokens,
        grad_gain,
        grad_gain_two,
        grad_bias,
        grad_down,
        grad_out_w,
    ) = last_gradients(
        acts_rows,
        grad_mixed,
        narrow,
        qkv_full,
        forget_full,
        tokens,
        scale_one,
        gain_attn[None],
        grad_resid,
        jnp.concatenate([jnp.zeros((width,), F32), gain_two_grad[0], bias_grad])[None],
        [sums[:2], sums[3:]],
        4,
    )
    return (
        output,
        grad_tokens,
        grad_gain[0],
        grad_qkv,
        grad_forget[:, :heads],
        grad_bias[0, :heads],
        grad_out_w,
        grad_gain_two[0],
        sums[2],
        grad_down,
    )


def solution(mesh):
    both = P(("fsdp", "grp"), None)
    in_specs = (
        both,
        P("fsdp", None),
        P("fsdp", None, None),
        P(),
        both,
        both,
        P(),
        both,
        P(),
        both,
        both,
        both,
    )
    out_specs = (both, both, P(), both, both, P(), both, P(), both, both)
    return jax.shard_map(
        on_device, mesh=mesh, in_specs=in_specs, out_specs=out_specs, check_vma=False
    )
```

```python
import functools
import itertools

import jax
import jax.numpy as jnp
from jax import lax
from jax.experimental import pallas as pl
from jax.experimental.pallas import tpu as pltpu
from jax.sharding import PartitionSpec as P

EPSILON = 1e-05
NEG = -1e30
AHEAD = 10
MESH = pl.DeviceIdType.MESH
F32 = jnp.float32
BF16 = jnp.bfloat16


def flip_bit(value, bit):
    return value + bit - 2 * bit * ((value // bit) % 2)


def flip(value, mask):
    bit = 1
    while bit <= mask:
        if mask & bit:
            value = flip_bit(value, bit)
        bit *= 2
    return value


def swap(value, axis, mask):
    return lax.ppermute(value, axis, [(i, i ^ mask) for i in range(lax.axis_size(axis))])


def gather_parts(shapes):
    return [(w, h) for w, s in enumerate(shapes) for h in (0, 1) if h == 0 or s[1] % 256 == 0]


class Gather:
    def __init__(self, kinds, ins, outs, send_sem, recv_sem, local_sem, n_fsdp, n_grp):
        self.kinds, self.ins, self.outs = kinds, ins, outs
        self.send_sem, self.recv_sem = send_sem, recv_sem
        self.f, self.z, self.n_grp = lax.axis_index("fsdp"), lax.axis_index("grp"), n_grp
        self.bits = [1 << i for i in range(1, n_fsdp.bit_length() - 1)]
        self.parts = gather_parts([r.shape[-2:] for r in ins])
        self.orders = [self.bits if h == 0 else self.bits[::-1] for _, h in self.parts]
        self.across = {b: {"fsdp": flip(self.f, b), "grp": self.z} for b in self.bits + [1]}
        self.up = {"fsdp": self.f, "grp": self.z + 1}
        self.down = {"fsdp": self.f, "grp": self.z - 1}
        self.count, self.sent, self.local = 0, [], []
        for w in range(len(ins)):
            target = {
                "full": self.f * n_grp + self.z,
                "line": self.z,
                "lined": pl.ds(self.f * n_grp, n_grp),
            }[kinds[w]]
            self.local.append(
                pltpu.make_async_copy(ins[w], outs[w].at[target], local_sem.at[w])
            )
        self.steps, self.done = self._steps(), 0

    def _columns(self, part):
        w, h = self.parts[part]
        width = self.ins[w].shape[-1]
        return pl.ds(0, width) if width % 256 else pl.ds(h * (width // 2), width // 2)

    def kind(self, part):
        return self.kinds[self.parts[part][0]]

    def _piece(self, part, fk, place):
        row = place if self.kind(part) == "line" else flip(self.f, fk) * self.n_grp + place
        return self.outs[self.parts[part][0]].at[row, :, self._columns(part)]

    def _send(self, part, fk, place, to, to_fk, own=False):
        index = self.count
        self.count += 1

        def copy():
            source = self._piece(part, fk, place)
            if own:
                source = self.ins[self.parts[part][0]]
                source = source.at[place] if self.kind(part) == "lined" else source
                source = source.at[:, self._columns(part)]
            return pltpu.make_async_remote_copy(
                src_ref=source,
                dst_ref=self._piece(part, fk, place),
                send_sem=self.send_sem.at[index],
                recv_sem=self.recv_sem.at[part, to_fk, place],
                device_id=to,
                device_id_type=MESH,
            )

        copy().start()
        return copy

    def _wait(self, part, fk, place):
        piece = self._piece(part, fk, place)
        pltpu.make_async_remote_copy(
            src_ref=piece,
            dst_ref=piece,
            send_sem=self.send_sem.at[0],
            recv_sem=self.recv_sem.at[part, fk, place],
            device_id=self.across[1],
            device_id_type=MESH,
        ).wait_recv()

    def _forward(self, part, stage, fk, place, own=False):
        if self.kind(part) == "line":
            return []
        return [
            self._send(part, fk, place, self.across[b], fk ^ b, own)
            for b in self.orders[part][stage:] + [1]
        ]

    def _when(self, condition, action):
        copies = []
        pl.when(condition)(lambda: copies.extend(action()))
        self.sent.append((condition, copies))

    def start(self):
        for copy in self.local:
            copy.start()
        last = self.n_grp - 1
        for part in range(len(self.parts)):
            if self.kind(part) == "lined":
                for place in range(self.n_grp):
                    self.sent.append((None, self._forward(part, 0, 0, place, True)))
                continue
            self._when(
                self.z < last, lambda: [self._send(part, 0, self.z, self.up, 0, True)]
            )
            self._when(self.z > 0, lambda: [self._send(part, 0, self.z, self.down, 0, True)])
            self.sent.append((None, self._forward(part, 0, 0, self.z, True)))

    def _line_step(self, part, j):
        z, last = self.z, self.n_grp - 1
        below, above = z - j, z + j

        def arrive(place):
            self._wait(part, 0, place)
            return self._forward(part, 0, 0, place)

        self._when(z >= j, lambda: arrive(below))
        if j < last:
            self._when(
                jnp.logical_and(z >= j, z < last),
                lambda: [self._send(part, 0, below, self.up, 0)],
            )
        self._when(above <= last, lambda: arrive(above))
        if j < last:
            self._when(
                jnp.logical_and(above <= last, z > 0),
                lambda: [self._send(part, 0, above, self.down, 0)],
            )

    def _cross_step(self, part, stage, fk, place):
        self._wait(part, fk, place)
        self.sent.append((None, self._forward(part, stage + 1, fk, place)))

    def _steps(self):
        lines = [p for p in range(len(self.parts)) if self.kind(p) != "lined"]
        crossing = [p for p in range(len(self.parts)) if self.kind(p) != "line"]
        early = [p for p in crossing if self.kind(p) == "lined"]
        bind = functools.partial

        def cross(parts, stage):
            known = [[0] for _ in parts]
            for i in range(stage):
                known = [
                    k + [v ^ self.orders[p][i] for v in k] for p, k in zip(parts, known)
                ]
            return [
                bind(self._cross_step, p, stage, k[a] ^ self.orders[p][stage], place)
                for a in range(len(known[0]) if parts else 0)
                for place in range(self.n_grp)
                for p, k in zip(parts, known)
            ]

        ahead = cross(early, 0)
        steps, self.marks = [], []
        for j in range(1, self.n_grp):
            steps += [bind(self._line_step, part, j) for part in lines]
            self.marks.append(len(steps))
            share = -(-len(ahead) // (self.n_grp - j))
            steps, ahead = steps + ahead[:share], ahead[share:]
        for stage in range(len(self.bits)):
            steps += cross([p for p in crossing if stage or p not in early], stage)
        everything = [0]
        for bit in self.bits:
            everything = everything + [v ^ bit for v in everything]
        for fk in everything:
            for place in range(self.n_grp):
                for p in crossing:
                    steps.append(bind(self._wait, p, fk ^ 1, place))
        return steps

    def run(self, until=None):
        until = len(self.steps) if until is None else until
        for step in self.steps[self.done : until]:
            step()
        self.done = max(self.done, until)

    def finish(self):
        self.run()
        for copy in self.local:
            copy.wait()
        for condition, copies in self.sent:
            if condition is None:
                for copy in copies:
                    copy().wait_send()
            else:

                def wait_sent():
                    for copy in copies:
                        copy().wait_send()

                pl.when(condition)(wait_sent)


def gather_scratch(weights, n_fsdp, n_grp):
    parts = len(gather_parts([w.shape[-2:] for w in weights]))
    bits = n_fsdp.bit_length() - 2
    crossing = n_fsdp // 2 - 1 + n_fsdp // 2
    sends = 2 + (n_grp - 1) * 2 * (bits + 1) + 2 * (n_grp - 2) + n_grp * crossing + bits + 1
    return [
        pltpu.SemaphoreType.DMA((parts * sends,)),
        pltpu.SemaphoreType.DMA((parts, n_fsdp, n_grp)),
        pltpu.SemaphoreType.DMA((len(weights),)),
    ]


def gathered(kinds, weights, n_fsdp, n_grp):
    return [
        jax.ShapeDtypeStruct(
            (n_grp if kind == "line" else n_fsdp * n_grp,) + w.shape[-2:], w.dtype
        )
        for kind, w in zip(kinds, weights)
    ]


def meet(n_fsdp, n_grp, line_only):
    f, z = lax.axis_index("fsdp"), lax.axis_index("grp")
    barrier = pltpu.get_barrier_semaphore()
    bits = [1 << i for i in range(n_fsdp.bit_length() - 1)]
    peers = [{"fsdp": flip(f, b), "grp": z} for b in bits]
    peers += [{"fsdp": f, "grp": flip(z, k)} for k in range(1, n_grp)]
    for peer in peers:
        pl.semaphore_signal(barrier, inc=1, device_id=peer, device_id_type=MESH)
    pl.semaphore_wait(barrier, len(peers))


def gather_kernel(kinds, n_fsdp, n_grp, *refs):
    meet(n_fsdp, n_grp, True)
    count = len(kinds)
    ins, outs, sems = refs[:count], refs[count : 2 * count], refs[2 * count :]
    first = [i for i, kind in enumerate(kinds) if kind == "full"]
    second = [i for i, kind in enumerate(kinds) if kind == "line"]
    gathers = [
        Gather(
            [kinds[i] for i in chosen],
            [ins[i] for i in chosen],
            [outs[i] for i in chosen],
            *sems[3 * n : 3 * n + 3],
            n_fsdp,
            n_grp,
        )
        for n, chosen in enumerate((first, second))
    ]
    gathers[0].start()
    gathers[0].run(gathers[0].marks[-2])
    gathers[1].start()
    gathers[0].run(gathers[0].marks[-1])
    for n in range(len(gathers[1].steps)):
        share = (len(gathers[0].steps) - gathers[0].marks[-1]) * (n + 1)
        gathers[0].run(gathers[0].marks[-1] + share // (2 * len(gathers[1].steps)))
        gathers[1].run(n + 1)
    for gather in gathers:
        gather.finish()


def gather_rows(kinds, weights, collective_id):
    n_fsdp, n_grp = lax.axis_size("fsdp"), lax.axis_size("grp")
    count = len(weights)
    return pl.pallas_call(
        functools.partial(gather_kernel, kinds, n_fsdp, n_grp),
        out_shape=gathered(kinds, weights, n_fsdp, n_grp),
        in_specs=[pl.BlockSpec(memory_space=pl.ANY)] * count,
        out_specs=[pl.BlockSpec(memory_space=pl.ANY)] * count,
        scratch_shapes=[
            v
            for kind in ("full", "line")
            for v in gather_scratch([w for k, w in zip(kinds, weights) if k == kind], n_fsdp, n_grp)
        ],
        compiler_params=pltpu.CompilerParams(
            collective_id=collective_id, has_side_effects=True
        ),
        name="gather_rows",
    )(*weights)


def dot_lanes(a, b):
    return lax.dot_general(a, b, (((1,), (1,)), ((), ())), preferred_element_type=F32)


def dot_rows(a, b):
    return lax.dot_general(a, b, (((0,), (0,)), ((), ())), preferred_element_type=F32)


def seen_blocks(block):
    if block == 0:
        return [(0, 0)]
    if block == 1:
        return [(0, None), (1, 0)]
    return [(0, None), (1, None), (block, block - 1)]


def column(values, index):
    lanes = lax.broadcasted_iota(jnp.int32, (1, values.shape[1]), 1)
    return jnp.sum(jnp.where(lanes == index, values, 0.0), axis=1, keepdims=True)


def pick(slots_ref, place, by_block):
    result = by_block[0]
    for block in range(1, len(by_block)):
        here = jnp.full((1, result.shape[1]), slots_ref[block], jnp.int32) == place
        result = jnp.where(here, by_block[block], result)
    return result


def attend_head(
    pair, h, blocks, head_size, slots_ref, x_ref, c_ref, mask_ref, o_ref, lse_ref
):
    scale = head_size**-0.5

    def head():
        lanes = lax.broadcasted_iota(jnp.int32, (1, 2 * head_size), 1)
        mine = lanes // head_size == h
        decays = [column(c_ref[b], 2 * pair + h) for b in range(blocks)]
        outs = []
        for block in range(blocks):
            query = jnp.where(mine, x_ref[slots_ref[block], 0] * scale, 0).astype(BF16)
            scores = []
            for other, mask in seen_blocks(block):
                s = dot_lanes(x_ref[slots_ref[other], 1], query) - decays[other]
                if mask is not None:
                    s = s + mask_ref[mask]
                scores.append(s)
            top = functools.reduce(
                jnp.maximum, [jnp.max(s, axis=0, keepdims=True) for s in scores]
            )
            total, mixed = 0.0, 0.0
            for s, (other, _) in zip(scores, seen_blocks(block)):
                weight = jnp.exp(s - top)
                total = total + jnp.sum(weight, axis=0, keepdims=True)
                mixed = mixed + dot_rows(x_ref[slots_ref[other], 2], weight.astype(BF16))
            lse_ref[pair, h, pl.ds(block, 1), :] = top + jnp.log(total)
            outs.append((mixed / total).T.astype(BF16))
        for place in range(blocks):
            o_ref[place] = jnp.where(mine, pick(slots_ref, place, outs), o_ref[place])

    head()


def sum_decay(blocks, slots_ref, log_ref, seen_ref, c_ref):
    total = 0.0
    for block in range(blocks):
        logs = log_ref[slots_ref[block]]
        high = logs.astype(BF16)
        rest = logs - high.astype(F32)
        middle = rest.astype(BF16)
        low = (rest - middle.astype(F32)).astype(BF16)
        seen = seen_ref[max(block - 1, 0)]
        local = dot_lanes(seen, high) + dot_lanes(seen, middle) + dot_lanes(seen, low)
        c_ref[block] = local + total if block < 2 else local
        if block == 0:
            total = local[local.shape[0] - 1 :, :]


class GroupExchange:
    def __init__(self, n_grp, send_sem, recv_sem):
        self.n_grp, self.send_sem, self.recv_sem = n_grp, send_sem, recv_sem
        self.f, self.z = lax.axis_index("fsdp"), lax.axis_index("grp")
        self.sent, self.landed = [], {}

    def send(self, key, index, source_of, target):
        self.landed[key] = (index, target)
        for k in range(1, self.n_grp):
            place = flip(self.z, k)
            copy = pltpu.make_async_remote_copy(
                src_ref=source_of(place),
                dst_ref=target(self.z),
                send_sem=self.send_sem.at[index, k],
                recv_sem=self.recv_sem.at[index, k],
                device_id={"fsdp": self.f, "grp": place},
                device_id_type=MESH,
            )
            copy.start()
            self.sent.append(copy)

    def wait(self, key):
        index, target = self.landed[key]
        for k in range(1, self.n_grp):
            place = flip(self.z, k)
            pltpu.make_async_remote_copy(
                src_ref=target(place),
                dst_ref=target(place),
                send_sem=self.send_sem.at[index, k],
                recv_sem=self.recv_sem.at[index, k],
                device_id={"fsdp": self.f, "grp": place},
                device_id_type=MESH,
            ).wait_recv()

    def finish(self):
        for copy in self.sent:
            copy.wait_send()


def forward_kernel(kinds, pairs, head_size, n_fsdp, n_grp, *refs):
    count = len(kinds)
    weights, refs = refs[:count], refs[count:]
    slots_ref, mixed_ref, log_ref, mask_ref, seen_ref = refs[:5]
    full, refs = refs[5 : 5 + count], refs[5 + count :]
    o_out, x_out, lse_ref, c_ref = refs[:4]
    gather_sems, refs = refs[4:7], refs[7:]
    x_refs, refs = refs[:pairs], refs[pairs:]
    o_refs, refs = refs[:pairs], refs[pairs:]
    logs_ref, send_sem, recv_sem, copy_sem = refs
    blocks = n_grp
    pair_width = 2 * head_size
    group_width = pairs * pair_width
    width = blocks * group_width
    z = lax.axis_index("grp")

    meet(n_fsdp, n_grp, False)
    gather = Gather(kinds, weights, full, *gather_sems, n_fsdp, n_grp)
    swap_heads = GroupExchange(n_grp, send_sem, recv_sem)
    started = itertools.count()

    def keep(source, target):
        copy = pltpu.make_async_copy(source, target, copy_sem.at[next(started)])
        copy.start()
        return copy

    def heads_of(part, place, pair):
        start = part * width + place * group_width + pair * pair_width
        return mixed_ref.at[:, pl.ds(pl.multiple_of(start, 128), pair_width)]

    own = []

    def send_pair(pair):
        for part in range(3):
            swap_heads.send(
                (pair, part),
                1 + 4 * pair + part,
                lambda place, pair=pair, part=part: heads_of(part, place, pair),
                lambda place, pair=pair, part=part: x_refs[pair].at[place, part],
            )
            own.append(keep(heads_of(part, z, pair), x_refs[pair].at[z, part]))

    late = []
    own_logs = keep(log_ref.at[z], logs_ref.at[z])
    swap_heads.send("logs", 0, lambda place: log_ref.at[place], lambda place: logs_ref.at[place])
    gather.start()
    send_pair(0)
    for pair in range(1, pairs):
        if pair <= len(gather.marks):
            gather.run(gather.marks[pair - 1])
        send_pair(pair)
    own_logs.wait()
    swap_heads.wait("logs")
    sum_decay(blocks, slots_ref, logs_ref, seen_ref, c_ref)
    last_wait = len(gather.steps) * 3 // 5
    share = -(-(last_wait - gather.done) // (2 * pairs))
    for pair in range(pairs):
        for part in range(3):
            own[3 * pair + part].wait()
            swap_heads.wait((pair, part))
        for h in range(2):
            attend_head(
                pair, h, blocks, head_size, slots_ref, x_refs[pair], c_ref, mask_ref,
                o_refs[pair], lse_ref,
            )
            if h == 0:
                late.append(keep(x_refs[pair], x_out.at[pair]))
                gather.run(gather.done + share)

        def columns(place, pair=pair):
            start = place * group_width + pair * pair_width
            return o_out.at[:, pl.ds(pl.multiple_of(start, 128), pair_width)]

        swap_heads.send(
            (pair, 3), 4 + 4 * pair, lambda place: o_refs[pair].at[place], columns
        )
        late.append(keep(o_refs[pair].at[z], columns(z)))
        gather.run(gather.done + share)
    gather.finish()
    for pair in range(pairs):
        swap_heads.wait((pair, 3))
    swap_heads.finish()
    for copy in late:
        copy.wait()


def forward_attention(kinds, weights, slots, mixed, logs, masks, seen, head_size, collective_id):
    n_fsdp, n_grp = lax.axis_size("fsdp"), lax.axis_size("grp")
    count = len(weights)
    tok, width = mixed.shape[0], mixed.shape[1] // 3
    pair_width = 2 * head_size
    pairs = width // n_grp // pair_width
    anywhere = pl.BlockSpec(memory_space=pl.ANY)
    vmem = pl.BlockSpec(memory_space=pltpu.VMEM)
    out = pl.pallas_call(
        functools.partial(forward_kernel, kinds, pairs, head_size, n_fsdp, n_grp),
        out_shape=gathered(kinds, weights, n_fsdp, n_grp)
        + [
            jax.ShapeDtypeStruct((tok, width), BF16),
            jax.ShapeDtypeStruct((pairs, n_grp, 3, tok, pair_width), BF16),
            jax.ShapeDtypeStruct((pairs, 2, 8, tok), F32),
            jax.ShapeDtypeStruct((n_grp, tok, logs.shape[1]), F32),
        ],
        in_specs=[anywhere] * count
        + [pl.BlockSpec(memory_space=pltpu.SMEM), anywhere, anywhere, vmem, vmem],
        out_specs=[anywhere] * count + [anywhere, anywhere, vmem, vmem],
        scratch_shapes=gather_scratch(weights, n_fsdp, n_grp)
        + [pltpu.VMEM((n_grp, 3, tok, pair_width), BF16)] * pairs
        + [pltpu.VMEM((n_grp, tok, pair_width), BF16)] * pairs
        + [
            pltpu.VMEM(logs.shape, F32),
            pltpu.SemaphoreType.DMA((1 + 4 * pairs, n_grp)),
            pltpu.SemaphoreType.DMA((1 + 4 * pairs, n_grp)),
            pltpu.SemaphoreType.DMA((1 + 5 * pairs,)),
        ],
        compiler_params=pltpu.CompilerParams(
            collective_id=collective_id, has_side_effects=True, vmem_limit_bytes=48 << 20
        ),
        name="forward_attention",
    )(*weights, slots, mixed, logs, masks, seen)
    return [v.reshape(-1, v.shape[2]) for v in out[:count]], out[count:]


def attend_back_pair(
    pair,
    blocks,
    head_size,
    slots_ref,
    x_ref,
    do_ref,
    c_ref,
    mask_ref,
    lse_ref,
    dx_ref,
    query_decay_ref,
    key_decay_ref,
):
    scale = head_size**-0.5

    def head(h, carry):
        lanes = lax.broadcasted_iota(jnp.int32, (1, 2 * head_size), 1)
        mine = lanes // head_size == h
        index = 2 * pair + h
        mine_decay = lax.broadcasted_iota(jnp.int32, (1, c_ref.shape[2]), 1) == index
        decays = [column(c_ref[b], index) for b in range(blocks)]
        query_grads = [None] * blocks
        key_grads, value_grads = [None] * blocks, [None] * blocks
        decay_grads = [None] * blocks

        def add(store, at, value):
            store[at] = value if store[at] is None else store[at] + value

        for block in range(blocks):
            query = jnp.where(mine, x_ref[slots_ref[block], 0] * scale, 0).astype(BF16)
            grad_o = jnp.where(mine, do_ref[slots_ref[block]], 0).astype(BF16)
            lse = lse_ref[pair, h, pl.ds(block, 1), :]
            weights, grads, delta = [], [], 0.0
            for other, mask in seen_blocks(block):
                s = dot_lanes(x_ref[slots_ref[other], 1], query) - decays[other]
                if mask is not None:
                    s = s + mask_ref[mask]
                weight = jnp.exp(s - lse)
                grad = dot_lanes(x_ref[slots_ref[other], 2], grad_o)
                delta = delta + jnp.sum(weight * grad, axis=0, keepdims=True)
                weights.append(weight)
                grads.append(grad)
            query_grad, query_decay = 0.0, 0.0
            for weight, grad, (other, _) in zip(weights, grads, seen_blocks(block)):
                ds = weight * (grad - delta)
                query_decay = query_decay + jnp.sum(ds, axis=0, keepdims=True)
                add(decay_grads, other, jnp.sum(ds, axis=1, keepdims=True))
                low = ds.astype(BF16)
                query_grad = query_grad + dot_rows(x_ref[slots_ref[other], 1], low)
                add(key_grads, other, jnp.dot(low, query, preferred_element_type=F32))
                add(
                    value_grads,
                    other,
                    jnp.dot(weight.astype(BF16), grad_o, preferred_element_type=F32),
                )
            query_grads[block] = (query_grad * scale).T
            turned = jnp.broadcast_to(query_decay, (c_ref.shape[2], query_decay.shape[1])).T
            query_decay_ref[block] = jnp.where(mine_decay, turned, query_decay_ref[block])
        for block in range(blocks):
            key_decay_ref[block] = jnp.where(
                mine_decay, decay_grads[block], key_decay_ref[block]
            )
        for part, by_block in enumerate((query_grads, key_grads, value_grads)):
            low = [v.astype(BF16) for v in by_block]
            for place in range(blocks):
                dx_ref[place, part] = jnp.where(
                    mine, pick(slots_ref, place, low), dx_ref[place, part]
                )
        return carry

    lax.fori_loop(0, 2, head, 0)


def split3(values):
    high = values.astype(BF16)
    rest = values - high.astype(F32)
    middle = rest.astype(BF16)
    return high, middle, (rest - middle.astype(F32)).astype(BF16)


def sum_decay_back(blocks, slots_ref, seen_ref, query_decay_ref, key_decay_ref, logs_ref):
    after = 0.0
    for block in range(2, blocks):
        after = after + jnp.sum(query_decay_ref[block], axis=0, keepdims=True)
    by_block = [None] * blocks
    for block in reversed(range(blocks)):
        grad = query_decay_ref[block] - key_decay_ref[block]
        seen = seen_ref[max(block - 1, 0)]
        value = sum(dot_rows(seen, part) for part in split3(grad))
        by_block[block] = value if block >= 2 else value + after
        if block == 1:
            after = after + jnp.sum(grad, axis=0, keepdims=True)
    for place in range(blocks):
        logs_ref[place] = pick(slots_ref, place, by_block)


def halving_orders(n_fsdp):
    bits = [1 << i for i in range(n_fsdp.bit_length() - 2)]
    return bits[::-1], bits


def kept_pieces(order):
    keep = [0]
    for bit in reversed(order[1:]):
        keep = keep + [k ^ bit for k in keep]
    return keep


class Scatter:
    def __init__(
        self, parts, groups, received, ahead, send_sem, recv_sem, line_sem, local_sem, n_fsdp, n_grp
    ):
        self.parts, self.groups, self.n_grp = parts, groups, n_grp
        self.received, self.ahead = received, ahead
        self.saved = []
        self.send_sem, self.recv_sem = send_sem, recv_sem
        self.line_sem, self.local_sem = line_sem, local_sem
        self.f, self.z = lax.axis_index("fsdp"), lax.axis_index("grp")
        orders = halving_orders(n_fsdp)
        self.orders = [orders[i % 2] for i in range(len(parts))]
        self.keeps = [kept_pieces(o) for o in self.orders]
        self.up = {"fsdp": self.f, "grp": self.z + 1}
        self.down = {"fsdp": self.f, "grp": self.z - 1}
        self.across = {b: {"fsdp": flip(self.f, 2 * b), "grp": self.z} for b in orders[1]}
        self.sent, self.count = [], [0] * len(parts)

    def stage_of(self, part, k):
        order = self.orders[part]
        return next((i for i, b in enumerate(order) if k & b), len(order))

    def slot(self, part, k, stage):
        slots = [(v, j) for v in self.keeps[part] for j in range(self.stage_of(part, v))]
        return slots.index((k, stage))

    def _send(self, part, source, target, recv_sem, to):
        index = self.count[part]
        self.count[part] += 1

        def copy():
            return pltpu.make_async_remote_copy(
                src_ref=source(),
                dst_ref=target(),
                send_sem=self.send_sem.at[part, index],
                recv_sem=recv_sem(),
                device_id=to,
                device_id_type=MESH,
            )

        copy().start()
        return copy

    def _cross(self, part, place, k, stage, source):
        bit = self.orders[part][stage]
        slot = self.slot(part, k ^ bit, stage)
        copy = self._send(
            part,
            lambda: source,
            lambda: self.parts[part][3].at[slot, place],
            lambda: self.recv_sem.at[part, slot, place],
            self.across[bit],
        )
        self.sent.append((None, [copy]))

    def _arrived(self, target, recv_sem):
        pltpu.make_async_remote_copy(
            src_ref=target,
            dst_ref=target,
            send_sem=self.send_sem.at[0, 0],
            recv_sem=recv_sem,
            device_id=self.across[1],
            device_id_type=MESH,
        ).wait_recv()

    def _load(self, part, place, i):
        kept, held = self.parts[part][1:3]
        return pltpu.make_async_copy(
            kept.at[i, place], held.at[i, place], self.local_sem.at[part, i, place]
        )

    def _fill(self, part, place, i):
        away, arrived = self.parts[part][0], self.parts[part][3]
        slot = self.slot(part, self.keeps[part][i], 0)
        return pltpu.make_async_copy(
            away.at[i, place], arrived.at[slot, place], self.recv_sem.at[part, slot, place]
        )

    def _begin(self, part, place):
        away = self.parts[part][0]
        for i, k in reversed(list(enumerate(self.keeps[part]))):
            if part in self.received:
                self._fill(part, place, i).start()
            else:
                self._cross(part, place, k ^ self.orders[part][0], 0, away.at[i, place])
            if self.parts[part][1] is not None:
                self._load(part, place, i).start()

    def _add_arrived(self, part, place, k):
        held, arrived = self.parts[part][2], self.parts[part][3]
        i = self.keeps[part].index(k)
        if self.parts[part][1] is not None:
            self._load(part, place, i).wait()
        for stage in range(self.stage_of(part, k)):
            slot = self.slot(part, k, stage)
            if stage == 0 and part in self.received:
                self._fill(part, place, i).wait()
            else:
                self._arrived(arrived.at[slot, place], self.recv_sem.at[part, slot, place])
        total = held[i, place]
        for stage in range(self.stage_of(part, k)):
            total = total + arrived[self.slot(part, k, stage), place]
        held[i, place] = total
        return held.at[i, place]

    def _save(self, part, place):
        source = self._add_arrived(part, place, 0)
        if self.parts[part][4] is None:
            copy = pltpu.make_async_copy(
                source, self.parts[part][6].at[place], self.local_sem.at[part, 0, place]
            )
            copy.start()
            self.saved.append(copy)

    def _halve(self, part, place, k):
        source = self._add_arrived(part, place, k)
        self._cross(part, place, k, self.stage_of(part, k), source)

    def _when(self, condition, action):
        copies = []
        pl.when(condition)(lambda: copies.extend(action()))
        self.sent.append((condition, copies))

    def _line(self, part, place, hop):
        last = self.n_grp - 1
        held = self.parts[part][2]
        ways = []
        if hop < place:
            ways.append((self.z == hop, 4, 0, self.up))
        if last - hop > place:
            ways.append((self.z == last - hop, 5, 1, self.down))
        for condition, which, way, to in ways:
            passing = self.parts[part][which]

            def action(passing=passing, way=way, to=to):
                target = lambda: passing.at[place]
                sem = lambda: self.line_sem.at[part, way, place]
                if hop == 0:
                    return [self._send(part, lambda: held.at[0, place], target, sem, to)]
                self._arrived(target(), sem())
                passing[place] = passing[place] + held[0, place]
                return [self._send(part, target, target, sem, to)]

            self._when(condition, action)

    def _result(self, part):
        held, below, above, result, columns = (self.parts[part][i] for i in (2, 4, 5, 6, 7))
        z, last = self.z, self.n_grp - 1
        result[:, columns] = held[0, z].astype(F32)

        def add(passing, index):
            self._arrived(passing.at[z], self.line_sem.at[part, index, z])
            result[:, columns] = result[:, columns] + passing[z].astype(F32)

        pl.when(z > 0)(lambda: add(below, 0))
        pl.when(z < last)(lambda: add(above, 1))

    def waves(self):
        bind = functools.partial
        low, high, places = 0, self.n_grp - 1, []
        while low <= high:
            places += [high] if low == high else [high, low]
            low, high = low + 1, high - 1
        units = []
        for i, count in enumerate(self.groups):
            first = sum(self.groups[:i])
            group = range(first, first + count)
            units += [(part, place) for place in places for part in group]
        ahead, stages = self.ahead, len(self.orders[0])
        length = len(units) + ahead + 2 * stages + 4 * self.n_grp
        waves = [[] for _ in range(length)]
        final = {}
        for n, (part, place) in enumerate(units):
            waves[max(0, n + 1 - ahead)].append(bind(self._begin, part, place))
            at = n + 1
            for stage in range(1, stages):
                for k in self.keeps[part]:
                    if self.stage_of(part, k) == stage:
                        waves[at].append(bind(self._halve, part, place, k))
                at += 2
            waves[at].append(bind(self._save, part, place))
            if self.parts[part][4] is None:
                continue
            for hop in range(self.n_grp - 1):
                waves[at + 2 * hop].append(bind(self._line, part, place, hop))
            final[part] = at + 2 * (self.n_grp - 1)
        for part, at in final.items():
            waves[at].append(bind(self._result, part))
        return waves

    def finish(self):
        for copy in self.saved:
            copy.wait()
        for condition, copies in self.sent:
            if condition is None:
                for copy in copies:
                    copy().wait_send()
            else:

                def wait_sent():
                    for copy in copies:
                        copy().wait_send()

                pl.when(condition)(wait_sent)


def scatter_buffers(kind, rows, width, n_fsdp, n_grp):
    m = n_fsdp.bit_length() - 2
    keep = n_fsdp // 4
    slots = m + sum(i << (m - 1 - i) for i in range(1, m))
    leading = {
        "full": [(keep, n_grp), (slots, n_grp), (n_grp,), (n_grp,)],
        "cross": [(keep, n_grp), (slots, n_grp)],
    }[kind]
    return [pltpu.VMEM(v + (rows, width), BF16) for v in leading]


def scatter_scratch(kinds, sizes, n_fsdp, n_grp, parts=None):
    m = n_fsdp.bit_length() - 2
    keep = n_fsdp // 4
    slots = m + sum(i << (m - 1 - i) for i in range(1, m))
    parts = parts or len(kinds)
    shapes = [
        pltpu.SemaphoreType.DMA((parts, n_grp * (2 * keep + 2 * n_grp))),
        pltpu.SemaphoreType.DMA((parts, slots, n_grp)),
        pltpu.SemaphoreType.DMA((parts, 2, n_grp)),
        pltpu.SemaphoreType.DMA((parts, keep, n_grp)),
    ]
    for kind, (rows, width) in zip(kinds, sizes):
        shapes += scatter_buffers(kind, rows, width, n_fsdp, n_grp)
    return shapes


def scatter_parts(kinds, aways, kepts, buffers, results):
    parts, buffers = [], list(buffers)
    for kind, away, kept, result in zip(kinds, aways, kepts, results):
        count = {"full": 4, "cross": 2}[kind]
        mine, buffers = buffers[:count], buffers[count:]
        if kind == "cross":
            mine = mine + [None, None]
        parts.append((away, kept, *mine, *result))
    return parts, buffers


def column_ranges(widths):
    start, ranges = 0, []
    for width in widths:
        ranges.append(pl.ds(start, width))
        start += width
    return ranges


def last_kernel(widths, lines, n_fsdp, n_grp, *refs):
    mixed_ref, narrow_ref, l_ref, l_other_ref, w_hbm, forget_ref = refs[:6]
    tokens_ref, scale_ref, gain_ref, resid_ref, small_ref = refs[6:11]
    count, more = len(widths), sum(len(w) for w in lines)
    lined, refs = refs[11 : 11 + more], refs[11 + more :]
    wide_ref, narrow_result, grad_ref, dgain_refs = refs[0], refs[1], refs[2], refs[3:6]
    results, refs = refs[6 : 6 + len(lines)], refs[6 + len(lines) :]
    sems, refs = refs[:4], refs[4:]
    ranges = column_ranges(widths)
    gathered_refs, aways, refs = refs[:more], refs[more : more + count], refs[more + count :]
    places = [(wide_ref, c) for c in ranges[:-1]] + [(narrow_result, pl.ds(0, widths[-1]))]
    parts, refs = scatter_parts(["full"] * count, aways, [None] * count, refs, places)
    mixed_other, narrow_other, rows_ref, w_ref, act_ref, incoming, send_sem, recv_sem, w_sem, own_sem, group_send, group_recv, total_ref = refs
    f, z = lax.axis_index("fsdp"), lax.axis_index("grp")
    tok, width = act_ref.shape
    pieces = n_fsdp // 2

    meet(n_fsdp, n_grp, False)

    def exchange(source, target, index, peer):
        return pltpu.make_async_remote_copy(
            src_ref=source,
            dst_ref=target,
            send_sem=send_sem.at[index],
            recv_sem=recv_sem.at[index],
            device_id=peer,
            device_id_type=MESH,
        )

    sibling = {"fsdp": flip(f, 1), "grp": z}
    others = []
    for i in range(count):
        if i < count - 1:
            pair = (mixed_ref.at[:, ranges[i]], mixed_other.at[:, ranges[i]])
        else:
            pair = (narrow_ref, narrow_other)
        others.append(exchange(*pair, i, sibling))
        others[-1].start()

    chunk = w_ref.shape[2]
    chunks = w_hbm.shape[1] // chunk

    def fetch(i):
        return pltpu.make_async_copy(
            w_hbm.at[:, pl.ds(i * chunk, chunk)], w_ref.at[i % 2], w_sem.at[i % 2]
        )

    fetch(0).start()
    for k in range(pieces):
        row = flip(f // 2, k) * 2 + f % 2
        rows_ref[k, :, :tok] = l_ref[row]
        rows_ref[k, :, tok:] = l_other_ref[row]

    scatter = Scatter(parts, [count], (), AHEAD, *sems, n_fsdp, n_grp)
    waves = iter(scatter.waves())

    def advance(steps=None):
        for wave in itertools.islice(waves, steps):
            for step in wave:
                step()

    direct = GroupExchange(n_grp, group_send, group_recv)
    own = []
    for i, (source, target) in enumerate(zip(lined, gathered_refs)):
        direct.send(
            i, i, lambda place, source=source: source.at[place],
            lambda place, target=target: target.at[place],
        )
        own.append(pltpu.make_async_copy(source.at[z], target.at[z], own_sem.at[i]))
        own[-1].start()

    def products(part, ks, target):
        if part < count - 1:
            right = (mixed_ref[:, ranges[part]], mixed_other[:, ranges[part]])
        else:
            right = (narrow_ref[...], narrow_other[...])
        right = jnp.concatenate(right, axis=0)
        left = jnp.concatenate([rows_ref[k] for k in ks], axis=0)
        value = jnp.dot(left, right, preferred_element_type=F32).astype(BF16)
        target[...] = value.reshape(target.shape)

    for part in range(count):
        others[part].wait_recv()
        first = scatter.orders[part][0]
        products(part, [k ^ first for k in scatter.keeps[part]], aways[part])
    advance(1)
    for part in range(count):
        products(part, scatter.keeps[part], parts[part][2])
    act_ref[...] = dot_lanes(narrow_ref[...], forget_ref[...])
    for i in range(chunks):
        if i + 1 < chunks:
            fetch(i + 1).start()
        fetch(i).wait()
        act_ref[...] += dot_lanes(mixed_ref[:, pl.ds(i * chunk, chunk)], w_ref[i % 2])
        advance(1)

    block = next(t for t in (64, 32, 16, 8) if tok % t == 0)
    total_ref[0] = small_ref[...]

    def finish_rows(i, carry):
        rows = pl.ds(pl.multiple_of(i * block, block), block)
        scale = scale_ref[rows, :]
        normed = tokens_ref[rows, :].astype(F32) * scale
        act = act_ref[rows, :]
        total_ref[0, :, :width] += jnp.sum(act * normed, axis=0, keepdims=True)
        scaled = act * gain_ref[...]
        average = jnp.mean(scaled * normed, axis=1, keepdims=True)
        grad_ref[rows, :] = (
            resid_ref[rows, :] + scale * (scaled - normed * average)
        ).astype(BF16)
        return carry

    lax.fori_loop(0, tok // block, finish_rows, 0)
    peers = [{"fsdp": f, "grp": flip(z, 1 << i)} for i in range(n_grp.bit_length() - 1)]
    peers += [{"fsdp": flip(f, 1 << i), "grp": z} for i in range(n_fsdp.bit_length() - 1)]
    sent = []
    for i, peer in enumerate(peers):
        copy = exchange(total_ref.at[i], incoming.at[i], count + i, peer)
        copy.start()
        sent.append(copy)
        advance(1)
        copy.wait_recv()
        total_ref[i + 1] = total_ref[i] + incoming[i]
    total = total_ref[len(peers)]
    for ref, start in zip(dgain_refs, (0, width, 2 * width)):
        ref[...] = total[:, start : start + ref.shape[1]]
    advance()
    i = 0
    for ref, line in zip(results, lines):
        for columns in column_ranges(line):
            own[i].wait()
            direct.wait(i)
            value = gathered_refs[i][0].astype(F32)
            for place in range(1, n_grp):
                value = value + gathered_refs[i][place].astype(F32)
            ref[:, columns] = value
            i += 1
    scatter.finish()
    direct.finish()
    for copy in others + sent:
        copy.wait_send()


def last_gradients(
    acts, mixed, narrow, w_qkv, forget, tokens, scale, gain, resid, small, lines, collective_id
):
    n_fsdp, n_grp = lax.axis_size("fsdp"), lax.axis_size("grp")
    tok, wide = mixed.shape
    width = tokens.shape[1]
    own_rows = width // (n_fsdp * n_grp)
    split = 4 if wide % 512 == 0 else 2
    more = sum(len(w) for w in lines)
    widths = [wide // split] * split + [narrow.shape[1]]
    keep = n_fsdp // 4
    rounds = n_fsdp.bit_length() + n_grp.bit_length() - 2
    aways = [jax.ShapeDtypeStruct((keep, n_grp, own_rows, w), BF16) for w in widths]
    chunk = next(t for t in (512, 384, 256, 128) if wide % t == 0)
    vmem = pl.BlockSpec(memory_space=pltpu.VMEM)
    anywhere = pl.BlockSpec(memory_space=pl.ANY)
    return pl.pallas_call(
        functools.partial(
            last_kernel, widths, [[v.shape[2] for v in w] for w in lines], n_fsdp, n_grp
        ),
        out_shape=[
            jax.ShapeDtypeStruct((own_rows, wide), F32),
            jax.ShapeDtypeStruct((own_rows, widths[-1]), F32),
            jax.ShapeDtypeStruct(tokens.shape, BF16),
            jax.ShapeDtypeStruct((1, width), F32),
            jax.ShapeDtypeStruct((1, width), F32),
            jax.ShapeDtypeStruct((1, widths[-1]), F32),
        ]
        + [
            jax.ShapeDtypeStruct((w[0].shape[1], sum(v.shape[2] for v in w)), F32) for w in lines
        ],
        in_specs=[vmem] * 4
        + [anywhere]
        + [vmem] * 6
        + [anywhere] * sum(len(w) for w in lines),
        out_specs=[vmem] * (6 + len(lines)),
        scratch_shapes=scatter_scratch([], [], n_fsdp, n_grp, len(widths))
        + [pltpu.VMEM(v.shape, BF16) for w in lines for v in w]
        + [pltpu.VMEM(a.shape, BF16) for a in aways]
        + [v for a in aways for v in scatter_buffers("full", *a.shape[2:], n_fsdp, n_grp)]
        + [
            pltpu.VMEM(mixed.shape, BF16),
            pltpu.VMEM(narrow.shape, BF16),
            pltpu.VMEM((n_fsdp // 2, n_grp * own_rows, 2 * tok), BF16),
            pltpu.VMEM((2, width, chunk), BF16),
            pltpu.VMEM((tok, width), F32),
            pltpu.VMEM((rounds, 1, small.shape[1]), F32),
            pltpu.SemaphoreType.DMA((len(widths) + rounds,)),
            pltpu.SemaphoreType.DMA((len(widths) + rounds,)),
            pltpu.SemaphoreType.DMA((2,)),
            pltpu.SemaphoreType.DMA((max(1, more),)),
            pltpu.SemaphoreType.DMA((max(1, more), n_grp)),
            pltpu.SemaphoreType.DMA((max(1, more), n_grp)),
            pltpu.VMEM((rounds + 1, 1, small.shape[1]), F32),
        ],
        compiler_params=pltpu.CompilerParams(
            collective_id=collective_id, has_side_effects=True, vmem_limit_bytes=58 << 20
        ),
        name="last_gradients",
    )(
        mixed, narrow, acts[0], acts[1], w_qkv, forget, tokens, scale, gain, resid, small,
        *(v for w in lines for v in w),
    )


def backward_kernel(kinds, widths, received, pairs, head_size, n_fsdp, n_grp, *refs):
    count = sum(len(w) for w in widths)
    aways, kepts, refs = refs[:count], refs[count : 2 * count], refs[2 * count :]
    slots_ref, grad_ref, x_hbm, c_ref, mask_ref, seen_ref, lse_ref = refs[:7]
    refs = refs[7:]
    results, part_kinds = [], []
    for kind, w in zip(kinds, widths):
        if kind == "full":
            results += [(refs[0], columns) for columns in column_ranges(w)]
            refs = refs[1:]
        else:
            results += [(ref, None) for ref in refs[: len(w)]]
            refs = refs[len(w) :]
        part_kinds += [kind] * len(w)
    mixed_out, logs_out = refs[:2]
    sems = refs[2:6]
    parts, refs = scatter_parts(part_kinds, aways, kepts, refs[6:], results)
    x_refs, refs = refs[:pairs], refs[pairs:]
    do_refs, refs = refs[:pairs], refs[pairs:]
    dx_refs, refs = refs[:pairs], refs[pairs:]
    query_decay_ref, key_decay_ref, logs_ref, send_sem, recv_sem, copy_sem = refs
    blocks = n_grp
    pair_width = 2 * head_size
    group_width = pairs * pair_width
    width = blocks * group_width
    z = lax.axis_index("grp")

    meet(n_fsdp, n_grp, False)
    scatter = Scatter(parts, [len(w) for w in widths], received, AHEAD, *sems, n_fsdp, n_grp)
    swap_heads = GroupExchange(n_grp, send_sem, recv_sem)
    started = itertools.count()

    def keep(source, target):
        copy = pltpu.make_async_copy(source, target, copy_sem.at[next(started)])
        copy.start()
        return copy

    def heads_of(ref, part, place, pair):
        start = part * width + place * group_width + pair * pair_width
        return ref.at[:, pl.ds(pl.multiple_of(start, 128), pair_width)]

    own, late = [], []
    for pair in range(pairs):
        swap_heads.send(
            (pair, "do"),
            4 * pair,
            lambda place, pair=pair: heads_of(grad_ref, 0, place, pair),
            lambda place, pair=pair: do_refs[pair].at[place],
        )
        own.append(keep(heads_of(grad_ref, 0, z, pair), do_refs[pair].at[z]))
        own.append(keep(x_hbm.at[pair], x_refs[pair]))
    waves = iter(scatter.waves())

    def advance(count=None):
        for wave in itertools.islice(waves, count):
            for step in wave:
                step()

    advance(1)
    for pair in range(pairs):
        own[2 * pair].wait()
        own[2 * pair + 1].wait()
        swap_heads.wait((pair, "do"))
        attend_back_pair(
            pair,
            blocks,
            head_size,
            slots_ref,
            x_refs[pair],
            do_refs[pair],
            c_ref,
            mask_ref,
            lse_ref,
            dx_refs[pair],
            query_decay_ref,
            key_decay_ref,
        )
        for part in range(3):
            swap_heads.send(
                (pair, part),
                1 + 4 * pair + part,
                lambda place, pair=pair, part=part: dx_refs[pair].at[place, part],
                lambda place, pair=pair, part=part: heads_of(mixed_out, part, place, pair),
            )
            late.append(keep(dx_refs[pair].at[z, part], heads_of(mixed_out, part, z, pair)))
        advance(3)
    sum_decay_back(blocks, slots_ref, seen_ref, query_decay_ref, key_decay_ref, logs_ref)
    swap_heads.send(
        "logs",
        4 * pairs,
        lambda place: logs_ref.at[place],
        lambda place: logs_out.at[place],
    )
    late.append(keep(logs_ref.at[z], logs_out.at[z]))
    advance()
    for pair in range(pairs):
        for part in range(3):
            swap_heads.wait((pair, part))
    swap_heads.wait("logs")
    scatter.finish()
    swap_heads.finish()
    for copy in late:
        copy.wait()


def backward_attention(
    kinds, weights, received, slots, grad, x, decay, masks, seen, lse, head_size, collective_id
):
    n_fsdp, n_grp = lax.axis_size("fsdp"), lax.axis_size("grp")
    aways = [away for parts in weights for away, _ in parts]
    kepts = [kept for parts in weights for _, kept in parts]
    widths = [[away.shape[3] for away, _ in parts] for parts in weights]
    pairs, _, _, tok, pair_width = x.shape
    lanes = decay.shape[2]
    anywhere = pl.BlockSpec(memory_space=pl.ANY)
    vmem = pl.BlockSpec(memory_space=pltpu.VMEM)
    shapes, specs = [], []
    for kind, parts, w in zip(kinds, weights, widths):
        own_rows = parts[0][0].shape[2]
        if kind == "full":
            shapes.append(jax.ShapeDtypeStruct((own_rows, sum(w)), F32))
            specs.append(vmem)
        else:
            shapes += [jax.ShapeDtypeStruct((n_grp, own_rows, v), BF16) for v in w]
            specs += [anywhere] * len(w)
    part_kinds = [kind for kind, w in zip(kinds, widths) for _ in w]
    out = pl.pallas_call(
        functools.partial(
            backward_kernel, kinds, widths, received, pairs, head_size, n_fsdp, n_grp
        ),
        out_shape=shapes
        + [
            jax.ShapeDtypeStruct((tok, 3 * grad.shape[1]), BF16),
            jax.ShapeDtypeStruct((n_grp, tok, lanes), F32),
        ],
        in_specs=[anywhere] * (2 * len(aways))
        + [pl.BlockSpec(memory_space=pltpu.SMEM), anywhere, anywhere]
        + [vmem] * 4,
        out_specs=specs + [anywhere] * 2,
        scratch_shapes=scatter_scratch(
            part_kinds, [v.shape[2:] for v in aways], n_fsdp, n_grp
        )
        + [pltpu.VMEM((n_grp, 3, tok, pair_width), BF16)] * pairs
        + [pltpu.VMEM((n_grp, tok, pair_width), BF16)] * pairs
        + [pltpu.VMEM((n_grp, 3, tok, pair_width), BF16)] * pairs
        + [pltpu.VMEM((n_grp, tok, lanes), F32)] * 3
        + [
            pltpu.SemaphoreType.DMA((1 + 4 * pairs, n_grp)),
            pltpu.SemaphoreType.DMA((1 + 4 * pairs, n_grp)),
            pltpu.SemaphoreType.DMA((1 + 5 * pairs,)),
        ],
        compiler_params=pltpu.CompilerParams(
            collective_id=collective_id, has_side_effects=True, vmem_limit_bytes=62 << 20
        ),
        name="backward_attention",
    )(*aways, *kepts, slots, grad, x, decay, masks, seen, lse)
    return out[:-2], out[-2], out[-1]


def project_kernel(act_ref, w_ref, out_ref):
    out_ref[...] = jnp.dot(act_ref[...], w_ref[...], preferred_element_type=F32).astype(BF16)


def project(act, w):
    tok, width = act.shape
    columns = w.shape[1]
    tile = next(t for t in (768, 512, 384, 256, 128) if columns % t == 0)
    return pl.pallas_call(
        project_kernel,
        out_shape=jax.ShapeDtypeStruct((tok, columns), BF16),
        grid=(columns // tile,),
        in_specs=[
            pl.BlockSpec((tok, width), lambda j: (0, 0), pipeline_mode=pl.Buffered(1)),
            pl.BlockSpec((width, tile), lambda j: (0, j)),
        ],
        out_specs=pl.BlockSpec((tok, tile), lambda j: (0, j)),
        compiler_params=pltpu.CompilerParams(vmem_limit_bytes=60 << 20),
        cost_estimate=pl.CostEstimate(
            flops=2 * tok * width * columns,
            bytes_accessed=2 * (width + tok) * columns,
            transcendentals=0,
        ),
        name="project",
    )(act, w)


def feed_forward_kernel(
    o_ref,
    tokens_ref,
    grad_ref,
    gain_ref,
    w_out_ref,
    gate_ref,
    up_ref,
    down_ref,
    inner_ref,
    dgate_ref,
    dup_ref,
    o_turned_ref,
    act_turned_ref,
    out_ref,
    dresid_ref,
    dbranch_ref,
    do_ref,
    dgain_ref,
    resid_ref,
    act_ref,
    sum_ref,
    dact_ref,
):
    tok = o_ref.shape[0]
    block = next(t for t in (128, 64, 32, 16, 8) if tok % t == 0)

    def rows_of(i):
        return pl.ds(pl.multiple_of(i * block, block), block)

    def norm(rows):
        resid = resid_ref[rows, :]
        scale = lax.rsqrt(jnp.mean(resid * resid, axis=1, keepdims=True) + EPSILON)
        return resid, resid * scale, scale

    @pl.when(pl.program_id(0) == 0)
    def _():
        resid_ref[...] = jnp.dot(o_ref[...], w_out_ref[...], preferred_element_type=F32)

        def begin(i, carry):
            rows = rows_of(i)
            resid_ref[rows, :] = tokens_ref[rows, :].astype(F32) + resid_ref[rows, :]
            _, normed, _ = norm(rows)
            act_ref[rows, :] = (normed * gain_ref[...]).astype(BF16)
            return carry

        lax.fori_loop(0, tok // block, begin, 0)
        sum_ref[...] = jnp.zeros_like(sum_ref)
        dact_ref[...] = jnp.zeros_like(dact_ref)
        o_turned_ref[...] = o_ref[...].T
        act_turned_ref[...] = act_ref[...].T

    act = act_ref[...]
    gate = jnp.dot(act, gate_ref[...], preferred_element_type=F32)
    up = jnp.dot(act, up_ref[...], preferred_element_type=F32)
    grad_inner = dot_lanes(grad_ref[...], down_ref[...])
    sigma = jax.nn.sigmoid(gate)
    swish = gate * sigma
    inner = (swish * up).astype(BF16)
    dgate = (grad_inner * up * (sigma * (1.0 + gate * (1.0 - sigma)))).astype(BF16)
    dup = (grad_inner * swish).astype(BF16)
    inner_ref[...] = inner.T
    dgate_ref[...] = dgate
    dup_ref[...] = dup
    sum_ref[...] += jnp.dot(inner, down_ref[...], preferred_element_type=F32)
    dact_ref[...] += dot_lanes(dgate, gate_ref[...]) + dot_lanes(dup, up_ref[...])

    @pl.when(pl.program_id(0) == pl.num_programs(0) - 1)
    def _():
        dgain_ref[...] = jnp.zeros_like(dgain_ref)

        def end(i, carry):
            rows = rows_of(i)
            resid, normed, scale = norm(rows)
            out_ref[rows, :] = (resid + sum_ref[rows, :]).astype(BF16)
            dact = dact_ref[rows, :]
            dgain_ref[...] += jnp.sum(dact * normed, axis=0, keepdims=True)
            scaled = dact * gain_ref[...]
            average = jnp.mean(scaled * normed, axis=1, keepdims=True)
            dresid = grad_ref[rows, :].astype(F32) + scale * (scaled - normed * average)
            dresid_ref[rows, :] = dresid
            dbranch_ref[rows, :] = dresid.astype(BF16)
            return carry

        lax.fori_loop(0, tok // block, end, 0)
        do_ref[...] = dot_lanes(dbranch_ref[...], w_out_ref[...]).astype(BF16)


def feed_forward(attn_o, tokens, grad, gain, w_out, gate_up, down):
    tok, width = tokens.shape
    hidden = down.shape[0]
    tile = 512
    steps = hidden // tile
    once = lambda rows, columns: pl.BlockSpec(
        (rows, columns), lambda j: (0, 0), pipeline_mode=pl.Buffered(1)
    )
    rows = once(tok, width)
    columns = pl.BlockSpec((tok, tile), lambda j: (0, j))
    low = lambda *shape: jax.ShapeDtypeStruct(shape, BF16)
    return pl.pallas_call(
        feed_forward_kernel,
        out_shape=[
            low(hidden, tok),
            low(tok, hidden),
            low(tok, hidden),
            low(width, tok),
            low(width, tok),
            low(tok, width),
            jax.ShapeDtypeStruct((tok, width), F32),
            low(tok, width),
            low(tok, width),
            jax.ShapeDtypeStruct((1, width), F32),
        ],
        grid=(steps,),
        in_specs=[
            rows,
            rows,
            rows,
            once(1, width),
            once(width, width),
            pl.BlockSpec((width, tile), lambda j: (0, j)),
            pl.BlockSpec((width, tile), lambda j: (0, steps + j)),
            pl.BlockSpec((tile, width), lambda j: (j, 0)),
        ],
        out_specs=[
            pl.BlockSpec((tile, tok), lambda j: (j, 0)),
            columns,
            columns,
            once(width, tok),
            once(width, tok),
            rows,
            rows,
            rows,
            rows,
            once(1, width),
        ],
        scratch_shapes=[
            pltpu.VMEM((tok, width), F32),
            pltpu.VMEM((tok, width), BF16),
            pltpu.VMEM((tok, width), F32),
            pltpu.VMEM((tok, width), F32),
        ],
        compiler_params=pltpu.CompilerParams(vmem_limit_bytes=60 << 20),
        cost_estimate=pl.CostEstimate(
            flops=12 * tok * width * hidden,
            bytes_accessed=6 * width * hidden,
            transcendentals=tok * hidden,
        ),
        name="feed_forward",
    )(attn_o, tokens, grad, gain, w_out, gate_up, gate_up, down)


def weight_grad_kernel(count, ids, *refs):
    own, other, (r_ref, r_other_ref, *outs) = (
        refs[: 2 * count],
        refs[2 * count : 4 * count],
        refs[4 * count :],
    )
    rows = [jnp.concatenate([ref[0] for ref in side], axis=0) for side in (own, other)]
    total = jnp.dot(
        jnp.concatenate(rows, axis=1),
        jnp.concatenate([r_ref[...], r_other_ref[...]], axis=0),
        preferred_element_type=F32,
    )
    total = total.astype(BF16).reshape(2 * count, -1, total.shape[1])
    outs[0][...] = total[:count]
    outs[1][...] = total[count:]


def weight_grad(ids, l_own, l_other, r_own, r_other, start, width):
    count = ids.shape[0] // 2
    _, rows, tok = l_own.shape
    limit = 1024 if rows * count < 1024 else 384
    tile = max(t for t in range(128, limit + 1, 128) if width % t == 0 and start % t == 0)
    steps, first = width // tile, start // tile
    pieces = [
        pl.BlockSpec(
            (1, rows, tok), lambda n, ids, k=k: (ids[k], 0, 0), pipeline_mode=pl.Buffered(1)
        )
        for k in range(2 * count)
    ]
    r_spec = pl.BlockSpec((tok, tile), lambda n, ids: (0, first + n))
    out_spec = pl.BlockSpec((count, rows, tile), lambda n, ids: (0, 0, n))
    return pl.pallas_call(
        functools.partial(weight_grad_kernel, count),
        out_shape=[jax.ShapeDtypeStruct((count, rows, width), BF16)] * 2,
        grid_spec=pltpu.PrefetchScalarGridSpec(
            num_scalar_prefetch=1,
            grid=(steps,),
            in_specs=pieces * 2 + [r_spec, r_spec],
            out_specs=[out_spec, out_spec],
        ),
        compiler_params=pltpu.CompilerParams(vmem_limit_bytes=60 << 20),
        cost_estimate=pl.CostEstimate(
            flops=8 * count * rows * tok * width,
            bytes_accessed=2 * (2 * count * rows * width + 2 * tok * width),
            transcendentals=0,
        ),
        name="weight_grad",
    )(ids, *[l_own] * (2 * count), *[l_other] * (2 * count), r_own, r_other)


def both_cores(turned):
    n_fsdp = lax.axis_size("fsdp")
    turned = turned.reshape(n_fsdp, turned.shape[0] // n_fsdp, turned.shape[1])
    return turned, swap(turned, "fsdp", 1)


def partial_rows(left, columns):
    n_fsdp, n_grp = lax.axis_size("fsdp"), lax.axis_size("grp")
    f = lax.axis_index("fsdp")
    parts = []
    for part, (right, right_other, start, width) in enumerate(columns):
        order = halving_orders(n_fsdp)[part % 2]
        keep = kept_pieces(order)
        ids = jnp.stack([flip(f // 2, k) for k in [k ^ order[0] for k in keep] + keep])
        pair = weight_grad(
            2 * ids + f % 2, left[0], left[1], right, right_other, start, width
        )
        parts.append(
            tuple(v.reshape(v.shape[0], n_grp, v.shape[1] // n_grp, width) for v in pair)
        )
    return parts


def norm_rows(features):
    row_scale = lax.rsqrt(jnp.mean(features * features, axis=-1, keepdims=True) + EPSILON)
    return (features * row_scale, row_scale)


def norm_back(grad_normed, normed, row_scale):
    average_addend = jnp.mean(grad_normed * normed, axis=-1, keepdims=True)
    return row_scale * (grad_normed - normed * average_addend)


def contract_cols(first_op, second_op):
    return lax.dot_general(
        first_op, second_op, (((1,), (1,)), ((), ())), preferred_element_type=F32
    )


def on_device(
    tokens,
    block_order,
    cont_lengths,
    gain_attn,
    w_qkv,
    w_forget,
    b_forget,
    w_out,
    gain_ffn,
    w_gate_up,
    w_down,
    grad_out,
):
    tok, width = tokens.shape
    heads = w_forget.shape[1]
    head_size = width // heads
    blocks = lax.axis_size("grp")
    own_heads = heads // blocks
    pairs = own_heads // 2
    group_width = width // blocks
    slots = block_order[0]

    positions = jnp.arange(tok, dtype=jnp.int32)
    causal = positions[None, :] <= positions[:, None]
    seg_ends = jnp.cumsum(cont_lengths[0], axis=1)
    segment = jnp.sum((positions[None, :, None] >= seg_ends[:, None, :]).astype(jnp.int32), axis=2)
    within = jnp.logical_and(segment[:, :, None] == segment[:, None, :], causal[None])
    seen = jnp.concatenate([causal[None], within], axis=0)
    masks = jnp.where(seen.transpose(0, 2, 1), 0.0, NEG).astype(F32)
    seen_low = seen.astype(BF16)

    forget_pad = 128 - heads
    qkv_full, forget_full, out_line, down_line = gather_rows(
        ("full", "full", "line", "line"),
        [w_qkv, jnp.pad(w_forget, ((0, 0), (0, forget_pad))), w_out, w_down],
        1,
    )
    qkv_full, forget_full = (v.reshape(-1, v.shape[2]) for v in (qkv_full, forget_full))
    inputs = tokens.astype(F32)
    normed_one, scale_one = norm_rows(inputs)
    acts = (normed_one * gain_attn).astype(BF16)
    grad_out_other = swap(grad_out, "fsdp", 1)
    acts_rows = both_cores(acts.T)
    logits = jnp.dot(acts, forget_full, preferred_element_type=F32)[:, :heads] + b_forget
    log_keep = jax.nn.log_sigmoid(logits)
    mixed = project(acts, qkv_full)
    mixed, grad_out_other = lax.optimization_barrier((mixed, grad_out_other))

    logs = jnp.pad(
        log_keep.T.reshape(blocks, own_heads, tok), ((0, 0), (0, 8 - own_heads), (0, 0))
    )
    (out_full, gate_up_full, down_full), (attn_o, x, lse, decay) = forward_attention(
        ("lined", "full", "lined"), [out_line, w_gate_up, down_line], slots, mixed, logs, masks, seen_low, head_size, 2
    )

    half, hidden = width // 2, down_full.shape[0]
    (
        inner_turned,
        grad_gate,
        grad_up,
        attn_turned,
        acts_two_turned,
        output,
        grad_resid,
        grad_branch,
        grad_heads,
        gain_two_grad,
    ) = feed_forward(attn_o, tokens, grad_out, gain_ffn[None], out_full, gate_up_full, down_full)
    down_rows = both_cores(inner_turned)
    down_rows, *later = lax.optimization_barrier(
        (down_rows, grad_gate, grad_up, grad_branch, acts_two_turned, attn_turned)
    )
    grad_gate_other, grad_up_other, grad_branch_other = (swap(v, "fsdp", 1) for v in later[:3])
    acts_two_rows, attn_rows = both_cores(later[3]), both_cores(later[4])
    part_down = partial_rows(
        down_rows, [(grad_out, grad_out_other, 0, half), (grad_out, grad_out_other, half, half)]
    )
    orders = halving_orders(lax.axis_size("fsdp"))
    part_down, grad_gate, grad_up, grad_branch = lax.optimization_barrier(
        (part_down, grad_gate, grad_up, grad_branch)
    )
    part_down = [
        (swap(away, "fsdp", 2 * order[0]), kept)
        for (away, kept), order in zip(part_down, orders)
    ]
    part_gate_up = partial_rows(
        acts_two_rows,
        [(grad_gate, grad_gate_other, 0, hidden), (grad_up, grad_up_other, 0, hidden)],
    )
    part_out = partial_rows(
        attn_rows,
        [
            (grad_branch, grad_branch_other, 0, half),
            (grad_branch, grad_branch_other, half, half),
        ],
    )

    sums, grad_mixed, log_grad = backward_attention(
        ("cross", "full", "cross"),
        [part_down, part_gate_up, part_out],
        range(len(part_down)),
        slots,
        grad_heads,
        x,
        decay,
        masks,
        seen_low,
        lse,
        head_size,
        3,
    )
    log_grad = log_grad[:, :, :own_heads].transpose(1, 0, 2).reshape(tok, heads)
    grad_logits = (log_grad * jax.nn.sigmoid(-logits)).astype(BF16)
    narrow = jnp.pad(grad_logits, ((0, 0), (0, forget_pad)))
    bias_grad = jnp.sum(narrow.astype(F32), axis=0)
    (
        grad_qkv,
        grad_forget,
        grad_tokens,
        grad_gain,
        grad_gain_two,
        grad_bias,
        grad_down,
        grad_out_w,
    ) = last_gradients(
        acts_rows,
        grad_mixed,
        narrow,
        qkv_full,
        forget_full,
        tokens,
        scale_one,
        gain_attn[None],
        grad_resid,
        jnp.concatenate([jnp.zeros((width,), F32), gain_two_grad[0], bias_grad])[None],
        [sums[:2], sums[3:]],
        4,
    )
    return (
        output,
        grad_tokens,
        grad_gain[0],
        grad_qkv,
        grad_forget[:, :heads],
        grad_bias[0, :heads],
        grad_out_w,
        grad_gain_two[0],
        sums[2],
        grad_down,
    )


def solution(mesh):
    both = P(("fsdp", "grp"), None)
    in_specs = (
        both,
        P("fsdp", None),
        P("fsdp", None, None),
        P(),
        both,
        both,
        P(),
        both,
        P(),
        both,
        both,
        both,
    )
    out_specs = (both, both, P(), both, both, P(), both, P(), both, both)
    return jax.shard_map(
        on_device, mesh=mesh, in_specs=in_specs, out_specs=out_specs, check_vma=False
    )
```
